32 devices in a mesh: dp: 16 (over z, y, core), tensor: 2 (over x).
Axes of the slice: x: 2, y: 2, z: 4, core: 2. Of those that a mesh axis runs over, the one named last changes fastest.
Arguments:
- tokens: bfloat16 [2, 9456, 768], P(None, 'dp'), may hold values from -6 to 6
- segment: int32 [2, 9456], P(None, 'dp'), may hold values from 0 to 3, as said below
- cotangent: bfloat16 [2, 9456, 768], P(None, 'dp'), may hold values from -6 to 6
- ln_gain: float32 [2, 768], replicated, may hold values from 0.5 to 1.5
- ln_shift: float32 [2, 768], replicated, may hold values from -1.8 to 1.8
- qkv_weight: bfloat16 [3, 768, 768], P(None, 'dp', 'tensor'), may hold values from -0.21875 to 0.21875
- qv_bias: float32 [2, 768], P(None, 'tensor'), may hold values from -1.8 to 1.8
- out_weight: bfloat16 [768, 768], P('tensor', 'dp'), may hold values from -2.5 to 2.5
- out_bias: float32 [2, 768], replicated, may hold values from -1.8 to 1.8
- layer_scale: float32 [2, 768], replicated, may hold values from 0.5 to 1.5
- up_weight: bfloat16 [768, 3072], P('dp', 'tensor'), may hold values from -0.21875 to 0.21875
- up_bias: float32 [3072], P('tensor'), may hold values from -1.8 to 1.8
- down_weight: bfloat16 [3072, 768], P('tensor', 'dp'), may hold values from -0.109375 to 0.109375
Outputs:
- block_output: bfloat16 [2, 9456, 768], P(None, 'dp')
- input_grad: bfloat16 [2, 9456, 768], P(None, 'dp')
- ln_gain_grad: float32 [2, 768], replicated
- ln_shift_grad: float32 [2, 768], replicated
- qkv_grad: float32 [3, 768, 768], P(None, 'dp', 'tensor')
- qv_bias_grad: float32 [2, 768], P(None, 'tensor')
- out_weight_grad: float32 [768, 768], P('tensor', 'dp')
- out_bias_grad: float32 [2, 768], replicated
- layer_scale_grad: float32 [2, 768], replicated
- up_grad: float32 [768, 3072], P('dp', 'tensor')
- up_bias_grad: float32 [3072], P('tensor')
- down_grad: float32 [3072, 768], P('tensor', 'dp')
The draws below stay inside these ranges and needn't reach their ends.
Inputs may be any that keep to these rules, and one draw needn't show every extreme that they name: `segment`: within each micro-batch, each device's block of 591 positions holds either three images of 197 patches (position p belongs to image p // 197) or one image of 577 patches (image 0) followed by padding numbered 3; the second layout falls on 6 devices (at least one) of each micro-batch, drawn from the seed.
All inputs are finite; a program needn't handle non-finite values.
Results may differ from the reference program's by a relative error of at most 0.015.
Values may be sent and summed in bfloat16 or wider, within the bound.
No kernel may reach another device: no remote copies, remote signals or barrier semaphores. Data moves between devices by JAX's collectives and lax.ppermute only.
A program may use at most 128 MiB of HBM per device.

```python
import jax
import jax.numpy as jnp
from jax import lax

D = 768
HEADS = 12
FF = 3072
SMALL_IMG = 197
LARGE_IMG = 577
MB = 2
CAP = 591
TOKENS = 9456
N_TENSOR = 2


def draw_segment(key, part):
    device_count = TOKENS // CAP
    chosen = max(1, 3 * device_count // 8)
    keys_all = jax.random.split(key, MB)
    orders = jax.vmap(lambda one_key: jax.random.permutation(one_key, device_count))(keys_all)
    large_layout = orders < chosen
    position = jnp.arange(CAP, dtype=jnp.int32)
    small_labels = position // SMALL_IMG
    large_labels = jnp.where(position < LARGE_IMG, 0, 3).astype(jnp.int32)
    labels = jnp.where(large_layout[:, :, None], large_labels[None, None, :], small_labels[None, None, :])
    return labels.reshape(MB, TOKENS).astype(jnp.int32)


def strengthened(values, stream_key, source, target, shards_of, factor):
    def block_of(dim):
        return (jnp.arange(values.shape[dim]) // (values.shape[dim] // shards_of)).reshape((-1,) + (1,) * (values.ndim - 1 - dim))

    near = jax.random.permutation(stream_key, shards_of)[block_of(target)]
    second = (block_of(target) + shards_of // 2) % shards_of
    return jnp.where((block_of(source) == near) | (block_of(source) == second), factor * values, values)


def shard_levels(key, dims, shards, least, largest):
    loudness, own = 1.0, jax.random.fold_in(key, 6)
    for dim, shards_of in shards:
        heights = jnp.exp(jax.random.uniform(jax.random.fold_in(own, dim), (shards_of,), jnp.float32, least / len(shards), largest / len(shards)))
        loudness = loudness * jnp.repeat(heights, dims[dim] // shards_of).reshape([-1 if axis == dim else 1 for axis in range(len(dims))])
    return loudness


def noise(rng, dims, scale, most, cuts=(), kind=jnp.bfloat16):
    drawn = scale * jax.random.normal(rng, dims, jnp.float32)
    if cuts:
        drawn = drawn * shard_levels(rng, dims, cuts, -0.22, 0.18)
    return jnp.clip(drawn, -most, most).astype(kind)


def gaussian_with(rng, dims, scale, limit, cuts, heavy, kind=jnp.bfloat16):
    array = scale * jax.random.normal(rng, dims, jnp.float32)
    if cuts:
        array = array * shard_levels(rng, dims, cuts, -0.22, 0.18)
    return jnp.clip(strengthened(array, jax.random.fold_in(rng, 3), *heavy), -limit, limit).astype(kind)


def setup_inputs(seed: int = 0) -> dict:
    seeds = jax.random.split(jax.random.key(seed), 14)
    return {
        "tokens": gaussian_with(seeds[0], (MB, TOKENS, D), 1.0, 6.0, ((1, 16),), (1, 2, 16, 2.0)),
        "segment": draw_segment(jax.random.fold_in(seeds[13], 71), 0),
        "cotangent": gaussian_with(seeds[2], (MB, TOKENS, D), 1.0, 6.0, ((1, 16),), (1, 2, 16, 2.0)),
        "ln_gain": jnp.clip(1.0 + 0.1 * jax.random.normal(seeds[3], (2, D), jnp.float32), 0.5, 1.5),
        "ln_shift": noise(seeds[4], (2, D), 0.3, 1.8, (), jnp.float32),
        "qkv_weight": noise(seeds[5], (3, D, D), D ** -0.5, 0.21875, ((1, 16), (2, 2))),
        "qv_bias": noise(seeds[6], (2, D), 0.3, 1.8, ((1, 2),), jnp.float32),
        "out_weight": noise(seeds[7], (D, D), (max(D // 128, 4)) ** -0.5, 2.5, ((0, 2), (1, 16))),
        "out_bias": noise(seeds[8], (2, D), 0.3, 1.8, (), jnp.float32),
        "layer_scale": jnp.clip(jax.random.uniform(seeds[9], (2, D), jnp.float32, 0.5, 1.5), 0.5, 1.5),
        "up_weight": noise(seeds[10], (D, FF), D ** -0.5, 0.21875, ((0, 16), (1, 2))),
        "up_bias": noise(seeds[11], (FF,), 0.3, 1.8, ((0, 2),), jnp.float32),
        "down_weight": noise(seeds[12], (FF, D), FF ** -0.5, 0.109375, ((0, 2), (1, 16))),
    }


epsilon = 1e-06
padding_id = 3
masked_score = -1e+30

@jax.custom_vjp
def low(v):
    return lax.optimization_barrier(v.astype(jnp.bfloat16)).astype(jnp.float32)

@jax.custom_vjp
def low_back(v):
    return v

def low_keep(v):
    return (low(v), None)

def low_pass(kept, grad):
    return (grad,)

def back_keep(v):
    return (v, None)

def back_low(kept, grad):
    return (low(grad),)
low.defvjp(low_keep, low_pass)
low_back.defvjp(back_keep, back_low)

def dot_highest(left_side, right_side):
    return jnp.dot(left_side, right_side, precision=lax.Precision.HIGHEST, preferred_element_type=jnp.float32)

def layer_norm(inputs, norm_gain, norm_shift):
    center = inputs - lax.optimization_barrier(jnp.mean(inputs, axis=-1, keepdims=True))
    spread = lax.optimization_barrier(jnp.mean(center * center, axis=-1, keepdims=True))
    return center * lax.rsqrt(spread + epsilon) * norm_gain + norm_shift

def split_product(left_side, right_side):
    share_width = left_side.shape[1] // N_TENSOR
    summed = jnp.zeros((left_side.shape[0], right_side.shape[1]), jnp.float32)
    for tensor_rank in range(N_TENSOR):
        lower = tensor_rank * share_width
        upper = lower + share_width
        summed = summed + low(dot_highest(left_side[:, lower:upper], right_side[lower:upper]))
    return summed

def one_block(token_rows, labels, params):
    ln_gain, ln_shift, qkv_weight, qv_bias, out_weight, out_bias, layer_scale, up_weight, up_bias, down_weight = params
    head_size = D // HEADS
    score_scale = head_size ** (-0.5)
    row_count = token_rows.shape[0]
    normed_one = low(layer_norm(token_rows, ln_gain[0], ln_shift[0]))
    queries = low_back(low(dot_highest(normed_one, qkv_weight[0]) + qv_bias[0])).reshape(row_count, HEADS, head_size)
    key_heads = low_back(low(dot_highest(normed_one, qkv_weight[1]))).reshape(row_count, HEADS, head_size)
    value_heads = low_back(low(dot_highest(normed_one, qkv_weight[2]) + qv_bias[1])).reshape(row_count, HEADS, head_size)
    raw_scores = jnp.einsum('qhd,khd->hqk', queries, key_heads, precision=lax.Precision.HIGHEST)
    same_image = labels[:, None] == labels[None, :]
    scores = low_back(jnp.where(same_image[None], raw_scores * score_scale, masked_score))
    probs = jax.nn.softmax(scores, axis=-1)
    mixed_heads = jnp.einsum('hqk,khd->qhd', low(probs), value_heads, precision=lax.Precision.HIGHEST)
    mixed_heads = low_back(low(mixed_heads)).reshape(row_count, D)
    attended = low_back(split_product(mixed_heads, out_weight)) + out_bias[0]
    middle = token_rows + layer_scale[0] * attended
    normed_two = low(layer_norm(middle, ln_gain[1], ln_shift[1]))
    hidden = low_back(dot_highest(normed_two, up_weight) + up_bias)
    activated = low(jax.nn.gelu(hidden, approximate=False))
    ffn_out = low_back(split_product(activated, down_weight)) + out_bias[1]
    return middle + layer_scale[1] * ffn_out

def forward(token_rows, params, labels):
    blocks = token_rows.reshape(-1, CAP, D)
    label_blocks = labels.reshape(-1, CAP)
    block_fn = jax.checkpoint(lambda block_pair: one_block(block_pair[0], block_pair[1], params))
    return lax.map(block_fn, (blocks, label_blocks)).reshape(token_rows.shape)

def reference(tokens, segment, cotangent, ln_gain, ln_shift, qkv_weight, qv_bias, out_weight, out_bias, layer_scale, up_weight, up_bias, down_weight):
    params = tuple((source_array.astype(jnp.float32) for source_array in (ln_gain, ln_shift, qkv_weight, qv_bias, out_weight, out_bias, layer_scale, up_weight, up_bias, down_weight)))
    token_rows = tokens.astype(jnp.float32)
    live = (segment != padding_id).astype(jnp.float32)[..., None]

    def closed(rows_in, params_in):
        return forward(rows_in, params_in, segment)
    result, pullback = jax.vjp(closed, token_rows, params)
    grad_rows, grad_params = pullback(cotangent.astype(jnp.float32) * live)
    return (result.astype(jnp.bfloat16), grad_rows.astype(jnp.bfloat16), grad_params[0], grad_params[1], grad_params[2], grad_params[3], grad_params[4], grad_params[5], grad_params[6], grad_params[7], grad_params[8], grad_params[9])
```

```python
import jax
import jax.numpy as jnp
from jax import lax
from jax.sharding import PartitionSpec as P

D = 768
HEADS = 12
HEAD = D // HEADS
EPS = 1e-06
PAD_ID = 3
NEG = -1e30
BF = jnp.bfloat16
F32 = jnp.float32


def mm(a, b):
    return jnp.dot(a, b, preferred_element_type=F32)


def mm_nt(a, b):
    return lax.dot_general(a, b, (((1,), (1,)), ((), ())), preferred_element_type=F32)


def mm_tn(a, b):
    return lax.dot_general(a, b, (((0,), (0,)), ((), ())), preferred_element_type=F32)


def layer_norm(v, gain, shift):
    c = v - jnp.mean(v, axis=-1, keepdims=True)
    s = jnp.mean(c * c, axis=-1, keepdims=True)
    return c * lax.rsqrt(s + EPS) * gain + shift


def exact_gelu(v):
    return jax.nn.gelu(v, approximate=False)


def swap(v, n_tensor):
    return lax.ppermute(v, "tensor", [(i, (i + 1) % n_tensor) for i in range(n_tensor)])


def one_batch(x16, labels, upstream, ln_gain, ln_shift, qv_bias, out_bias, layer_scale, up_bias, wa, wf):
    rows = x16.shape[0]
    half = wa.shape[2] // 4
    hid_half = wf.shape[2] // 2
    scale = HEAD ** (-0.5)
    wq = jnp.concatenate([wa[0, :, 0:half], wa[1, :, 0:half]], axis=1)
    wk = jnp.concatenate([wa[0, :, half : 2 * half], wa[1, :, half : 2 * half]], axis=1)
    wv = jnp.concatenate([wa[0, :, 2 * half : 3 * half], wa[1, :, 2 * half : 3 * half]], axis=1)
    wo = [wa[t, :, 3 * half :] for t in range(2)]
    wu = [wf[t, :, :hid_half] for t in range(2)]
    wd = [wf[t, :, hid_half:] for t in range(2)]
    x = x16.astype(F32)
    n1 = layer_norm(x, ln_gain[0], ln_shift[0]).astype(BF)
    q = (mm(n1, wq) + qv_bias[0]).astype(BF).reshape(rows, HEADS, HEAD)
    k = mm(n1, wk).astype(BF).reshape(rows, HEADS, HEAD)
    v = (mm(n1, wv) + qv_bias[1]).astype(BF).reshape(rows, HEADS, HEAD)
    same = labels[:, None] == labels[None, :]

    def scores_of():
        raw = jnp.einsum("qhd,khd->hqk", q, k, preferred_element_type=F32)
        return jnp.where(same[None], raw * scale, NEG)

    s = scores_of()
    top = jnp.max(s, axis=-1, keepdims=True)
    lse = top + jnp.log(jnp.sum(jnp.exp(s - top), axis=-1, keepdims=True))
    p16 = jnp.exp(s - lse).astype(BF)
    o = jnp.einsum("hqk,khd->qhd", p16, v, preferred_element_type=F32).astype(BF).reshape(rows, D)
    a = sum(mm_nt(o[:, t * half : (t + 1) * half], wo[t]).astype(BF).astype(F32) for t in range(2))
    attn = a + out_bias[0]
    x1 = x + layer_scale[0] * attn
    n2 = layer_norm(x1, ln_gain[1], ln_shift[1]).astype(BF)
    dy = upstream.astype(F32) * (labels != PAD_ID).astype(F32)[:, None]
    df = dy * layer_scale[1]
    dfr = df.astype(BF)
    f = 0.0
    dn2 = 0.0
    gf = []
    dub = []
    for t in range(2):
        hid = mm(n2, wu[t]) + up_bias[t * hid_half : (t + 1) * hid_half]
        g = exact_gelu(hid).astype(BF)
        f = f + mm_nt(g, wd[t]).astype(BF).astype(F32)
        dg = mm(dfr, wd[t])
        dh = jax.vjp(exact_gelu, hid)[1](dg)[0].astype(BF)
        dub.append(jnp.sum(dh.astype(F32), axis=0))
        gf.append(jnp.concatenate([mm_tn(n2, dh).astype(BF), mm_tn(dfr, g).astype(BF)], axis=1))
        dn2 = dn2 + mm_nt(dh, wu[t])
    ffo = f + out_bias[1]
    y = (x1 + layer_scale[1] * ffo).astype(BF)
    g_ls1 = jnp.sum(dy * ffo, axis=0)
    g_ob1 = jnp.sum(df, axis=0)
    dmid, g_gain1, g_shift1 = jax.vjp(layer_norm, x1, ln_gain[1], ln_shift[1])[1](dn2)
    dx1 = dy + dmid
    g_ls0 = jnp.sum(dx1 * attn, axis=0)
    da = dx1 * layer_scale[0]
    g_ob0 = jnp.sum(da, axis=0)
    dar = da.astype(BF)
    do = jnp.concatenate([mm(dar, wo[t]) for t in range(2)], axis=1).astype(BF).reshape(rows, HEADS, HEAD)
    go = [mm_tn(dar, o[:, t * half : (t + 1) * half]).astype(BF) for t in range(2)]
    p = jnp.exp(scores_of() - lse)
    dp = jnp.einsum("qhd,khd->hqk", do, v, preferred_element_type=F32)
    dv = jnp.einsum("hqk,qhd->khd", p.astype(BF), do, preferred_element_type=F32)
    ds = (p * (dp - jnp.sum(p * dp, axis=-1, keepdims=True))).astype(BF)
    dq = jnp.einsum("hqk,khd->qhd", ds, k, preferred_element_type=F32) * scale
    dk = jnp.einsum("hqk,qhd->khd", ds, q, preferred_element_type=F32) * scale
    dq, dk, dv = (e.astype(BF).reshape(rows, D) for e in (dq, dk, dv))
    g_qb = jnp.sum(dq.astype(F32), axis=0)
    g_vb = jnp.sum(dv.astype(F32), axis=0)
    ga = [
        jnp.concatenate([mm_tn(n1, e[:, t * half : (t + 1) * half]).astype(BF) for e in (dq, dk, dv)] + [go[t]], axis=1)
        for t in range(2)
    ]
    dn1 = mm_nt(dq, wq) + mm_nt(dk, wk) + mm_nt(dv, wv)
    din, g_gain0, g_shift0 = jax.vjp(layer_norm, x, ln_gain[0], ln_shift[0])[1](dn1)
    dx = (dx1 + din).astype(BF)
    vec = [g_gain0, g_gain1, g_shift0, g_shift1, g_qb, g_vb, g_ob0, g_ob1, g_ls0, g_ls1, *dub]
    return y, dx, jnp.stack(ga), jnp.stack(gf), jnp.concatenate(vec)


def make_on_device(n_dp, n_tensor):
    def on_device(
        tokens, segment, cotangent, ln_gain, ln_shift, qkv_weight, qv_bias, out_weight,
        out_bias, layer_scale, up_weight, up_bias, down_weight,
    ):
        me = lax.axis_index("tensor")
        mine = lambda v: lax.dynamic_index_in_dim(v, me, 0, keepdims=False)
        own_first = lambda own, other: jnp.where(me == 0, jnp.stack([own, other]), jnp.stack([other, own]))
        wa = jnp.concatenate([qkv_weight[0], qkv_weight[1], qkv_weight[2], out_weight.T], axis=1)
        wf = jnp.concatenate([up_weight, down_weight.T], axis=1)
        wa_full = lax.all_gather(own_first(wa, swap(wa, n_tensor)), "dp", axis=1, tiled=True)
        wf_full = lax.all_gather(own_first(wf, swap(wf, n_tensor)), "dp", axis=1, tiled=True)
        qb = lax.all_gather(qv_bias, "tensor", axis=1, tiled=True)
        ub = lax.all_gather(up_bias, "tensor", axis=0, tiled=True)
        y, dx, ga, gf, vec = one_batch(
            mine(tokens), mine(segment), mine(cotangent), ln_gain, ln_shift, qb, out_bias, layer_scale, ub, wa_full, wf_full
        )
        out = own_first(y, swap(y, n_tensor))
        dxs = own_first(dx, swap(dx, n_tensor))

        def settle(g):
            part = lax.psum_scatter(g, "dp", scatter_dimension=1, tiled=True)
            other = lax.dynamic_index_in_dim(part, 1 - me, 0, keepdims=False)
            return mine(part).astype(F32) + swap(other, n_tensor).astype(F32)

        gf = settle(gf)
        ga = settle(ga)
        vec = lax.psum(vec, ("dp", "tensor"))
        half = wa.shape[1] // 4
        hid_half = wf.shape[1] // 2
        pair = lambda i: vec[i * D : (i + 2) * D].reshape(2, D)
        qv = lax.dynamic_slice_in_dim(pair(4), me * half, half, axis=1)
        dub = lax.dynamic_slice_in_dim(vec, 10 * D + me * hid_half, hid_half)
        return (
            out, dxs, pair(0), pair(2),
            jnp.stack([ga[:, i * half : (i + 1) * half] for i in range(3)]),
            qv, ga[:, 3 * half :].T, pair(6), pair(8), gf[:, :hid_half], dub, gf[:, hid_half:].T,
        )

    return on_device


def solution(mesh):
    rows = P(None, "dp", None)
    wt = P("tensor", "dp")
    return jax.shard_map(
        make_on_device(mesh.shape["dp"], mesh.shape["tensor"]),
        mesh=mesh,
        in_specs=(
            rows, P(None, "dp"), rows, P(), P(), P(None, "dp", "tensor"), P(None, "tensor"), wt,
            P(), P(), P("dp", "tensor"), P("tensor"), wt,
        ),
        out_specs=(
            rows, rows, P(), P(), P(None, "dp", "tensor"), P(None, "tensor"), wt,
            P(), P(), P("dp", "tensor"), P("tensor"), wt,
        ),
        check_vma=False,
    )
```

```python
import functools

import jax
import jax.numpy as jnp
from jax import lax
from jax.experimental import pallas as pl
from jax.experimental.pallas import tpu as pltpu
from jax.sharding import PartitionSpec as P

D = 768
HEADS = 12
HEAD = D // HEADS
EPS = 1e-06
PAD_ID = 3
NEG = -1e30
BF = jnp.bfloat16
F32 = jnp.float32
LOG2E = 1.4426950408889634
VMEM_LIMIT = 58 * 1024 * 1024

BLOCKS = 16
BROWS = D // BLOCKS


def mm(a, b):
    return jnp.dot(a, b, preferred_element_type=F32)


def mm_nt(a, b):
    return lax.dot_general(a, b, (((1,), (1,)), ((), ())), preferred_element_type=F32)


def mm_tn(a, b):
    return lax.dot_general(a, b, (((0,), (0,)), ((), ())), preferred_element_type=F32)


def row_stats(v):
    mean = jnp.mean(v, axis=-1, keepdims=True)
    c = v - mean
    rstd = lax.rsqrt(jnp.mean(c * c, axis=-1, keepdims=True) + EPS)
    return c * rstd, rstd


def norm_back(xhat, rstd, dn, gain):
    dxh = dn * gain
    m1 = jnp.mean(dxh, axis=-1, keepdims=True)
    m2 = jnp.mean(dxh * xhat, axis=-1, keepdims=True)
    return rstd * (dxh - m1 - xhat * m2)


def col_sum(v):
    return jnp.sum(v, axis=0, keepdims=True)


def load_blocks(dest, parts, dst, sem):
    copies = []
    n = 0
    for part in parts:
        for j in range(part.shape[0]):
            row = pl.multiple_of(dest[n] * BROWS, BROWS)
            copies.append(pltpu.make_async_copy(part.at[j], dst.at[pl.ds(row, BROWS)], sem.at[n]))
            n += 1
    for c in copies:
        c.start()
    return copies


def store_copies(core, slots, t, stage, outs, cols, sem):
    keep, send = outs
    copies = []
    half = BLOCKS // 2
    for m in range(half):
        a = pl.multiple_of((2 * m + core) * BROWS, BROWS)
        b = pl.multiple_of((2 * m + 1 - core) * BROWS, BROWS)
        copies.append(pltpu.make_async_copy(stage.at[pl.ds(a, BROWS)], keep.at[slots[t * half + m], :, cols], sem.at[2 * m]))
        copies.append(pltpu.make_async_copy(stage.at[pl.ds(b, BROWS)], send.at[slots[BLOCKS + t * half + m], :, cols], sem.at[2 * m + 1]))
    return copies


def pair_mask(h, dtype=BF):
    lane = lax.broadcasted_iota(jnp.int32, (1, 2 * HEAD), 1)
    return (lane // HEAD == h).astype(dtype)


def attn_fwd_kernel(rows, rp, cp, dest, me, x_ref, segc_ref, segr_ref, ln_ref, qb_ref, ob_ref, *rest):
    w = rest[:-14] if len(rest) > 14 else ()
    nw = len(rest) - 13
    w = rest[:nw]
    (x1_ref, attn_ref, q_ref, k_ref, v_ref, o_ref, lse_ref, w_s, x_s, bias_s, k_s, v_s, sem) = rest[nw:]
    copies = load_blocks(dest, w, w_s, sem)
    x_s[0:rows, :] = x_ref[0].astype(F32)
    x_s[rows:rp, :] = jnp.zeros((rp - rows, D), F32)
    bias_s[...] = jnp.where(segc_ref[...] == segr_ref[...], 0.0, NEG)
    xhat, _ = row_stats(x_s[...])
    n1 = (xhat * ln_ref[0:1] + ln_ref[1:2]).astype(BF)
    for c in copies:
        c.wait()
    half = D // 2
    scale = (HEAD ** (-0.5)) * LOG2E
    k_s[:, rp:cp, :] = jnp.zeros((6, cp - rp, 128), BF)
    v_s[:, rp:cp, :] = jnp.zeros((6, cp - rp, 128), BF)
    for t in range(2):
        z = mm(n1, w_s[t * D : (t + 1) * D, 0 : 3 * half]) + qb_ref[t : t + 1]
        z = z.astype(BF)
        for i in range(3):
            q_ref[3 * t + i] = z[:, i * 128 : (i + 1) * 128]
            k_s[3 * t + i, 0:rp, :] = z[:, half + i * 128 : half + (i + 1) * 128]
            v_s[3 * t + i, 0:rp, :] = z[:, 2 * half + i * 128 : 2 * half + (i + 1) * 128]
    k_ref[...] = k_s[:, 0:rp, :]
    v_ref[...] = v_s[:, 0:rp, :]

    def pair(p, _):
        q2 = q_ref[p]
        k2 = k_s[p]
        v2 = v_s[p]
        acc = None
        for h in range(2):
            m = pair_mask(h)
            s = mm_nt(q2, k2 * m) * scale + bias_s[...]
            top = jnp.max(s, axis=-1, keepdims=True)
            e = jnp.exp2(s - top)
            tot = jnp.sum(e, axis=-1, keepdims=True)
            oh = mm(e.astype(BF), v2 * m) * (1.0 / tot)
            acc = oh if acc is None else acc + oh
            lse_ref[2 * p + h] = top + jnp.log2(tot)
        o_ref[p] = acc.astype(BF)
        return 0

    lax.fori_loop(0, 6, pair, 0)
    a = jnp.zeros((rp, D), F32)
    for t in range(2):
        o_t = jnp.concatenate([o_ref[3 * t + i] for i in range(3)], axis=1)
        a = a + mm_nt(o_t, w_s[t * D : (t + 1) * D, 3 * half :]).astype(BF).astype(F32)
    attn = a + ob_ref[0:1]
    attn_ref[...] = attn
    x1_ref[...] = x_s[...] + ln_ref[2:3] * attn


def attn_fwd(dest, me, tokens, segc, segr, ln, qb, ob, weights):
    rows = tokens.shape[1]
    rp, cp = segc.shape[0], segr.shape[1]
    vm = pl.BlockSpec(memory_space=pltpu.VMEM)
    full = lambda a: pl.BlockSpec(a.shape, lambda i, d, m: (0,) * a.ndim)
    wcols = weights[0].shape[2]
    gs = pltpu.PrefetchScalarGridSpec(
        num_scalar_prefetch=2,
        grid=(1,),
        in_specs=[pl.BlockSpec((1, rows, D), lambda i, d, m: (m[0], 0, 0))]
        + [full(a) for a in (segc, segr, ln, qb, ob)]
        + [pl.BlockSpec(memory_space=pl.ANY)] * len(weights),
        out_specs=[
            pl.BlockSpec((rp, D), lambda i, d, m: (0, 0)),
            pl.BlockSpec((rp, D), lambda i, d, m: (0, 0)),
            pl.BlockSpec((6, rp, 128), lambda i, d, m: (0, 0, 0)),
            pl.BlockSpec((6, rp, 128), lambda i, d, m: (0, 0, 0)),
            pl.BlockSpec((6, rp, 128), lambda i, d, m: (0, 0, 0)),
            pl.BlockSpec((6, rp, 128), lambda i, d, m: (0, 0, 0)),
            pl.BlockSpec((HEADS, rp, 1), lambda i, d, m: (0, 0, 0)),
        ],
        scratch_shapes=[
            pltpu.VMEM((2 * D, wcols), BF),
            pltpu.VMEM((rp, D), F32),
            pltpu.VMEM((rp, cp), F32),
            pltpu.VMEM((6, cp, 128), BF),
            pltpu.VMEM((6, cp, 128), BF),
            pltpu.SemaphoreType.DMA((2 * BLOCKS,)),
        ],
    )
    sh = jax.ShapeDtypeStruct
    return pl.pallas_call(
        functools.partial(attn_fwd_kernel, rows, rp, cp),
        grid_spec=gs,
        out_shape=[
            sh((rp, D), F32), sh((rp, D), F32), sh((6, rp, 128), BF), sh((6, rp, 128), BF), sh((6, rp, 128), BF),
            sh((6, rp, 128), BF), sh((HEADS, rp, 1), F32),
        ],
        compiler_params=pltpu.CompilerParams(vmem_limit_bytes=VMEM_LIMIT),
        cost_estimate=pl.CostEstimate(flops=5_000_000_000, bytes_accessed=16_000_000, transcendentals=4_500_000),
        name="attn_fwd",
    )(dest, me, tokens, segc, segr, ln, qb, ob, *weights)


def gelu_parts(h):
    x = jnp.abs(h) * 0.7071067811865476
    t = 1.0 / (1.0 + 0.3275911 * x)
    e = jnp.exp2(h * h * (-0.5 * LOG2E))
    poly = t * (0.254829592 * 0.5 + t * (-0.284496736 * 0.5 + t * (1.421413741 * 0.5 + t * (-1.453152027 * 0.5 + t * (1.061405429 * 0.5)))))
    tail = poly * e
    phi = jnp.where(h < 0, tail, 1.0 - tail)
    return phi, phi + h * e * 0.3989422804014327


FCH = 768


def ffn_kernel(rows, rp, dest, slots, ctl, x1_ref, attn_ref, cot_ref, segc_ref, ln_ref, ub_ref, *rest):
    nw = len(rest) - 15
    w = rest[:nw]
    (y_ref, dx1_ref, vec_ref, dub_ref, keep, send, w_s, n2_s, n2t_s, dft_s, f_s, dn_s, stage, lsem, ssem) = rest[nw:]
    copies = load_blocks(dest, w, w_s, lsem)
    core = ctl[1]
    half = D * 2
    live = (segc_ref[...] != PAD_ID).astype(F32)
    x1 = x1_ref[...]
    xhat, rstd = row_stats(x1)
    n2 = (xhat * ln_ref[0:1] + ln_ref[1:2]).astype(BF)
    n2_s[...] = n2
    n2t_s[...] = n2.T
    dx1_ref[rows:rp, :] = jnp.zeros((rp - rows, D), F32)
    dx1_ref[0:rows, :] = cot_ref[0].astype(F32)
    dy = dx1_ref[...] * live
    dx1_ref[...] = dy
    df = dy * ln_ref[2:3]
    vec_ref[2:3] = col_sum(df)
    dfr = df.astype(BF)
    dft_s[...] = dfr.T
    for c in copies:
        c.wait()
    f = None
    n_ch = half // FCH
    inflight = [None, None]
    for t in range(2):
        fa = None
        for cc in range(n_ch):
            i = t * n_ch + cc
            lo = cc * FCH
            wu = w_s[t * D : (t + 1) * D, lo : lo + FCH]
            wd = w_s[t * D : (t + 1) * D, half + lo : half + lo + FCH]
            hid = mm(n2_s[...], wu) + ub_ref[i : i + 1]
            phi, slope = gelu_parts(hid)
            g = (hid * phi).astype(BF)
            dh = (mm(dfr, wd) * slope).astype(BF)
            dub_ref[i : i + 1] = col_sum(dh.astype(F32))
            fp = mm_nt(g, wd)
            fa = fp if fa is None else fa + fp
            dp = mm_nt(dh, wu)
            if i == 0:
                dn_s[...] = dp
            else:
                dn_s[...] += dp
            slot = i % 2
            if inflight[slot] is not None:
                for c in inflight[slot]:
                    c.wait()
            stage[slot, :, 0:FCH] = mm(n2t_s[...], dh).astype(BF)
            stage[slot, :, FCH:] = mm(dft_s[...], g).astype(BF)
            cps = store_copies(core, slots, t, stage.at[slot, :, 0:FCH], (keep, send), pl.ds(lo, FCH), ssem.at[slot, 0])
            cps += store_copies(core, slots, t, stage.at[slot, :, FCH:], (keep, send), pl.ds(half + lo, FCH), ssem.at[slot, 1])
            for c in cps:
                c.start()
            inflight[slot] = cps
        fr = fa.astype(BF).astype(F32)
        if t == 0:
            f_s[...] = fr
        else:
            f_s[...] += fr
    ffo = f_s[...] + ln_ref[3:4]
    dy = dx1_ref[...]
    vec_ref[3:4] = col_sum(dy * ffo)
    y_ref[...] = (x1_ref[...] + ln_ref[2:3] * ffo)[0:rows].astype(BF)
    dn2 = dn_s[...]
    xhat, rstd = row_stats(x1_ref[...])
    vec_ref[0:1] = col_sum(dn2 * xhat)
    vec_ref[1:2] = col_sum(dn2)
    dx1 = dy + norm_back(xhat, rstd, dn2, ln_ref[0:1])
    dx1_ref[...] = dx1
    vec_ref[4:5] = col_sum(dx1 * ln_ref[4:5])
    vec_ref[5:6] = col_sum(dx1 * attn_ref[...])
    vec_ref[6:8] = jnp.zeros((2, D), F32)
    for cps in inflight:
        for c in cps:
            c.wait()


def ffn(dest, slots, ctl, x1, attn, cotangent, segc, ln, ub, weights):
    rows = cotangent.shape[1]
    rp = x1.shape[0]
    full = lambda a: pl.BlockSpec(a.shape, lambda i, d, s, m: (0,) * a.ndim)
    wcols = weights[0].shape[2]
    n_all = ub.shape[0]
    sh = jax.ShapeDtypeStruct
    gshape = sh((BLOCKS, BROWS, wcols), BF)
    hbm = pl.BlockSpec(memory_space=pl.ANY)
    gs = pltpu.PrefetchScalarGridSpec(
        num_scalar_prefetch=3,
        grid=(1,),
        in_specs=[full(x1), full(attn), pl.BlockSpec((1, rows, D), lambda i, d, s, m: (m[0], 0, 0))]
        + [full(a) for a in (segc, ln, ub)]
        + [hbm] * len(weights),
        out_specs=[
            pl.BlockSpec((rows, D), lambda i, d, s, m: (0, 0)),
            pl.BlockSpec((rp, D), lambda i, d, s, m: (0, 0)),
            pl.BlockSpec((8, D), lambda i, d, s, m: (0, 0)),
            pl.BlockSpec((n_all, FCH), lambda i, d, s, m: (0, 0)),
            hbm, hbm,
        ],
        scratch_shapes=[
            pltpu.VMEM((2 * D, wcols), BF),
            pltpu.VMEM((rp, D), BF),
            pltpu.VMEM((D, rp), BF),
            pltpu.VMEM((D, rp), BF),
            pltpu.VMEM((rp, D), F32),
            pltpu.VMEM((rp, D), F32),
            pltpu.VMEM((2, D, 2 * FCH), BF),
            pltpu.SemaphoreType.DMA((2 * BLOCKS,)),
            pltpu.SemaphoreType.DMA((2, 2, BLOCKS)),
        ],
    )
    return pl.pallas_call(
        functools.partial(ffn_kernel, rows, rp),
        grid_spec=gs,
        out_shape=[sh((rows, D), BF), sh((rp, D), F32), sh((8, D), F32), sh((n_all, FCH), F32), gshape, gshape],
        compiler_params=pltpu.CompilerParams(vmem_limit_bytes=VMEM_LIMIT),
        cost_estimate=pl.CostEstimate(flops=17_000_000_000, bytes_accessed=28_000_000, transcendentals=4_000_000),
        name="ffn",
    )(dest, slots, ctl, x1, attn, cotangent, segc, ln, ub, *weights)


def attn_bwd_kernel(rows, rp, cp, dest, slots, ctl, x_ref, dx1_ref, q_ref, k_ref, v_ref, o_ref, lse_ref, segc_ref, segr_ref, ln_ref, *rest):
    nw = len(rest) - 15
    w = rest[:nw]
    (dx_ref, vec_ref, keep, send, w_s, x_s, q_s, do_s, bias_s, lser_s, dq_s, dk_s, dv_s, stage, sems) = rest[nw:]
    lsem, ssem = sems
    copies = load_blocks(dest, w, w_s, lsem)
    core = ctl[1]
    half = D // 2
    scale = HEAD ** (-0.5)
    x_s[0:rows, :] = x_ref[0].astype(F32)
    x_s[rows:rp, :] = jnp.zeros((rp - rows, D), F32)
    bias_s[...] = jnp.where(segc_ref[...] == segr_ref[...], 0.0, NEG)
    dar = (dx1_ref[...] * ln_ref[2:3]).astype(BF)
    dart = dar.T
    q_s[:, 0:rp, :] = q_ref[...]
    q_s[:, rp:cp, :] = jnp.zeros((6, cp - rp, 128), BF)
    do_s[:, rp:cp, :] = jnp.zeros((6, cp - rp, 128), BF)
    for c in copies:
        c.wait()
    for t in range(2):
        z = mm(dar, w_s[t * D : (t + 1) * D, 3 * half :]).astype(BF)
        for i in range(3):
            do_s[3 * t + i, 0:rp, :] = z[:, i * 128 : (i + 1) * 128]
        o_t = jnp.concatenate([o_ref[3 * t + i] for i in range(3)], axis=1)
        stage[t, :, 3 * half :] = mm(dart, o_t).astype(BF)

    def pair(p, _):
        q2 = q_s[p]
        do2 = do_s[p]
        k2 = k_ref[p]
        v2 = v_ref[p]
        dq = dk = dv = None
        for h in range(2):
            m = pair_mask(h)
            km = k2 * m
            st = mm_nt(km, q2) * (scale * LOG2E) + bias_s[...]
            pt = jnp.exp2(st - lser_s[2 * p + h])
            dpt = mm_nt(v2 * m, do2)
            delta = jnp.sum(pt * dpt, axis=0, keepdims=True)
            dst = (pt * (dpt - delta)).astype(BF)
            a = mm(pt.astype(BF), do2 * m)
            b = mm(dst, q2 * m)
            c = mm_tn(dst, km)
            dv = a if dv is None else dv + a
            dk = b if dk is None else dk + b
            dq = c if dq is None else dq + c
        dq_s[p] = (dq[0:rp] * scale).astype(BF)
        dk_s[p] = (dk * scale).astype(BF)
        dv_s[p] = dv.astype(BF)
        return 0

    for h in range(HEADS):
        lser_s[h, :, 0:rp] = lse_ref[h].reshape(1, rp)
        lser_s[h, :, rp:cp] = jnp.zeros((1, cp - rp), F32)
    lax.fori_loop(0, 6, pair, 0)
    xhat, rstd = row_stats(x_s[...])
    n1t = (xhat * ln_ref[0:1] + ln_ref[1:2]).astype(BF).T
    dn1 = None
    pend = []
    for t in range(2):
        dz = jnp.concatenate([s[3 * t + i] for s in (dq_s, dk_s, dv_s) for i in range(3)], axis=1)
        stage[t, :, 0 : 3 * half] = mm(n1t, dz).astype(BF)
        cps = store_copies(core, slots, t, stage.at[t], (keep, send), pl.ds(0, 4 * half), ssem.at[t])
        for c in cps:
            c.start()
        pend += cps
        part = mm_nt(dz, w_s[t * D : (t + 1) * D, 0 : 3 * half])
        dn1 = part if dn1 is None else dn1 + part
        vec_ref[2:3, t * half : (t + 1) * half] = col_sum(dz[:, 0:half].astype(F32))
        vec_ref[3:4, t * half : (t + 1) * half] = col_sum(dz[:, 2 * half :].astype(F32))
    vec_ref[0:1] = col_sum(dn1 * xhat)
    vec_ref[1:2] = col_sum(dn1)
    vec_ref[4:8] = jnp.zeros((4, D), F32)
    dx = dx1_ref[...] + norm_back(xhat, rstd, dn1, ln_ref[0:1])
    dx_ref[...] = dx[0:rows].astype(BF)
    for c in pend:
        c.wait()


def attn_bwd(dest, slots, ctl, tokens, dx1, q, k, v, o, lse, segc, segr, ln, weights):
    rows = tokens.shape[1]
    rp, cp = segc.shape[0], segr.shape[1]
    full = lambda a: pl.BlockSpec(a.shape, lambda i, d, s, m: (0,) * a.ndim)
    wcols = weights[0].shape[2]
    sh = jax.ShapeDtypeStruct
    gshape = sh((BLOCKS, BROWS, wcols), BF)
    hbm = pl.BlockSpec(memory_space=pl.ANY)
    gs = pltpu.PrefetchScalarGridSpec(
        num_scalar_prefetch=3,
        grid=(1,),
        in_specs=[pl.BlockSpec((1, rows, D), lambda i, d, s, m: (m[0], 0, 0))]
        + [full(a) for a in (dx1, q, k, v, o, lse, segc, segr, ln)]
        + [hbm] * len(weights),
        out_specs=[
            pl.BlockSpec((rows, D), lambda i, d, s, m: (0, 0)),
            pl.BlockSpec((8, D), lambda i, d, s, m: (0, 0)),
            hbm, hbm,
        ],
        scratch_shapes=[
            pltpu.VMEM((2 * D, wcols), BF),
            pltpu.VMEM((rp, D), F32),
            pltpu.VMEM((6, cp, 128), BF),
            pltpu.VMEM((6, cp, 128), BF),
            pltpu.VMEM((rp, cp), F32),
            pltpu.VMEM((HEADS, 1, cp), F32),
            pltpu.VMEM((6, rp, 128), BF),
            pltpu.VMEM((6, rp, 128), BF),
            pltpu.VMEM((6, rp, 128), BF),
            pltpu.VMEM((2, D, wcols), BF),
            (pltpu.SemaphoreType.DMA((2 * BLOCKS,)), pltpu.SemaphoreType.DMA((2, BLOCKS))),
        ],
    )
    return pl.pallas_call(
        functools.partial(attn_bwd_kernel, rows, rp, cp),
        grid_spec=gs,
        out_shape=[sh((rows, D), BF), sh((8, D), F32), gshape, gshape],
        compiler_params=pltpu.CompilerParams(vmem_limit_bytes=VMEM_LIMIT),
        cost_estimate=pl.CostEstimate(flops=12_000_000_000, bytes_accessed=24_000_000, transcendentals=4_500_000),
        name="attn_bwd",
    )(dest, slots, ctl, tokens, dx1, q, k, v, o, lse, segc, segr, ln, *weights)


def prepare(segment, me, ln_gain, ln_shift, qb, out_bias, layer_scale, ub):
    rows = segment.shape[1]
    rp = -(-rows // 16) * 16
    cp = -(-rp // 128) * 128
    seg = lax.dynamic_index_in_dim(segment, me, 0, keepdims=False)
    seg = jnp.concatenate([seg, jnp.full((rp - rows,), -2, jnp.int32), jnp.full((cp - rp,), -1, jnp.int32)])
    segr = seg.reshape(1, cp)
    segc = seg[:rp].reshape(rp, 1)
    half = D // 2
    ln1 = jnp.stack([ln_gain[0], ln_shift[0], layer_scale[0]])
    ln2 = jnp.stack([ln_gain[1], ln_shift[1], layer_scale[1], out_bias[1], layer_scale[0]])
    z = jnp.zeros((2, half), F32)
    qbt = jnp.concatenate([qb[0].reshape(2, half), z, qb[1].reshape(2, half)], axis=1)
    return segc, segr, ln1, ln2, qbt, out_bias[0:1], ub.reshape(-1, FCH)


def swap(v, n_tensor):
    return lax.ppermute(v, "tensor", [(i, (i + 1) % n_tensor) for i in range(n_tensor)])


def make_on_device(n_dp, n_tensor):
    def on_device(
        tokens, segment, cotangent, ln_gain, ln_shift, qkv_weight, qv_bias, out_weight,
        out_bias, layer_scale, up_weight, up_bias, down_weight,
    ):
        me = lax.axis_index("tensor")
        own_first = lambda own, other: jnp.where(me == 0, jnp.stack([own, other]), jnp.stack([other, own]))
        mine = lambda v: lax.dynamic_index_in_dim(v, me, 0, keepdims=False)
        wa = jnp.concatenate([qkv_weight[0], qkv_weight[1], qkv_weight[2], out_weight.T], axis=1)
        wf = jnp.concatenate([up_weight, down_weight.T], axis=1)
        gather = lambda w: lax.all_gather(own_first(w, swap(w, n_tensor)), "dp", axis=1, tiled=True).reshape(
            2 * BLOCKS, BROWS, w.shape[1]
        )
        wa_full = gather(wa)
        wf_full = gather(wf)
        qb = lax.all_gather(qv_bias, "tensor", axis=1, tiled=True)
        ub = lax.all_gather(up_bias, "tensor", axis=0, tiled=True)
        dest = jnp.arange(2 * BLOCKS, dtype=jnp.int32)
        slots = jnp.arange(BLOCKS, dtype=jnp.int32)
        slots = jnp.concatenate([slots, slots])
        ctl = jnp.stack([me, 0]).astype(jnp.int32)
        segc, segr, ln1, ln2, qbt, ob0, ubt = prepare(segment, me, ln_gain, ln_shift, qb, out_bias, layer_scale, ub)
        x1, attn, q, k, v, o, lse = attn_fwd(dest, ctl, tokens, segc, segr, ln1, qbt, ob0, [wa_full])
        y, dx1, vec_f, dub, f_keep, f_send = ffn(dest, slots, ctl, x1, attn, cotangent, segc, ln2, ubt, [wf_full])
        dx, vec_a, a_keep, a_send = attn_bwd(dest, slots, ctl, tokens, dx1, q, k, v, o, lse, segc, segr, ln1, [wa_full])
        out = own_first(y, swap(y, n_tensor))
        dxs = own_first(dx, swap(dx, n_tensor))

        def settle(keep, send):
            h = BLOCKS // 2
            g = jnp.stack([keep.reshape(2, h, BROWS, -1), send.reshape(2, h, BROWS, -1)], axis=2).reshape(2, D, -1)
            part = lax.psum_scatter(g, "dp", scatter_dimension=1, tiled=True)
            other = lax.dynamic_index_in_dim(part, 1 - me, 0, keepdims=False)
            return mine(part).astype(F32) + swap(other, n_tensor).astype(F32)

        gf = settle(f_keep, f_send)
        ga = settle(a_keep, a_send)
        vec = jnp.concatenate([vec_a[:4].reshape(-1), vec_f[:6].reshape(-1), dub.reshape(-1)])
        vec = lax.psum(vec, ("dp", "tensor"))
        half = D // 2
        hid_half = up_weight.shape[1]
        row = lambda i: vec[i * D : (i + 1) * D]
        g_gain0, g_shift0, g_qb, g_vb, g_gain1, g_shift1, g_ob1, g_ls1, g_ob0, g_ls0 = (row(i) for i in range(10))
        qv = lax.dynamic_slice_in_dim(jnp.stack([g_qb, g_vb]), me * half, half, axis=1)
        dubs = lax.dynamic_slice_in_dim(vec, 10 * D + me * hid_half, hid_half)
        return (
            out, dxs, jnp.stack([g_gain0, g_gain1]), jnp.stack([g_shift0, g_shift1]),
            jnp.stack([ga[:, i * half : (i + 1) * half] for i in range(3)]),
            qv, ga[:, 3 * half :].T, jnp.stack([g_ob0, g_ob1]), jnp.stack([g_ls0, g_ls1]),
            gf[:, :hid_half], dubs, gf[:, hid_half:].T,
        )

    return on_device


def solution(mesh):
    rows = P(None, "dp", None)
    wt = P("tensor", "dp")
    return jax.shard_map(
        make_on_device(mesh.shape["dp"], mesh.shape["tensor"]),
        mesh=mesh,
        in_specs=(
            rows, P(None, "dp"), rows, P(), P(), P(None, "dp", "tensor"), P(None, "tensor"), wt,
            P(), P(), P("dp", "tensor"), P("tensor"), wt,
        ),
        out_specs=(
            rows, rows, P(), P(), P(None, "dp", "tensor"), P(None, "tensor"), wt,
            P(), P(), P("dp", "tensor"), P("tensor"), wt,
        ),
        check_vma=False,
    )
```

```python
import functools

import jax
import jax.numpy as jnp
from jax import lax
from jax.experimental import pallas as pl
from jax.experimental.pallas import tpu as pltpu
from jax.sharding import PartitionSpec as P

D = 768
HEADS = 12
HEAD = D // HEADS
EPS = 1e-06
PAD_ID = 3
NEG = -1e30
BF = jnp.bfloat16
F32 = jnp.float32
LOG2E = 1.4426950408889634
VMEM_LIMIT = 58 * 1024 * 1024

BLOCKS = 16
BROWS = D // BLOCKS


def mm(a, b):
    return jnp.dot(a, b, preferred_element_type=F32)


def mm_nt(a, b):
    return lax.dot_general(a, b, (((1,), (1,)), ((), ())), preferred_element_type=F32)


def mm_tn(a, b):
    return lax.dot_general(a, b, (((0,), (0,)), ((), ())), preferred_element_type=F32)


def row_stats(v):
    mean = jnp.mean(v, axis=-1, keepdims=True)
    c = v - mean
    rstd = lax.rsqrt(jnp.mean(c * c, axis=-1, keepdims=True) + EPS)
    return c * rstd, rstd


def norm_back(xhat, rstd, dn, gain):
    dxh = dn * gain
    m1 = jnp.mean(dxh, axis=-1, keepdims=True)
    m2 = jnp.mean(dxh * xhat, axis=-1, keepdims=True)
    return rstd * (dxh - m1 - xhat * m2)


def col_sum(v):
    return jnp.sum(v, axis=0, keepdims=True)


def load_blocks(dest, parts, dst, sem, cols=slice(None)):
    copies = []
    n = 0
    for part in parts:
        for j in range(part.shape[0]):
            row = pl.multiple_of(dest[n] * BROWS, BROWS)
            copies.append(pltpu.make_async_copy(part.at[j, :, cols], dst.at[pl.ds(row, BROWS)], sem.at[n]))
            n += 1
    for c in copies:
        c.start()
    return copies


def store_copies(core, slots, t, stage, outs, cols, sem):
    keep, send = outs
    copies = []
    half = BLOCKS // 2
    for m in range(half):
        a = pl.multiple_of((2 * m + core) * BROWS, BROWS)
        b = pl.multiple_of((2 * m + 1 - core) * BROWS, BROWS)
        copies.append(pltpu.make_async_copy(stage.at[pl.ds(a, BROWS)], keep.at[slots[t * half + m], :, cols], sem.at[2 * m]))
        copies.append(pltpu.make_async_copy(stage.at[pl.ds(b, BROWS)], send.at[slots[BLOCKS + t * half + m], :, cols], sem.at[2 * m + 1]))
    return copies


def pair_mask(h, dtype=BF):
    lane = lax.broadcasted_iota(jnp.int32, (1, 2 * HEAD), 1)
    return (lane // HEAD == h).astype(dtype)


def call(kernel, name, scalars, ins, outs, scratch, us):
    def spec(shape, how):
        if how == "hbm":
            return pl.BlockSpec(memory_space=pl.ANY)
        if how == "mine":
            return pl.BlockSpec((1,) + shape[1:], lambda i, *p: (p[0][0], 0, 0))
        return pl.BlockSpec(shape, lambda i, *p: (0,) * len(shape))

    gs = pltpu.PrefetchScalarGridSpec(
        num_scalar_prefetch=len(scalars),
        grid=(1,),
        in_specs=[spec(v.shape, how) for v, how in ins],
        out_specs=[spec(shape, "hbm" if hbm else None) for shape, _, hbm in outs],
        scratch_shapes=scratch,
    )
    return pl.pallas_call(
        kernel,
        grid_spec=gs,
        out_shape=[jax.ShapeDtypeStruct(shape, dtype) for shape, dtype, _ in outs],
        compiler_params=pltpu.CompilerParams(vmem_limit_bytes=VMEM_LIMIT),
        cost_estimate=pl.CostEstimate(flops=us * 1_150_000_000, bytes_accessed=us * 1_000_000, transcendentals=0),
        name=name,
    )(*scalars, *[v for v, _ in ins])


PAIRS = HEADS // 2
HP = PAIRS // 2


def fwd_pairs(q_ref, k_ref, v_ref, bias_s, o_ref, lse_ref, lo):
    scale = (HEAD ** (-0.5)) * LOG2E

    def pair(p, _):
        q2 = q_ref[lo + p]
        k2 = k_ref[lo + p]
        v2 = v_ref[lo + p]
        acc = None
        for h in range(2):
            m = pair_mask(h)
            s = mm_nt(q2, k2 * m) * scale + bias_s[...]
            top = jnp.max(s, axis=-1, keepdims=True)
            e = jnp.exp2(s - top)
            tot = jnp.sum(e, axis=-1, keepdims=True)
            oh = mm(e.astype(BF), v2 * m) * (1.0 / tot)
            acc = oh if acc is None else acc + oh
            lse_ref[2 * p + h] = top + jnp.log2(tot)
        o_ref[p] = acc.astype(BF)
        return 0

    lax.fori_loop(0, HP, pair, 0)


def attn_fwd1_kernel(nw, rows, rp, cp, ctl, dest, x_ref, segc_ref, segr_ref, ln_ref, qb_ref, *rest):
    w = rest[:nw]
    q_ref, k_ref, v_ref, o_ref, lse_ref, w_s, x_s, bias_s, sem = rest[nw:]
    copies = load_blocks(dest, w, w_s, sem)
    x_s[0:rows, :] = x_ref[0].astype(F32)
    x_s[rows:rp, :] = jnp.zeros((rp - rows, D), F32)
    bias_s[...] = jnp.where(segc_ref[...] == segr_ref[...], 0.0, NEG)
    xhat, _ = row_stats(x_s[...])
    n1 = (xhat * ln_ref[0:1] + ln_ref[1:2]).astype(BF)
    for c in copies:
        c.wait()
    half = D // 2
    k_ref[:, rp:cp, :] = jnp.zeros((PAIRS, cp - rp, 128), BF)
    v_ref[:, rp:cp, :] = jnp.zeros((PAIRS, cp - rp, 128), BF)
    for t in range(2):
        z = mm(n1, w_s[t * D : (t + 1) * D, 0 : 3 * half]) + qb_ref[t : t + 1]
        z = z.astype(BF)
        for i in range(HP):
            q_ref[HP * t + i] = z[:, i * 128 : (i + 1) * 128]
            k_ref[HP * t + i, 0:rp, :] = z[:, half + i * 128 : half + (i + 1) * 128]
            v_ref[HP * t + i, 0:rp, :] = z[:, 2 * half + i * 128 : 2 * half + (i + 1) * 128]
    fwd_pairs(q_ref, k_ref, v_ref, bias_s, o_ref, lse_ref, 0)


def attn_fwd2_kernel(nw, rows, rp, cp, ctl, dest, x_ref, segc_ref, segr_ref, ln_ref, ob_ref, q_ref, k_ref, v_ref, o1_ref, *rest):
    w = rest[:nw]
    x1_ref, attn_ref, o_ref, lse_ref, w_s, bias_s, sem = rest[nw:]
    half = D // 2
    copies = load_blocks(dest, w, w_s, sem, slice(3 * half, 4 * half))
    bias_s[...] = jnp.where(segc_ref[...] == segr_ref[...], 0.0, NEG)
    fwd_pairs(q_ref, k_ref, v_ref, bias_s, o_ref, lse_ref, HP)
    for c in copies:
        c.wait()
    a = ob_ref[0:1]
    for t, src in enumerate((o1_ref, o_ref)):
        o_t = jnp.concatenate([src[i] for i in range(HP)], axis=1)
        a = a + mm_nt(o_t, w_s[t * D : (t + 1) * D, :]).astype(BF).astype(F32)
    attn_ref[...] = a
    x1_ref[...] = ln_ref[2:3] * a
    x1_ref[0:rows, :] += x_ref[0].astype(F32)


def attn_fwd1(ctl, dest, tokens, segc, segr, ln, qb, weights):
    rows, rp, cp = tokens.shape[1], segc.shape[0], segr.shape[1]
    wcols = weights[0].shape[2]
    return call(
        functools.partial(attn_fwd1_kernel, len(weights), rows, rp, cp), "attn_fwd1", (ctl, dest),
        [(tokens, "mine"), (segc, None), (segr, None), (ln, None), (qb, None)] + [(w, "hbm") for w in weights],
        [((PAIRS, rp, 128), BF, 0), ((PAIRS, cp, 128), BF, 0), ((PAIRS, cp, 128), BF, 0), ((HP, rp, 128), BF, 0), ((HEADS // 2, rp, 1), F32, 0)],
        [pltpu.VMEM((2 * D, wcols), BF), pltpu.VMEM((rp, D), F32), pltpu.VMEM((rp, cp), F32), pltpu.SemaphoreType.DMA((2 * BLOCKS,))],
        14,
    )


def attn_fwd2(ctl, dest, tokens, segc, segr, ln, ob, q, k, v, o1, weights):
    rows, rp, cp = tokens.shape[1], segc.shape[0], segr.shape[1]
    wcols = weights[0].shape[2]
    return call(
        functools.partial(attn_fwd2_kernel, len(weights), rows, rp, cp), "attn_fwd2", (ctl, dest),
        [(tokens, "mine"), (segc, None), (segr, None), (ln, None), (ob, None), (q, None), (k, None), (v, None), (o1, None)] + [(w, "hbm") for w in weights],
        [((rp, D), F32, 0), ((rp, D), F32, 0), ((HP, rp, 128), BF, 0), ((HEADS // 2, rp, 1), F32, 0)],
        [pltpu.VMEM((2 * D, wcols // 4), BF), pltpu.VMEM((rp, cp), F32), pltpu.SemaphoreType.DMA((2 * BLOCKS,))],
        12,
    )


def gelu_parts(h):
    x = jnp.abs(h) * 0.7071067811865476
    t = 1.0 / (1.0 + 0.3275911 * x)
    e = jnp.exp2(h * h * (-0.5 * LOG2E))
    poly = t * (0.254829592 * 0.5 + t * (-0.284496736 * 0.5 + t * (1.421413741 * 0.5 + t * (-1.453152027 * 0.5 + t * (1.061405429 * 0.5)))))
    tail = poly * e
    phi = jnp.where(h < 0, tail, 1.0 - tail)
    return phi, phi + h * e * 0.3989422804014327


FCH = 768


def ffn_kernel(rows, rp, first, ctl, dest, slots, x1_ref, cot_ref, segc_ref, ln_ref, ub_ref, *rest):
    if first:
        nw = len(rest) - 13
        w = rest[:nw]
        (f_ref, dn_ref, dub_ref, keep, send, w_s, n2_s, n2t_s, dft_s, dy_s, stage, lsem, ssem) = rest[nw:]
    else:
        attn_ref, fin_ref, dnin_ref = rest[:3]
        nw = len(rest) - 3 - 16
        w = rest[3 : 3 + nw]
        (y_ref, dx1_ref, vec_ref, dub_ref, keep, send, w_s, n2_s, n2t_s, dft_s, dy_s, stage, f_ref, dn_ref, lsem, ssem) = rest[3 + nw :]
    copies = load_blocks(dest, w, w_s, lsem)
    core = ctl[1]
    live = (segc_ref[...] != PAD_ID).astype(F32)
    xhat, rstd = row_stats(x1_ref[...])
    n2 = (xhat * ln_ref[0:1] + ln_ref[1:2]).astype(BF)
    n2_s[...] = n2
    n2t_s[...] = n2.T
    dy_s[rows:rp, :] = jnp.zeros((rp - rows, D), F32)
    dy_s[0:rows, :] = cot_ref[0].astype(F32)
    dy = dy_s[...] * live
    dy_s[...] = dy
    df = dy * ln_ref[2:3]
    dfr = df.astype(BF)
    dft_s[...] = dfr.T
    if not first:
        vec_ref[2:3] = col_sum(df)
    for c in copies:
        c.wait()
    pending = []
    for t in range(2):
        wu = w_s[t * D : (t + 1) * D, 0:FCH]
        wd = w_s[t * D : (t + 1) * D, FCH:]
        hid = mm(n2_s[...], wu) + ub_ref[t : t + 1]
        phi, slope = gelu_parts(hid)
        g = (hid * phi).astype(BF)
        dh = (mm(dfr, wd) * slope).astype(BF)
        dub_ref[t : t + 1] = col_sum(dh.astype(F32))
        fp = mm_nt(g, wd)
        dp = mm_nt(dh, wu)
        if t == 0 and first:
            f_ref[...] = fp
            dn_ref[...] = dp
        elif t == 0:
            f_ref[...] = fin_ref[...] + fp
            dn_ref[...] = dnin_ref[...] + dp
        else:
            f_ref[...] += fp
            dn_ref[...] += dp
        stage[t, :, 0:FCH] = mm(n2t_s[...], dh).astype(BF)
        stage[t, :, FCH:] = mm(dft_s[...], g).astype(BF)
        cps = store_copies(core, slots, t, stage.at[t], (keep, send), pl.ds(0, 2 * FCH), ssem.at[t])
        for c in cps:
            c.start()
        pending += cps
    if not first:
        ffo = f_ref[...] + ln_ref[3:4]
        dy = dy_s[...]
        vec_ref[3:4] = col_sum(dy * ffo)
        y_ref[...] = (x1_ref[...] + ln_ref[2:3] * ffo)[0:rows].astype(BF)
        dn2 = dn_ref[...]
        xhat, rstd = row_stats(x1_ref[...])
        vec_ref[0:1] = col_sum(dn2 * xhat)
        vec_ref[1:2] = col_sum(dn2)
        dx1 = dy + norm_back(xhat, rstd, dn2, ln_ref[0:1])
        dx1_ref[...] = dx1
        vec_ref[4:5] = col_sum(dx1 * ln_ref[4:5])
        vec_ref[5:6] = col_sum(dx1 * attn_ref[...])
        vec_ref[6:8] = jnp.zeros((2, D), F32)
    for c in pending:
        c.wait()


def ffn(first, ctl, dest, slots, x1, cotangent, segc, ln, ub, more, weights):
    rows, rp = cotangent.shape[1], x1.shape[0]
    wcols = weights[0].shape[2]
    if first:
        outs = [((rp, D), F32, 0), ((rp, D), F32, 0)]
    else:
        outs = [((rows, D), BF, 0), ((rp, D), F32, 0), ((8, D), F32, 0)]
    outs += [((2, FCH), F32, 0)] + [((BLOCKS, BROWS, wcols), BF, 1)] * 2
    return call(
        functools.partial(ffn_kernel, rows, rp, first), "ffn_first" if first else "ffn_last", (ctl, dest, slots),
        [(x1, None), (cotangent, "mine"), (segc, None), (ln, None), (ub, None)] + [(v, None) for v in more] + [(w, "hbm") for w in weights],
        outs,
        [
            pltpu.VMEM((2 * D, wcols), BF), pltpu.VMEM((rp, D), BF), pltpu.VMEM((D, rp), BF), pltpu.VMEM((D, rp), BF),
            pltpu.VMEM((rp, D), F32), pltpu.VMEM((2, D, 2 * FCH), BF),
        ]
        + ([] if first else [pltpu.VMEM((rp, D), F32)] * 2)
        + [pltpu.SemaphoreType.DMA((2 * BLOCKS,)), pltpu.SemaphoreType.DMA((2, BLOCKS))],
        20,
    )


def attn_bwd_kernel(nw, t, rp, cp, ctl, dest, dx1_ref, q_ref, k_ref, v_ref, lse_ref, segc_ref, segr_ref, ln_ref, *rest):
    w = rest[:nw]
    dq_ref, dk_ref, dv_ref, w_s, do_s, q_s, bias_s, lser_s, sem = rest[nw:]
    half = D // 2
    copies = load_blocks(dest, w, w_s, sem, slice(3 * half, 4 * half))
    scale = HEAD ** (-0.5)
    bias_s[...] = jnp.where(segc_ref[...] == segr_ref[...], 0.0, NEG)
    q_s[:, 0:rp, :] = q_ref[HP * t : HP * (t + 1)]
    q_s[:, rp:cp, :] = jnp.zeros((HP, cp - rp, 128), BF)
    do_s[:, rp:cp, :] = jnp.zeros((HP, cp - rp, 128), BF)
    dar = (dx1_ref[...] * ln_ref[2:3]).astype(BF)
    for h in range(HEADS // 2):
        lser_s[h, :, 0:rp] = lse_ref[h].reshape(1, rp)
        lser_s[h, :, rp:cp] = jnp.zeros((1, cp - rp), F32)
    for c in copies:
        c.wait()
    z = mm(dar, w_s[t * D : (t + 1) * D, :]).astype(BF)
    for i in range(HP):
        do_s[i, 0:rp, :] = z[:, i * 128 : (i + 1) * 128]

    def pair(p, _):
        q2 = q_s[p]
        do2 = do_s[p]
        k2 = k_ref[HP * t + p, 0:rp, :]
        v2 = v_ref[HP * t + p, 0:rp, :]
        dq = dk = dv = None
        for h in range(2):
            m = pair_mask(h)
            km = k2 * m
            st = mm_nt(km, q2) * (scale * LOG2E) + bias_s[...]
            pt = jnp.exp2(st - lser_s[2 * p + h])
            dpt = mm_nt(v2 * m, do2)
            delta = jnp.sum(pt * dpt, axis=0, keepdims=True)
            dst = (pt * (dpt - delta)).astype(BF)
            a = mm(pt.astype(BF), do2 * m)
            b = mm(dst, q2 * m)
            c = mm_tn(dst, km)
            dv = a if dv is None else dv + a
            dk = b if dk is None else dk + b
            dq = c if dq is None else dq + c
        dq_ref[p] = (dq[0:rp] * scale).astype(BF)
        dk_ref[p] = (dk * scale).astype(BF)
        dv_ref[p] = dv.astype(BF)
        return 0

    lax.fori_loop(0, HP, pair, 0)


def attn_bwd(t, ctl, dest, dx1, q, k, v, lse, segc, segr, ln, weights):
    rp, cp = segc.shape[0], segr.shape[1]
    wcols = weights[0].shape[2]
    return call(
        functools.partial(attn_bwd_kernel, len(weights), t, rp, cp), "attn_bwd", (ctl, dest),
        [(e, None) for e in (dx1, q, k, v, lse, segc, segr, ln)] + [(w, "hbm") for w in weights],
        [((HP, rp, 128), BF, 0)] * 3,
        [
            pltpu.VMEM((2 * D, wcols // 4), BF), pltpu.VMEM((HP, cp, 128), BF), pltpu.VMEM((HP, cp, 128), BF),
            pltpu.VMEM((rp, cp), F32), pltpu.VMEM((HEADS // 2, 1, cp), F32), pltpu.SemaphoreType.DMA((2 * BLOCKS,)),
        ],
        15,
    )


def attn_grad_kernel(rows, rp, ctl, slots, x_ref, dx1_ref, o1_ref, o2_ref, dq1, dk1, dv1, dq2, dk2, dv2, ln_ref, keep, send, stage, x_s, ssem):
    core = ctl[1]
    half = D // 2
    x_s[0:rows, :] = x_ref[0].astype(F32)
    x_s[rows:rp, :] = jnp.zeros((rp - rows, D), F32)
    dart = (dx1_ref[...] * ln_ref[2:3]).astype(BF).T
    xhat, _ = row_stats(x_s[...])
    n1t = (xhat * ln_ref[0:1] + ln_ref[1:2]).astype(BF).T
    pend = []
    for t, (o, dz) in enumerate(((o1_ref, (dq1, dk1, dv1)), (o2_ref, (dq2, dk2, dv2)))):
        o_t = jnp.concatenate([o[i] for i in range(HP)], axis=1)
        stage[t, :, 3 * half :] = mm(dart, o_t).astype(BF)
        z = jnp.concatenate([e[i] for e in dz for i in range(HP)], axis=1)
        stage[t, :, 0 : 3 * half] = mm(n1t, z).astype(BF)
        cps = store_copies(core, slots, t, stage.at[t], (keep, send), pl.ds(0, 4 * half), ssem.at[t])
        for c in cps:
            c.start()
        pend += cps
    for c in pend:
        c.wait()


def attn_grad(ctl, slots, tokens, dx1, o1, o2, dz1, dz2, ln):
    rows, rp = tokens.shape[1], dx1.shape[0]
    wcols = 2 * D
    return call(
        functools.partial(attn_grad_kernel, rows, rp), "attn_grad", (ctl, slots),
        [(tokens, "mine")] + [(e, None) for e in (dx1, o1, o2, *dz1, *dz2, ln)],
        [((BLOCKS, BROWS, wcols), BF, 1)] * 2,
        [pltpu.VMEM((2, D, wcols), BF), pltpu.VMEM((rp, D), F32), pltpu.SemaphoreType.DMA((2, BLOCKS))],
        10,
    )


def input_grad_kernel(nw, rows, rp, ctl, dest, x_ref, dx1_ref, dq1, dk1, dv1, dq2, dk2, dv2, ln_ref, *rest):
    w = rest[:nw]
    dx_ref, vec_ref, w_s, x_s, sem = rest[nw:]
    half = D // 2
    copies = load_blocks(dest, w, w_s, sem, slice(0, 3 * half))
    x_s[0:rows, :] = x_ref[0].astype(F32)
    x_s[rows:rp, :] = jnp.zeros((rp - rows, D), F32)
    xhat, rstd = row_stats(x_s[...])
    for c in copies:
        c.wait()
    dn1 = None
    for t, dz in enumerate(((dq1, dk1, dv1), (dq2, dk2, dv2))):
        z = jnp.concatenate([e[i] for e in dz for i in range(HP)], axis=1)
        part = mm_nt(z, w_s[t * D : (t + 1) * D, :])
        dn1 = part if dn1 is None else dn1 + part
        vec_ref[2:3, t * half : (t + 1) * half] = col_sum(z[:, 0:half].astype(F32))
        vec_ref[3:4, t * half : (t + 1) * half] = col_sum(z[:, 2 * half :].astype(F32))
    vec_ref[0:1] = col_sum(dn1 * xhat)
    vec_ref[1:2] = col_sum(dn1)
    vec_ref[4:8] = jnp.zeros((4, D), F32)
    dx = dx1_ref[...] + norm_back(xhat, rstd, dn1, ln_ref[0:1])
    dx_ref[...] = dx[0:rows].astype(BF)


def input_grad(ctl, dest, tokens, dx1, dz1, dz2, ln, weights):
    rows, rp = tokens.shape[1], dx1.shape[0]
    wcols = weights[0].shape[2]
    return call(
        functools.partial(input_grad_kernel, len(weights), rows, rp), "input_grad", (ctl, dest),
        [(tokens, "mine")] + [(e, None) for e in (dx1, *dz1, *dz2, ln)] + [(w, "hbm") for w in weights],
        [((rows, D), BF, 0), ((8, D), F32, 0)],
        [pltpu.VMEM((2 * D, wcols * 3 // 4), BF), pltpu.VMEM((rp, D), F32), pltpu.SemaphoreType.DMA((2 * BLOCKS,))],
        10,
    )


def prepare(segment, me, ln_gain, ln_shift, qb, out_bias, layer_scale):
    rows = segment.shape[1]
    rp = -(-rows // 16) * 16
    cp = -(-rp // 128) * 128
    seg = lax.dynamic_index_in_dim(segment, me, 0, keepdims=False)
    seg = jnp.concatenate([seg, jnp.full((rp - rows,), -2, jnp.int32), jnp.full((cp - rp,), -1, jnp.int32)])
    segr = seg.reshape(1, cp)
    segc = seg[:rp].reshape(rp, 1)
    half = D // 2
    ln1 = jnp.stack([ln_gain[0], ln_shift[0], layer_scale[0]])
    ln2 = jnp.stack([ln_gain[1], ln_shift[1], layer_scale[1], out_bias[1], layer_scale[0]])
    z = jnp.zeros((2, half), F32)
    qbt = jnp.concatenate([qb[0].reshape(2, half), z, qb[1].reshape(2, half)], axis=1)
    return segc, segr, ln1, ln2, qbt, out_bias[0:1]


def swap(v, n_tensor):
    return lax.ppermute(v, "tensor", [(i, (i + 1) % n_tensor) for i in range(n_tensor)])


def after(v, *done):
    return lax.optimization_barrier((v, done))[0]


class Grid:
    axes = ("dp", "tensor")
    places = [(z, y, c, t) for z in range(4) for y in range(2) for c in range(2) for t in range(2)]

    def number(self, p):
        return ((p[0] * 2 + p[1]) * 2 + p[2]) * 2 + p[3]

    def x(self, p):
        return p[0], p[1], p[2], 1 - p[3]

    def y(self, p):
        return p[0], 1 - p[1], p[2], p[3]

    def core(self, p):
        return p[0], p[1], 1 - p[2], p[3]

    def first(self, p):
        return self.y(p) if p[2] else self.x(p)

    def second(self, p):
        return self.x(p) if p[2] else self.y(p)

    def down(self, p):
        return (p[0] + 3) % 4, p[1], p[2], p[3]

    def z1(self, p):
        return p[0] ^ 1, p[1], p[2], p[3]

    def z2(self, p):
        return p[0] ^ 2, p[1], p[2], p[3]

    def send(self, v, to):
        return lax.ppermute(v, self.axes, [(self.number(p), self.number(to(p))) for p in self.places])

    def line(self, p):
        return [((p[0] + k) % 4, p[1], p[2], p[3]) for k in range(4)]

    def held(self, p):
        b = self.second(p)
        return self.line(p) + self.line(self.first(p)) + self.line(b) + self.line(self.first(b))

    def tables(self):
        where = lambda q: q[3] * BLOCKS + (q[0] * 2 + q[1]) * 2 + q[2]
        dest, slots = [], []
        for p in self.places:
            mine, theirs = self.held(p), self.held(self.core(p))
            dest.append([where(q) for q in mine + theirs])
            at = {where(q): i for i, q in enumerate(mine)} | {where(q): i for i, q in enumerate(theirs)}
            half = BLOCKS // 2
            slots.append(
                [at[t * BLOCKS + 2 * m + p[2]] for t in range(2) for m in range(half)]
                + [at[t * BLOCKS + 2 * m + 1 - p[2]] for t in range(2) for m in range(half)]
            )
        return jnp.array(dest, jnp.int32), jnp.array(slots, jnp.int32)

    def total_steps(self):
        return self.core, self.x, self.y, self.z1, self.z2


def wide(v):
    return v.astype(F32)


class Reduce:
    def __init__(self, net, keep, sent):
        self.net, self.terms, self.sent = net, [keep], sent
        self.order = [net.core, net.second, net.first, net.down, net.down, net.down]
        self.stage = 0

    def begin(self):
        self.got = self.net.send(self.sent, self.order[0])

    def start(self, *dep):
        got = after(self.got, *dep)
        self.stage += 1
        n = self.stage
        if n <= 2:
            self.terms.append(got)
            half = BLOCKS >> n
            self.sent = sum(wide(v[half : 2 * half]) for v in self.terms).astype(BF)
        elif n == 3:
            self.terms.append(got)
            self.sent = sum(wide(v[1]) for v in self.terms).astype(BF)
        else:
            self.sent = (sum(wide(v[n - 2]) for v in self.terms) + wide(got)).astype(BF)
        self.got = self.net.send(self.sent, self.order[n])

    def result(self):
        return sum(wide(v[0]) for v in self.terms) + wide(self.got)


class Plain:
    def __init__(self, n_tensor):
        self.n_tensor = n_tensor

    def gather(self, w):
        me = lax.axis_index("tensor")
        other = swap(w, self.n_tensor)
        both = jnp.where(me == 0, jnp.stack([w, other]), jnp.stack([other, w]))
        full = lax.all_gather(both, "dp", axis=1, tiled=True)
        return [full.reshape(2 * BLOCKS, BROWS, w.shape[1])]

    def settle(self, keep, sent):
        me = lax.axis_index("tensor")
        h = BLOCKS // 2
        g = jnp.stack([keep.reshape(2, h, BROWS, -1), sent.reshape(2, h, BROWS, -1)], axis=2).reshape(2, D, -1)
        part = lax.psum_scatter(g, "dp", scatter_dimension=1, tiled=True).astype(F32)
        return jnp.where(me == 0, part[0], part[1]) + swap(jnp.where(me == 0, part[1], part[0]), self.n_tensor)

    def total(self, v):
        return lax.psum(v, ("dp", "tensor"))


def make_on_device(n_dp, n_tensor):
    def on_device(
        tokens, segment, cotangent, ln_gain, ln_shift, qkv_weight, qv_bias, out_weight,
        out_bias, layer_scale, up_weight, up_bias, down_weight,
    ):
        me = lax.axis_index("tensor")
        own_first = lambda own, other, axis=0: jnp.where(me == 0, jnp.stack([own, other], axis), jnp.stack([other, own], axis))
        both = lambda own, other: own_first(own, other, 1).transpose(1, 0, 2)
        half = D // 2
        hid_half = up_weight.shape[1]
        wa = jnp.concatenate([qkv_weight[0], qkv_weight[1], qkv_weight[2], out_weight.T], axis=1)
        small = jnp.concatenate([qv_bias.reshape(-1), up_bias])

        def pack_ffn(up, down):
            down_t = down.T
            return [jnp.concatenate([up[:, lo : lo + FCH], down_t[:, lo : lo + FCH]], axis=1) for lo in range(0, hid_half, FCH)]

        def consts(small, segment):
            small = own_first(small, swap(small, n_tensor))
            qb = small[:, : 2 * half].reshape(2, 2, half).transpose(1, 0, 2).reshape(2, D)
            ub = small[:, 2 * half :]
            return (ub[:, :FCH], ub[:, FCH:]) + prepare(segment, me, ln_gain, ln_shift, qb, out_bias, layer_scale)

        def results(out, dxs, vec_a, vec_f, dub, ga, gup, gdown):
            g_gain0, g_shift0, g_qb, g_vb = (vec_a[i] for i in range(4))
            g_gain1, g_shift1, g_ob1, g_ls1, g_ob0, g_ls0 = (vec_f[i] for i in range(6))
            qv = lax.dynamic_slice_in_dim(jnp.stack([g_qb, g_vb]), me * half, half, axis=1)
            dubs = lax.dynamic_index_in_dim(dub.reshape(2, hid_half), me, 0, keepdims=False)
            return (
                out, dxs, jnp.stack([g_gain0, g_gain1]), jnp.stack([g_shift0, g_shift1]),
                jnp.stack([ga[:, i * half : (i + 1) * half] for i in range(3)]),
                qv, ga[:, 3 * half :].T, jnp.stack([g_ob0, g_ob1]), jnp.stack([g_ls0, g_ls1]),
                gup, dubs, gdown.T,
            )

        if n_dp != 16 or n_tensor != 2:
            net = Plain(n_tensor)
            dest = jnp.arange(2 * BLOCKS, dtype=jnp.int32)
            slots = jnp.concatenate([jnp.arange(BLOCKS, dtype=jnp.int32)] * 2)
            ctl = jnp.stack([me, 0]).astype(jnp.int32)
            wa = net.gather(wa)
            wf = [net.gather(w) for w in pack_ffn(up_weight, down_weight)]
            ub1, ub2, segc, segr, ln1, ln2, qbt, ob0 = consts(small, segment)
            q, k, v, o1, lse1 = attn_fwd1(ctl, dest, tokens, segc, segr, ln1, qbt, wa)
            x1, attn, o2, lse2 = attn_fwd2(ctl, dest, tokens, segc, segr, ln1, ob0, q, k, v, o1, wa)
            f, dn, dub1, k1, s1 = ffn(True, ctl, dest, slots, x1, cotangent, segc, ln2, ub1, (), wf[0])
            y, dx1, vec_f, dub2, k2, s2 = ffn(False, ctl, dest, slots, x1, cotangent, segc, ln2, ub2, (attn, f, dn), wf[1])
            dz1 = attn_bwd(0, ctl, dest, dx1, q, k, v, lse1, segc, segr, ln1, wa)
            dz2 = attn_bwd(1, ctl, dest, dx1, q, k, v, lse2, segc, segr, ln1, wa)
            ka, sa = attn_grad(ctl, slots, tokens, dx1, o1, o2, dz1, dz2, ln1)
            dx, vec_a = input_grad(ctl, dest, tokens, dx1, dz1, dz2, ln1, wa)
            gf1, gf2, ga = net.settle(k1, s1), net.settle(k2, s2), net.settle(ka, sa)
            dub = jnp.concatenate([dub1, dub2], axis=1)
            vec_a, vec_f, dub = (net.total(e) for e in (vec_a, vec_f, dub))
            gup = jnp.concatenate([gf1[:, :FCH], gf2[:, :FCH]], axis=1)
            gdown = jnp.concatenate([gf1[:, FCH:], gf2[:, FCH:]], axis=1)
            return results(both(y, swap(y, n_tensor)), both(dx, swap(dx, n_tensor)), vec_a, vec_f, dub, ga, gup, gdown)

        net = Grid()
        place = lax.axis_index("dp") * 2 + me
        b1 = net.send(wa, net.down)
        up_weight, down_weight, segment, small, tokens, cotangent, place = after(
            (up_weight, down_weight, segment, small, tokens, cotangent, place), b1
        )
        b2 = net.send(b1, net.down)
        b3 = net.send(b2, net.down)
        w2 = jnp.stack(pack_ffn(up_weight, down_weight))
        w2, b3 = after((w2, b3), b3)
        s = jnp.stack([wa, b1, b2, b3])
        ra = net.send(s, net.first)
        f1 = net.send(after(w2, s), net.down)
        tokens, small, segment, place = after((tokens, small, segment, place), s)
        ub1, ub2, segc, segr, ln1, ln2, qbt, ob0 = consts(small, segment)
        dest, slots = net.tables()
        dest = lax.dynamic_index_in_dim(dest, place, 0, keepdims=False)
        slots = lax.dynamic_index_in_dim(slots, place, 0, keepdims=False)
        ctl = jnp.stack([me, lax.axis_index("dp") % 2]).astype(jnp.int32)
        ra, f1 = after((ra, f1), f1, segc, dest, qbt)
        s = jnp.concatenate([s, ra])
        r = net.send(s, net.second)
        sc = net.send(s, net.core)
        f2 = net.send(after(f1, s), net.down)
        cotangent = after(cotangent, s)
        r, f2 = after((r, f2), sc)
        rc = net.send(r, net.core)
        f3 = net.send(after(f2, r), net.down)
        wa = [s, r, sc, rc]
        fs = after(jnp.stack([w2, f1, f2, f3], axis=1), rc)
        fr = net.send(fs, net.first)
        wa = after(wa, fs)
        q, k, v, o1, lse1 = attn_fwd1(ctl, dest, tokens, segc, segr, ln1, qbt, wa)
        q, fr = after((q, fr), o1)
        fs1, fs2 = (jnp.concatenate([fs[j], fr[j]]) for j in range(2))
        r1 = net.send(fs1, net.second)
        c1 = net.send(fs1, net.core)
        q = after(q, fs1)
        x1, attn, o2, lse2 = attn_fwd2(ctl, dest, tokens, segc, segr, ln1, ob0, q, k, v, o1, wa)
        r1, fs2, c1 = after((r1, fs2, c1), x1)
        w1 = [fs1, r1, c1, net.send(r1, net.core)]
        r2 = net.send(fs2, net.second)
        c2 = net.send(fs2, net.core)
        f, dn, dub1, k1, s1 = ffn(True, ctl, dest, slots, x1, cotangent, segc, ln2, ub1, (), w1)
        r2, c2 = after((r2, c2), f)
        w2 = [fs2, r2, c2, net.send(r2, net.core)]
        g1 = Reduce(net, k1, s1)
        g1.begin()
        y, dx1, vec_f, dub2, k2, s2 = ffn(False, ctl, dest, slots, x1, cotangent, segc, ln2, ub2, (attn, f, dn), w2)
        g2 = Reduce(net, k2, s2)
        g2.begin()
        g1.start(dx1)
        dx1 = after(dx1, g1.sent)
        dz1 = attn_bwd(0, ctl, dest, dx1, q, k, v, lse1, segc, segr, ln1, wa)
        y_other = swap(after(y, g1.got), n_tensor)
        g2.start(dz1[0], g1.got)
        dx1 = after(dx1, dz1[0], g2.sent)
        dz2 = attn_bwd(1, ctl, dest, dx1, q, k, v, lse2, segc, segr, ln1, wa)
        dz2, g1.got, g2.got = after((dz2, g1.got, g2.got))
        g1.terms.append(g1.got)
        g2.terms.append(g2.got)
        gf = Reduce(net, None, None)
        gf.terms = [jnp.concatenate([e[:8], h[:8]], axis=-1) for e, h in zip(g1.terms, g2.terms)]
        gf.stage = 2
        gf.sent = sum(wide(e[4:8]) for e in gf.terms).astype(BF)
        gf.got = net.send(gf.sent, net.first)
        dx1 = after(dx1, gf.sent, dz2[0])
        ka, sa = attn_grad(ctl, slots, tokens, dx1, o1, o2, dz1, dz2, ln1)
        g = Reduce(net, ka, sa)
        g.begin()
        gf.start(ka)
        dx1 = after(dx1, gf.sent, ka)
        dx, vec_a = input_grad(ctl, dest, tokens, dx1, dz1, dz2, ln1, wa)
        vec = jnp.concatenate([vec_a[:4], vec_f[:6], jnp.concatenate([dub1, dub2], axis=1).reshape(-1, D)])
        vec_steps = net.total_steps()

        def add(v, to, *dep):
            v = after(v, *dep)
            return v + net.send(v, to)

        g.start(dx, gf.got)
        gf.start(g.sent)
        vec = add(add(vec, vec_steps[0], g.sent), vec_steps[1])
        out = both(*after((y, y_other), g.sent))
        g.start(gf.got, vec)
        gf.start(g.sent)
        vec = add(add(vec, vec_steps[2], g.sent), vec_steps[3])
        g.start(gf.got, vec)
        vec = add(vec, vec_steps[4], g.sent)
        dx_other = swap(after(dx, g.sent), n_tensor)
        gff = after(gf.result(), g.sent)
        g.start(vec)
        g.start()
        dxs = both(dx, dx_other)
        w = 2 * FCH
        gup = jnp.concatenate([gff[:, :FCH], gff[:, w : w + FCH]], axis=1)
        gdown = jnp.concatenate([gff[:, FCH:w], gff[:, w + FCH :]], axis=1)
        return results(out, dxs, vec[:4], vec[4:10], vec[10:], g.result(), gup, gdown)

    return on_device


def solution(mesh):
    rows = P(None, "dp", None)
    wt = P("tensor", "dp")
    return jax.shard_map(
        make_on_device(mesh.shape["dp"], mesh.shape["tensor"]),
        mesh=mesh,
        in_specs=(
            rows, P(None, "dp"), rows, P(), P(), P(None, "dp", "tensor"), P(None, "tensor"), wt,
            P(), P(), P("dp", "tensor"), P("tensor"), wt,
        ),
        out_specs=(
            rows, rows, P(), P(), P(None, "dp", "tensor"), P(None, "tensor"), wt,
            P(), P(), P("dp", "tensor"), P("tensor"), wt,
        ),
        check_vma=False,
    )
```

```python
import functools

import jax
import jax.numpy as jnp
from jax import lax
from jax.experimental import pallas as pl
from jax.experimental.pallas import tpu as pltpu
from jax.sharding import PartitionSpec as P

D = 768
HEADS = 12
HEAD = D // HEADS
EPS = 1e-06
PAD_ID = 3
NEG = -1e30
BF = jnp.bfloat16
F32 = jnp.float32
LOG2E = 1.4426950408889634

BLOCKS = 16
BROWS = D // BLOCKS


def mm(a, b):
    return jnp.dot(a, b, preferred_element_type=F32)


def mm_nt(a, b):
    return lax.dot_general(a, b, (((1,), (1,)), ((), ())), preferred_element_type=F32)


def mm_tn(a, b):
    return lax.dot_general(a, b, (((0,), (0,)), ((), ())), preferred_element_type=F32)


def row_stats(v):
    mean = jnp.mean(v, axis=-1, keepdims=True)
    c = v - mean
    rstd = lax.rsqrt(jnp.mean(c * c, axis=-1, keepdims=True) + EPS)
    return c * rstd, rstd


def norm_back(xhat, rstd, dn, gain):
    dxh = dn * gain
    m1 = jnp.mean(dxh, axis=-1, keepdims=True)
    m2 = jnp.mean(dxh * xhat, axis=-1, keepdims=True)
    return rstd * (dxh - m1 - xhat * m2)


def col_sum(v):
    return jnp.sum(v, axis=0, keepdims=True)


def load_blocks(dest, parts, dst, sem, cols=slice(None)):
    copies = []
    n = 0
    for part in parts:
        for j in range(part.shape[0]):
            row = pl.multiple_of(dest[n] * BROWS, BROWS)
            copies.append(pltpu.make_async_copy(part.at[j, :, cols], dst.at[pl.ds(row, BROWS)], sem.at[n]))
            n += 1
    for c in copies:
        c.start()
    return copies


def store_copies(core, slots, t, stage, outs, cols, sem):
    keep, send = outs
    copies = []
    half = BLOCKS // 2
    for m in range(half):
        a = pl.multiple_of((2 * m + core) * BROWS, BROWS)
        b = pl.multiple_of((2 * m + 1 - core) * BROWS, BROWS)
        copies.append(pltpu.make_async_copy(stage.at[pl.ds(a, BROWS)], keep.at[slots[t * half + m], :, cols], sem.at[2 * m]))
        copies.append(pltpu.make_async_copy(stage.at[pl.ds(b, BROWS)], send.at[slots[BLOCKS + t * half + m], :, cols], sem.at[2 * m + 1]))
    return copies


def pair_mask(h, dtype=BF):
    lane = lax.broadcasted_iota(jnp.int32, (1, 2 * HEAD), 1)
    return (lane // HEAD == h).astype(dtype)


def call(kernel, name, scalars, ins, outs, scratch, us, vmem=32):
    spaces = {None: pltpu.VMEM, 0: pltpu.VMEM, 1: pl.ANY, "hbm": pl.ANY, "far": pltpu.HBM}
    at = lambda how: pl.BlockSpec(memory_space=spaces[how])
    return pl.pallas_call(
        kernel,
        in_specs=[pl.BlockSpec(memory_space=pltpu.SMEM)] * len(scalars) + [at(how) for _, how in ins],
        out_specs=[at(how) for _, _, how in outs],
        out_shape=[jax.ShapeDtypeStruct(shape, dtype) for shape, dtype, _ in outs],
        scratch_shapes=scratch,
        compiler_params=pltpu.CompilerParams(vmem_limit_bytes=vmem * 1024 * 1024),
        cost_estimate=pl.CostEstimate(flops=us * 5_000_000_000, bytes_accessed=us * 1_000_000, transcendentals=0),
        name=name,
    )(*scalars, *[v for v, _ in ins])


PAIRS = HEADS // 2
HP = PAIRS // 2


def fwd_pairs(q_ref, k_ref, v_ref, bias_s, o_ref, lse_ref):
    scale = (HEAD ** (-0.5)) * LOG2E

    def pair(p, _):
        q2 = q_ref[p]
        k2 = k_ref[p]
        v2 = v_ref[p]
        acc = None
        for h in range(2):
            m = pair_mask(h)
            s = mm_nt(q2, k2 * m) * scale + bias_s[...]
            top = jnp.max(s, axis=-1, keepdims=True)
            e = jnp.exp2(s - top)
            tot = jnp.sum(e, axis=-1, keepdims=True)
            oh = mm(e.astype(BF), v2 * m) * (1.0 / tot)
            acc = oh if acc is None else acc + oh
            lse_ref[2 * p + h, :, 0 : top.shape[0]] = (top + jnp.log2(tot)).reshape(1, -1)
        o_ref[p] = acc.astype(BF)
        return 0

    lse_ref[...] = jnp.zeros_like(lse_ref)
    lax.fori_loop(0, HP, pair, 0)


def half_heads(t, src, dst, sem):
    copies = []
    for i, (a, b) in enumerate(zip(src, dst)):
        n = min(a.shape[1], b.shape[1])
        copies.append(pltpu.make_async_copy(a.at[HP * t : HP * (t + 1), 0:n], b.at[:, 0:n], sem.at[i]))
    for c in copies:
        c.start()
    return copies


def attn_fwd1_kernel(nw, rows, rp, cp, ctl, dest, x_ref, segc_ref, segr_ref, ln_ref, qb_ref, *rest):
    w = rest[:nw]
    qh, kh, vh, o_ref, lse_ref, w_s, x_s, bias_s, q_ref, k_ref, v_ref, sem, osem = rest[nw:]
    copies = load_blocks(dest, w, w_s, sem)
    x_s[0:rows, :] = x_ref[...].astype(F32)
    x_s[rows:rp, :] = jnp.zeros((rp - rows, D), F32)
    bias_s[...] = jnp.where(segc_ref[...] == segr_ref[...], 0.0, NEG)
    xhat, _ = row_stats(x_s[...])
    n1 = (xhat * ln_ref[0:1] + ln_ref[1:2]).astype(BF)
    for c in copies:
        c.wait()
    half = D // 2
    k_ref[:, rp:cp, :] = jnp.zeros((PAIRS, cp - rp, 128), BF)
    v_ref[:, rp:cp, :] = jnp.zeros((PAIRS, cp - rp, 128), BF)
    for t in range(2):
        z = mm(n1, w_s[t * D : (t + 1) * D, 0 : 3 * half]) + qb_ref[t : t + 1]
        z = z.astype(BF)
        for i in range(HP):
            q_ref[HP * t + i] = z[:, i * 128 : (i + 1) * 128]
            k_ref[HP * t + i, 0:rp, :] = z[:, half + i * 128 : half + (i + 1) * 128]
            v_ref[HP * t + i, 0:rp, :] = z[:, 2 * half + i * 128 : 2 * half + (i + 1) * 128]
    out = [pltpu.make_async_copy(a, b, osem.at[i]) for i, (a, b) in enumerate(((q_ref, qh), (k_ref, kh), (v_ref, vh)))]
    for c in out:
        c.start()
    fwd_pairs(q_ref, k_ref, v_ref, bias_s, o_ref, lse_ref)
    for c in out:
        c.wait()


def attn_fwd2_kernel(nw, rows, rp, cp, ctl, dest, x_ref, segc_ref, segr_ref, ln_ref, ob_ref, qh, kh, vh, o1_ref, *rest):
    w = rest[:nw]
    x1_ref, attn_ref, o_ref, lse_ref, w_s, bias_s, q_s, k_s, v_s, sem, isem = rest[nw:]
    heads = half_heads(1, (qh, kh, vh), (q_s, k_s, v_s), isem)
    half = D // 2
    copies = load_blocks(dest, w, w_s, sem, slice(3 * half, 4 * half))
    bias_s[...] = jnp.where(segc_ref[...] == segr_ref[...], 0.0, NEG)
    for c in heads:
        c.wait()
    fwd_pairs(q_s, k_s, v_s, bias_s, o_ref, lse_ref)
    for c in copies:
        c.wait()
    a = ob_ref[0:1]
    for t, src in enumerate((o1_ref, o_ref)):
        o_t = jnp.concatenate([src[i] for i in range(HP)], axis=1)
        a = a + mm_nt(o_t, w_s[t * D : (t + 1) * D, :]).astype(BF).astype(F32)
    attn_ref[...] = a
    x1_ref[...] = ln_ref[2:3] * a
    x1_ref[0:rows, :] += x_ref[...].astype(F32)


def attn_fwd1(ctl, dest, tokens, segc, segr, ln, qb, weights):
    rows, rp, cp = tokens.shape[0], segc.shape[0], segr.shape[1]
    wcols = weights[0].shape[2]
    return call(
        functools.partial(attn_fwd1_kernel, len(weights), rows, rp, cp), "attn_fwd1", (ctl, dest),
        [(tokens, None), (segc, None), (segr, None), (ln, None), (qb, None)] + [(w, "hbm") for w in weights],
        [((PAIRS, rp, 128), BF, "far"), ((PAIRS, cp, 128), BF, "far"), ((PAIRS, cp, 128), BF, "far"), ((HP, rp, 128), BF, 0), ((HEADS // 2, 1, cp), F32, 0)],
        [
            pltpu.VMEM((2 * D, wcols), BF), pltpu.VMEM((rp, D), F32), pltpu.VMEM((rp, cp), F32), pltpu.VMEM((PAIRS, rp, 128), BF), pltpu.VMEM((PAIRS, cp, 128), BF), pltpu.VMEM((PAIRS, cp, 128), BF),
            pltpu.SemaphoreType.DMA((2 * BLOCKS,)), pltpu.SemaphoreType.DMA((3,)),
        ],
        14,
    )


def attn_fwd2(ctl, dest, tokens, segc, segr, ln, ob, q, k, v, o1, weights):
    rows, rp, cp = tokens.shape[0], segc.shape[0], segr.shape[1]
    wcols = weights[0].shape[2]
    return call(
        functools.partial(attn_fwd2_kernel, len(weights), rows, rp, cp), "attn_fwd2", (ctl, dest),
        [(tokens, None), (segc, None), (segr, None), (ln, None), (ob, None), (q, "far"), (k, "far"), (v, "far"), (o1, None)] + [(w, "hbm") for w in weights],
        [((rp, D), F32, 0), ((rp, D), F32, 0), ((HP, rp, 128), BF, 0), ((HEADS // 2, 1, cp), F32, 0)],
        [
            pltpu.VMEM((2 * D, wcols // 4), BF), pltpu.VMEM((rp, cp), F32), pltpu.VMEM((HP, rp, 128), BF), pltpu.VMEM((HP, cp, 128), BF), pltpu.VMEM((HP, cp, 128), BF),
            pltpu.SemaphoreType.DMA((2 * BLOCKS,)), pltpu.SemaphoreType.DMA((3,)),
        ],
        12,
    )


def gelu_parts(h):
    x = jnp.abs(h) * 0.7071067811865476
    t = 1.0 / (1.0 + 0.3275911 * x)
    e = jnp.exp2(h * h * (-0.5 * LOG2E))
    poly = t * (0.254829592 * 0.5 + t * (-0.284496736 * 0.5 + t * (1.421413741 * 0.5 + t * (-1.453152027 * 0.5 + t * (1.061405429 * 0.5)))))
    tail = poly * e
    phi = jnp.where(h < 0, tail, 1.0 - tail)
    return phi, phi + h * e * 0.3989422804014327


FCH = 768


def ffn_kernel(rows, rp, first, ctl, dest, slots, x1_ref, cot_ref, segc_ref, ln_ref, ub_ref, *rest):
    if first:
        nw = len(rest) - 13
        w = rest[:nw]
        (f_ref, dn_ref, dub_ref, keep, send, w_s, n2_s, n2t_s, dft_s, dy_s, stage, lsem, ssem) = rest[nw:]
    else:
        attn_ref, fin_ref, dnin_ref = rest[:3]
        nw = len(rest) - 3 - 16
        w = rest[3 : 3 + nw]
        (y_ref, dx1_ref, vec_ref, dub_ref, keep, send, w_s, n2_s, n2t_s, dft_s, dy_s, stage, f_ref, dn_ref, lsem, ssem) = rest[3 + nw :]
    copies = load_blocks(dest, w, w_s, lsem)
    core = ctl[1]
    live = (segc_ref[...] != PAD_ID).astype(F32)
    xhat, rstd = row_stats(x1_ref[...])
    n2 = (xhat * ln_ref[0:1] + ln_ref[1:2]).astype(BF)
    n2_s[...] = n2
    n2t_s[...] = n2.T
    dy_s[rows:rp, :] = jnp.zeros((rp - rows, D), F32)
    dy_s[0:rows, :] = cot_ref[...].astype(F32)
    dy = dy_s[...] * live
    dy_s[...] = dy
    df = dy * ln_ref[2:3]
    dfr = df.astype(BF)
    dft_s[...] = dfr.T
    if not first:
        vec_ref[2:3] = col_sum(df)
    for c in copies:
        c.wait()
    pending = []
    for t in range(2):
        wu = w_s[t * D : (t + 1) * D, 0:FCH]
        wd = w_s[t * D : (t + 1) * D, FCH:]
        hid = mm(n2_s[...], wu) + ub_ref[t : t + 1]
        phi, slope = gelu_parts(hid)
        g = (hid * phi).astype(BF)
        dh = (mm(dfr, wd) * slope).astype(BF)
        dub_ref[t : t + 1] = col_sum(dh.astype(F32))
        fp = mm_nt(g, wd)
        dp = mm_nt(dh, wu)
        if t == 0 and first:
            f_ref[...] = fp
            dn_ref[...] = dp
        elif t == 0:
            f_ref[...] = fin_ref[...] + fp
            dn_ref[...] = dnin_ref[...] + dp
        else:
            f_ref[...] += fp
            dn_ref[...] += dp
        stage[t, :, 0:FCH] = mm(n2t_s[...], dh).astype(BF)
        stage[t, :, FCH:] = mm(dft_s[...], g).astype(BF)
        cps = store_copies(core, slots, t, stage.at[t], (keep, send), pl.ds(0, 2 * FCH), ssem.at[t])
        for c in cps:
            c.start()
        pending += cps
    if not first:
        ffo = f_ref[...] + ln_ref[3:4]
        dy = dy_s[...]
        vec_ref[3:4] = col_sum(dy * ffo)
        y_ref[...] = (x1_ref[...] + ln_ref[2:3] * ffo)[0:rows].astype(BF)
        dn2 = dn_ref[...]
        xhat, rstd = row_stats(x1_ref[...])
        vec_ref[0:1] = col_sum(dn2 * xhat)
        vec_ref[1:2] = col_sum(dn2)
        dx1 = dy + norm_back(xhat, rstd, dn2, ln_ref[0:1])
        dx1_ref[...] = dx1
        vec_ref[4:5] = col_sum(dx1 * ln_ref[4:5])
        vec_ref[5:6] = col_sum(dx1 * attn_ref[...])
        vec_ref[6:8] = jnp.zeros((2, D), F32)
    for c in pending:
        c.wait()


def ffn(first, ctl, dest, slots, x1, cotangent, segc, ln, ub, more, weights):
    rows, rp = cotangent.shape[0], x1.shape[0]
    wcols = weights[0].shape[2]
    if first:
        outs = [((rp, D), F32, 0), ((rp, D), F32, 0)]
    else:
        outs = [((rows, D), BF, 0), ((rp, D), F32, 0), ((8, D), F32, 0)]
    outs += [((2, FCH), F32, 0)] + [((BLOCKS, BROWS, wcols), BF, 1)] * 2
    return call(
        functools.partial(ffn_kernel, rows, rp, first), "ffn_first" if first else "ffn_last", (ctl, dest, slots),
        [(x1, None), (cotangent, None), (segc, None), (ln, None), (ub, None)] + [(v, None) for v in more] + [(w, "hbm") for w in weights],
        outs,
        [
            pltpu.VMEM((2 * D, wcols), BF), pltpu.VMEM((rp, D), BF), pltpu.VMEM((D, rp), BF), pltpu.VMEM((D, rp), BF),
            pltpu.VMEM((rp, D), F32), pltpu.VMEM((2, D, 2 * FCH), BF),
        ]
        + ([] if first else [pltpu.VMEM((rp, D), F32)] * 2)
        + [pltpu.SemaphoreType.DMA((2 * BLOCKS,)), pltpu.SemaphoreType.DMA((2, BLOCKS))],
        20, 60,
    )


def attn_bwd_kernel(nw, t, rp, cp, ctl, dest, dx1_ref, qh, kh, vh, lse_ref, segc_ref, segr_ref, ln_ref, *rest):
    w = rest[:nw]
    dq_ref, dk_ref, dv_ref, w_s, do_s, q_s, k_s, v_s, bias_s, sem, isem = rest[nw:]
    heads = half_heads(t, (qh, kh, vh), (q_s, k_s, v_s), isem)
    half = D // 2
    copies = load_blocks(dest, w, w_s, sem, slice(3 * half, 4 * half))
    scale = HEAD ** (-0.5)
    bias_s[...] = jnp.where(segc_ref[...] == segr_ref[...], 0.0, NEG)
    q_s[:, rp:cp, :] = jnp.zeros((HP, cp - rp, 128), BF)
    do_s[:, rp:cp, :] = jnp.zeros((HP, cp - rp, 128), BF)
    dar = (dx1_ref[...] * ln_ref[2:3]).astype(BF)
    for c in copies:
        c.wait()
    z = mm(dar, w_s[t * D : (t + 1) * D, :]).astype(BF)
    for i in range(HP):
        do_s[i, 0:rp, :] = z[:, i * 128 : (i + 1) * 128]
    for c in heads:
        c.wait()

    def pair(p, _):
        q2 = q_s[p]
        do2 = do_s[p]
        k2 = k_s[p]
        v2 = v_s[p]
        dq = dk = dv = None
        for h in range(2):
            m = pair_mask(h)
            km = k2 * m
            st = mm_nt(km, q2) * (scale * LOG2E) + bias_s[...]
            pt = jnp.exp2(st - lse_ref[2 * p + h])
            dpt = mm_nt(v2 * m, do2)
            delta = jnp.sum(pt * dpt, axis=0, keepdims=True)
            dst = (pt * (dpt - delta)).astype(BF)
            a = mm(pt.astype(BF), do2 * m)
            b = mm(dst, q2 * m)
            c = mm_tn(dst, km)
            dv = a if dv is None else dv + a
            dk = b if dk is None else dk + b
            dq = c if dq is None else dq + c
        dq_ref[p] = (dq[0:rp] * scale).astype(BF)
        dk_ref[p] = (dk * scale).astype(BF)
        dv_ref[p] = dv.astype(BF)
        return 0

    lax.fori_loop(0, HP, pair, 0)


def attn_bwd(t, ctl, dest, dx1, q, k, v, lse, segc, segr, ln, weights):
    rp, cp = segc.shape[0], segr.shape[1]
    wcols = weights[0].shape[2]
    return call(
        functools.partial(attn_bwd_kernel, len(weights), t, rp, cp), "attn_bwd", (ctl, dest),
        [(dx1, None), (q, "far"), (k, "far"), (v, "far")] + [(e, None) for e in (lse, segc, segr, ln)] + [(w, "hbm") for w in weights],
        [((HP, rp, 128), BF, 0)] * 3,
        [
            pltpu.VMEM((2 * D, wcols // 4), BF), pltpu.VMEM((HP, cp, 128), BF), pltpu.VMEM((HP, cp, 128), BF), pltpu.VMEM((HP, rp, 128), BF), pltpu.VMEM((HP, rp, 128), BF),
            pltpu.VMEM((rp, cp), F32), pltpu.SemaphoreType.DMA((2 * BLOCKS,)), pltpu.SemaphoreType.DMA((3,)),
        ],
        15,
    )


def attn_grad_kernel(rows, rp, ctl, slots, x_ref, dx1_ref, o1_ref, o2_ref, dq1, dk1, dv1, dq2, dk2, dv2, ln_ref, keep, send, stage, x_s, ssem):
    core = ctl[1]
    half = D // 2
    x_s[0:rows, :] = x_ref[...].astype(F32)
    x_s[rows:rp, :] = jnp.zeros((rp - rows, D), F32)
    dart = (dx1_ref[...] * ln_ref[2:3]).astype(BF).T
    xhat, _ = row_stats(x_s[...])
    n1t = (xhat * ln_ref[0:1] + ln_ref[1:2]).astype(BF).T
    pend = []
    for t, (o, dz) in enumerate(((o1_ref, (dq1, dk1, dv1)), (o2_ref, (dq2, dk2, dv2)))):
        o_t = jnp.concatenate([o[i] for i in range(HP)], axis=1)
        stage[t, :, 3 * half :] = mm(dart, o_t).astype(BF)
        z = jnp.concatenate([e[i] for e in dz for i in range(HP)], axis=1)
        stage[t, :, 0 : 3 * half] = mm(n1t, z).astype(BF)
        cps = store_copies(core, slots, t, stage.at[t], (keep, send), pl.ds(0, 4 * half), ssem.at[t])
        for c in cps:
            c.start()
        pend += cps
    for c in pend:
        c.wait()


def attn_grad(ctl, slots, tokens, dx1, o1, o2, dz1, dz2, ln):
    rows, rp = tokens.shape[0], dx1.shape[0]
    wcols = 2 * D
    return call(
        functools.partial(attn_grad_kernel, rows, rp), "attn_grad", (ctl, slots),
        [(tokens, None)] + [(e, None) for e in (dx1, o1, o2, *dz1, *dz2, ln)],
        [((BLOCKS, BROWS, wcols), BF, 1)] * 2,
        [pltpu.VMEM((2, D, wcols), BF), pltpu.VMEM((rp, D), F32), pltpu.SemaphoreType.DMA((2, BLOCKS))],
        10, 48,
    )


def input_grad_kernel(nw, rows, rp, ctl, dest, x_ref, dx1_ref, dq1, dk1, dv1, dq2, dk2, dv2, ln_ref, *rest):
    w = rest[:nw]
    dx_ref, vec_ref, w_s, x_s, sem = rest[nw:]
    half = D // 2
    copies = load_blocks(dest, w, w_s, sem, slice(0, 3 * half))
    x_s[0:rows, :] = x_ref[...].astype(F32)
    x_s[rows:rp, :] = jnp.zeros((rp - rows, D), F32)
    xhat, rstd = row_stats(x_s[...])
    for c in copies:
        c.wait()
    dn1 = None
    for t, dz in enumerate(((dq1, dk1, dv1), (dq2, dk2, dv2))):
        z = jnp.concatenate([e[i] for e in dz for i in range(HP)], axis=1)
        part = mm_nt(z, w_s[t * D : (t + 1) * D, :])
        dn1 = part if dn1 is None else dn1 + part
        vec_ref[2:3, t * half : (t + 1) * half] = col_sum(z[:, 0:half].astype(F32))
        vec_ref[3:4, t * half : (t + 1) * half] = col_sum(z[:, 2 * half :].astype(F32))
    vec_ref[0:1] = col_sum(dn1 * xhat)
    vec_ref[1:2] = col_sum(dn1)
    vec_ref[4:8] = jnp.zeros((4, D), F32)
    dx = dx1_ref[...] + norm_back(xhat, rstd, dn1, ln_ref[0:1])
    dx_ref[...] = dx[0:rows].astype(BF)


def input_grad(ctl, dest, tokens, dx1, dz1, dz2, ln, weights):
    rows, rp = tokens.shape[0], dx1.shape[0]
    wcols = weights[0].shape[2]
    return call(
        functools.partial(input_grad_kernel, len(weights), rows, rp), "input_grad", (ctl, dest),
        [(tokens, None)] + [(e, None) for e in (dx1, *dz1, *dz2, ln)] + [(w, "hbm") for w in weights],
        [((rows, D), BF, 0), ((8, D), F32, 0)],
        [pltpu.VMEM((2 * D, wcols * 3 // 4), BF), pltpu.VMEM((rp, D), F32), pltpu.SemaphoreType.DMA((2 * BLOCKS,))],
        10,
    )


def prepare(segment, me, ln_gain, ln_shift, qb, out_bias, layer_scale):
    rows = segment.shape[1]
    rp = -(-rows // 16) * 16
    cp = -(-rp // 128) * 128
    seg = lax.dynamic_index_in_dim(segment, me, 0, keepdims=False)
    seg = jnp.concatenate([seg, jnp.full((rp - rows,), -2, jnp.int32), jnp.full((cp - rp,), -1, jnp.int32)])
    segr = seg.reshape(1, cp)
    segc = seg[:rp].reshape(rp, 1)
    half = D // 2
    ln1 = jnp.stack([ln_gain[0], ln_shift[0], layer_scale[0]])
    ln2 = jnp.stack([ln_gain[1], ln_shift[1], layer_scale[1], out_bias[1], layer_scale[0]])
    z = jnp.zeros((2, half), F32)
    qbt = jnp.concatenate([qb[0].reshape(2, half), z, qb[1].reshape(2, half)], axis=1)
    return segc, segr, ln1, ln2, qbt, out_bias[0:1]


def swap(v, n_tensor):
    return lax.ppermute(v, "tensor", [(i, (i + 1) % n_tensor) for i in range(n_tensor)])


def after(v, *done):
    return lax.optimization_barrier((v, done))[0]


class Grid:
    axes = ("dp", "tensor")
    places = [(z, y, c, t) for z in range(4) for y in range(2) for c in range(2) for t in range(2)]

    def number(self, p):
        return ((p[0] * 2 + p[1]) * 2 + p[2]) * 2 + p[3]

    def x(self, p):
        return p[0], p[1], p[2], 1 - p[3]

    def y(self, p):
        return p[0], 1 - p[1], p[2], p[3]

    def core(self, p):
        return p[0], p[1], 1 - p[2], p[3]

    def first(self, p):
        return self.y(p) if p[2] else self.x(p)

    def second(self, p):
        return self.x(p) if p[2] else self.y(p)

    def z1(self, p):
        return p[0] ^ 1, p[1], p[2], p[3]

    def z2(self, p):
        return p[0] ^ 2, p[1], p[2], p[3]

    def z3(self, p):
        return p[0] ^ 3, p[1], p[2], p[3]

    def along(self, v):
        return [self.send(e, to) for e, to in zip(v, (self.z1, self.z2, self.z3))]

    def send(self, v, to):
        return lax.ppermute(v, self.axes, [(self.number(p), self.number(to(p))) for p in self.places])

    def line(self, p):
        return [(p[0] ^ k, p[1], p[2], p[3]) for k in range(4)]

    def held(self, p):
        b = self.second(p)
        return self.line(p) + self.line(self.first(p)) + self.line(b) + self.line(self.first(b))

    def tables(self):
        where = lambda q: q[3] * BLOCKS + (q[0] * 2 + q[1]) * 2 + q[2]
        dest, slots = [], []
        for p in self.places:
            mine, theirs = self.held(p), self.held(self.core(p))
            dest.append([where(q) for q in mine + theirs])
            at = {where(q): i for i, q in enumerate(mine)} | {where(q): i for i, q in enumerate(theirs)}
            half = BLOCKS // 2
            slots.append(
                [at[t * BLOCKS + 2 * m + p[2]] for t in range(2) for m in range(half)]
                + [at[t * BLOCKS + 2 * m + 1 - p[2]] for t in range(2) for m in range(half)]
            )
        return jnp.array(dest, jnp.int32), jnp.array(slots, jnp.int32)


def wide(v):
    return v.astype(F32)


class Reduce:
    def __init__(self, net, keep, sent):
        self.net, self.terms, self.sent = net, [keep], sent
        self.stage = 0
        self.got = net.send(sent, net.core)

    def total(self, at):
        return sum(wide(e[at]) for e in self.terms)

    def start(self, *dep):
        self.stage += 1
        n = self.stage
        self.terms.append(after(self.got, *dep))
        if n < 3:
            self.sent = self.total(slice(BLOCKS >> n, 2 * BLOCKS >> n)).astype(BF)
            self.got = self.net.send(self.sent, self.net.second if n == 1 else self.net.first)
        else:
            self.sent = [self.total(k).astype(BF) for k in (1, 2, 3)]
            self.got = self.net.along(self.sent)

    def result(self, *dep):
        return self.total(0) + sum(wide(e) for e in after(self.got, *dep))


class Plain:
    def __init__(self, n_tensor):
        self.n_tensor = n_tensor

    def gather(self, w):
        me = lax.axis_index("tensor")
        other = swap(w, self.n_tensor)
        both = jnp.where(me == 0, jnp.stack([w, other]), jnp.stack([other, w]))
        full = lax.all_gather(both, "dp", axis=1, tiled=True)
        return [full.reshape(2 * BLOCKS, BROWS, w.shape[1])]

    def settle(self, keep, sent):
        me = lax.axis_index("tensor")
        h = BLOCKS // 2
        g = jnp.stack([keep.reshape(2, h, BROWS, -1), sent.reshape(2, h, BROWS, -1)], axis=2).reshape(2, D, -1)
        part = lax.psum_scatter(g, "dp", scatter_dimension=1, tiled=True).astype(F32)
        return jnp.where(me == 0, part[0], part[1]) + swap(jnp.where(me == 0, part[1], part[0]), self.n_tensor)

    def total(self, v):
        return lax.psum(v, ("dp", "tensor"))


def make_on_device(n_dp, n_tensor):
    def on_device(
        tokens, segment, cotangent, ln_gain, ln_shift, qkv_weight, qv_bias, out_weight,
        out_bias, layer_scale, up_weight, up_bias, down_weight,
    ):
        me = lax.axis_index("tensor")
        own_first = lambda own, other, axis=0: jnp.where(me == 0, jnp.stack([own, other], axis), jnp.stack([other, own], axis))
        both = lambda own, other: own_first(own, other, 1).transpose(1, 0, 2)
        half = D // 2
        hid_half = up_weight.shape[1]
        wa = jnp.concatenate([qkv_weight[0], qkv_weight[1], qkv_weight[2], out_weight.T], axis=1)
        small = jnp.concatenate([qv_bias.reshape(-1), up_bias])

        def pack_ffn(up, down):
            down_t = down.T
            return [jnp.concatenate([up[:, lo : lo + FCH], down_t[:, lo : lo + FCH]], axis=1) for lo in range(0, hid_half, FCH)]

        def consts(small, segment):
            small = own_first(small, swap(small, n_tensor))
            qb = small[:, : 2 * half].reshape(2, 2, half).transpose(1, 0, 2).reshape(2, D)
            ub = small[:, 2 * half :]
            return (ub[:, :FCH], ub[:, FCH:]) + prepare(segment, me, ln_gain, ln_shift, qb, out_bias, layer_scale)

        def results(out, dxs, vec_a, vec_f, dub, ga, gup, gdown):
            g_gain0, g_shift0, g_qb, g_vb = (vec_a[i] for i in range(4))
            g_gain1, g_shift1, g_ob1, g_ls1, g_ob0, g_ls0 = (vec_f[i] for i in range(6))
            qv = lax.dynamic_slice_in_dim(jnp.stack([g_qb, g_vb]), me * half, half, axis=1)
            dubs = lax.dynamic_index_in_dim(dub.reshape(2, hid_half), me, 0, keepdims=False)
            return (
                out, dxs, jnp.stack([g_gain0, g_gain1]), jnp.stack([g_shift0, g_shift1]),
                jnp.stack([ga[:, i * half : (i + 1) * half] for i in range(3)]),
                qv, ga[:, 3 * half :].T, jnp.stack([g_ob0, g_ob1]), jnp.stack([g_ls0, g_ls1]),
                gup, dubs, gdown.T,
            )

        pick = lambda v: lax.dynamic_index_in_dim(v, me, 0, keepdims=False)
        if n_dp != 16 or n_tensor != 2:
            tokens, cotangent = pick(tokens), pick(cotangent)
            net = Plain(n_tensor)
            dest = jnp.arange(2 * BLOCKS, dtype=jnp.int32)
            slots = jnp.concatenate([jnp.arange(BLOCKS, dtype=jnp.int32)] * 2)
            ctl = jnp.stack([me, 0]).astype(jnp.int32)
            wa = net.gather(wa)
            wf = [net.gather(w) for w in pack_ffn(up_weight, down_weight)]
            ub1, ub2, segc, segr, ln1, ln2, qbt, ob0 = consts(small, segment)
            q, k, v, o1, lse1 = attn_fwd1(ctl, dest, tokens, segc, segr, ln1, qbt, wa)
            x1, attn, o2, lse2 = attn_fwd2(ctl, dest, tokens, segc, segr, ln1, ob0, q, k, v, o1, wa)
            f, dn, dub1, k1, s1 = ffn(True, ctl, dest, slots, x1, cotangent, segc, ln2, ub1, (), wf[0])
            y, dx1, vec_f, dub2, k2, s2 = ffn(False, ctl, dest, slots, x1, cotangent, segc, ln2, ub2, (attn, f, dn), wf[1])
            dz1 = attn_bwd(0, ctl, dest, dx1, q, k, v, lse1, segc, segr, ln1, wa)
            dz2 = attn_bwd(1, ctl, dest, dx1, q, k, v, lse2, segc, segr, ln1, wa)
            ka, sa = attn_grad(ctl, slots, tokens, dx1, o1, o2, dz1, dz2, ln1)
            dx, vec_a = input_grad(ctl, dest, tokens, dx1, dz1, dz2, ln1, wa)
            gf1, gf2, ga = net.settle(k1, s1), net.settle(k2, s2), net.settle(ka, sa)
            dub = jnp.concatenate([dub1, dub2], axis=1)
            vec_a, vec_f, dub = (net.total(e) for e in (vec_a, vec_f, dub))
            gup = jnp.concatenate([gf1[:, :FCH], gf2[:, :FCH]], axis=1)
            gdown = jnp.concatenate([gf1[:, FCH:], gf2[:, FCH:]], axis=1)
            return results(both(y, swap(y, n_tensor)), both(dx, swap(dx, n_tensor)), vec_a, vec_f, dub, ga, gup, gdown)

        net = Grid()
        place = lax.axis_index("dp") * 2 + me
        bs = net.along([wa] * 3)
        up_weight, down_weight, segment, small, place = after((up_weight, down_weight, segment, small, place), bs[0])
        fs, es = pack_ffn(up_weight, down_weight)
        fs, bs = after((fs, bs))
        s = after(jnp.stack([wa, *bs]))
        ra = net.send(s, net.first)
        fz = net.along([after(fs, s)] * 3)
        tokens, small, segment, place = after((tokens, small, segment, place), s)
        tokens = pick(tokens)
        ub1, ub2, segc, segr, ln1, ln2, qbt, ob0 = consts(small, segment)
        dest, slots = net.tables()
        dest = lax.dynamic_index_in_dim(dest, place, 0, keepdims=False)
        slots = lax.dynamic_index_in_dim(slots, place, 0, keepdims=False)
        ctl = jnp.stack([me, lax.axis_index("dp") % 2]).astype(jnp.int32)
        ra = after(ra, segc, dest, qbt)
        s = jnp.concatenate([s, ra])
        r = net.send(s, net.second)
        sc = net.send(s, net.core)
        cotangent = pick(after(cotangent, s))
        fz = after(fz, s)
        fs = after(jnp.stack([fs, *fz]))
        ez = net.along([after(es, fs)] * 3)
        r = after(r, sc, fs, cotangent)
        rc = net.send(r, net.core)
        fs = after(fs, r)
        fr = net.send(fs, net.first)
        fr = after(fr, rc)
        fs = jnp.concatenate([fs, fr])
        r1 = net.send(fs, net.second)
        c1 = net.send(fs, net.core)
        wa = after([s, r, sc, rc], fs)
        q, k, v, o1, lse1 = attn_fwd1(ctl, dest, tokens, segc, segr, ln1, qbt, wa)
        r1, c1, ez = after((r1, c1, ez), o1)
        w1 = [fs, r1, c1, net.send(r1, net.core)]
        es = after(jnp.stack([es, *ez]), r1)
        er = net.send(es, net.first)
        q = after(q, es, r1)
        x1, attn, o2, lse2 = attn_fwd2(ctl, dest, tokens, segc, segr, ln1, ob0, q, k, v, o1, wa)
        w1, er = after((w1, er), x1)
        es = jnp.concatenate([es, er])
        r2 = net.send(es, net.second)
        c2 = net.send(es, net.core)
        w1 = after(w1, es)
        f, dn, dub1, k1, s1 = ffn(True, ctl, dest, slots, x1, cotangent, segc, ln2, ub1, (), w1)
        r2, c2 = after((r2, c2), f)
        w2 = [es, r2, c2, net.send(r2, net.core)]
        g1 = Reduce(net, k1, s1)
        y, dx1, vec_f, dub2, k2, s2 = ffn(False, ctl, dest, slots, x1, cotangent, segc, ln2, ub2, (attn, f, dn), w2)
        g2 = Reduce(net, k2, s2)
        g1.start(dx1)
        y_other = swap(after(y, g1.sent), n_tensor)
        dx1 = after(dx1, g1.sent)
        dz1 = attn_bwd(0, ctl, dest, dx1, q, k, v, lse1, segc, segr, ln1, wa)
        g2.start(dz1[0], g1.got)
        g1.start(dz1[0], g2.sent)
        dx1 = after(dx1, dz1[0], g1.sent, g2.sent, y_other)
        dz2 = attn_bwd(1, ctl, dest, dx1, q, k, v, lse2, segc, segr, ln1, wa)
        g1.start(dz2[0])
        g2.start(dz2[0], g1.sent)
        dx1 = after(dx1, g1.sent, g2.sent, dz2[0])
        ka, sa = attn_grad(ctl, slots, tokens, dx1, o1, o2, dz1, dz2, ln1)
        g = Reduce(net, ka, sa)
        dx1 = after(dx1, ka)
        dx, vec_a = input_grad(ctl, dest, tokens, dx1, dz1, dz2, ln1, wa)
        vec = jnp.concatenate([vec_a[:4], vec_f[:6], jnp.concatenate([dub1, dub2], axis=1).reshape(-1, D)])

        def add(v, to, *dep):
            v = after(v, *dep)
            return v + net.send(v, to)

        g.start(dx)
        g2.start(g.sent, g1.got)
        vec = add(add(add(vec, net.core, g.sent), net.x), net.y)
        out = both(*after((y, y_other), g.sent))
        gf1 = g1.result(g.sent)
        g.start(vec, gf1, out)
        dx_other = swap(after(dx, g.sent), n_tensor)
        vec = add(vec, net.z1, g.sent)
        gf2 = g2.result(g.sent)
        g.start(vec, gf2)
        vec = add(vec, net.z2, g.sent)
        gup = jnp.concatenate([gf1[:, :FCH], gf2[:, :FCH]], axis=1)
        gdown = jnp.concatenate([gf1[:, FCH:], gf2[:, FCH:]], axis=1)
        dxs = both(dx, dx_other)
        return results(out, dxs, vec[:4], vec[4:10], vec[10:], g.result(), gup, gdown)

    return on_device


def solution(mesh):
    rows = P(None, "dp", None)
    wt = P("tensor", "dp")
    return jax.shard_map(
        make_on_device(mesh.shape["dp"], mesh.shape["tensor"]),
        mesh=mesh,
        in_specs=(
            rows, P(None, "dp"), rows, P(), P(), P(None, "dp", "tensor"), P(None, "tensor"), wt,
            P(), P(), P("dp", "tensor"), P("tensor"), wt,
        ),
        out_specs=(
            rows, rows, P(), P(), P(None, "dp", "tensor"), P(None, "tensor"), wt,
            P(), P(), P("dp", "tensor"), P("tensor"), wt,
        ),
        check_vma=False,
    )
```

```python
import functools

import jax
import jax.numpy as jnp
from jax import lax
from jax.experimental import pallas as pl
from jax.experimental.pallas import tpu as pltpu
from jax.sharding import PartitionSpec as P

D = 768
HEADS = 12
HEAD = D // HEADS
EPS = 1e-06
PAD_ID = 3
NEG = -1e30
BF = jnp.bfloat16
F32 = jnp.float32
LOG2E = 1.4426950408889634

BLOCKS = 16
BROWS = D // BLOCKS


def mm(a, b):
    return jnp.dot(a, b, preferred_element_type=F32)


def mm_nt(a, b):
    return lax.dot_general(a, b, (((1,), (1,)), ((), ())), preferred_element_type=F32)


def mm_tn(a, b):
    return lax.dot_general(a, b, (((0,), (0,)), ((), ())), preferred_element_type=F32)


def row_stats(v):
    mean = jnp.mean(v, axis=-1, keepdims=True)
    c = v - mean
    rstd = lax.rsqrt(jnp.mean(c * c, axis=-1, keepdims=True) + EPS)
    return c * rstd, rstd


def norm_back(xhat, rstd, dn, gain):
    dxh = dn * gain
    m1 = jnp.mean(dxh, axis=-1, keepdims=True)
    m2 = jnp.mean(dxh * xhat, axis=-1, keepdims=True)
    return rstd * (dxh - m1 - xhat * m2)


def col_sum(v):
    return jnp.sum(v, axis=0, keepdims=True)


def load_blocks(dest, parts, dst, sem, cols=slice(None)):
    copies = []
    n = 0
    for part in parts:
        for j in range(part.shape[0]):
            row = pl.multiple_of(dest[n] * BROWS, BROWS)
            copies.append(pltpu.make_async_copy(part.at[j, :, cols], dst.at[pl.ds(row, BROWS)], sem.at[n]))
            n += 1
    for c in copies:
        c.start()
    return copies


def store_copies(core, slots, t, stage, outs, cols, sem):
    keep, send = outs
    copies = []
    half = BLOCKS // 2
    for m in range(half):
        a = pl.multiple_of((2 * m + core) * BROWS, BROWS)
        b = pl.multiple_of((2 * m + 1 - core) * BROWS, BROWS)
        copies.append(pltpu.make_async_copy(stage.at[pl.ds(a, BROWS)], keep.at[slots[t * half + m], :, cols], sem.at[2 * m]))
        copies.append(pltpu.make_async_copy(stage.at[pl.ds(b, BROWS)], send.at[slots[BLOCKS + t * half + m], :, cols], sem.at[2 * m + 1]))
    return copies


def pair_mask(h, dtype=BF):
    lane = lax.broadcasted_iota(jnp.int32, (1, 2 * HEAD), 1)
    return (lane // HEAD == h).astype(dtype)


def call(kernel, name, scalars, ins, outs, scratch, us, vmem=32):
    spaces = {None: pltpu.VMEM, 0: pltpu.VMEM, 1: pl.ANY, "hbm": pl.ANY, "far": pltpu.HBM}
    at = lambda how: pl.BlockSpec(memory_space=spaces[how])
    return pl.pallas_call(
        kernel,
        in_specs=[pl.BlockSpec(memory_space=pltpu.SMEM)] * len(scalars) + [at(how) for _, how in ins],
        out_specs=[at(how) for _, _, how in outs],
        out_shape=[jax.ShapeDtypeStruct(shape, dtype) for shape, dtype, _ in outs],
        scratch_shapes=scratch,
        compiler_params=pltpu.CompilerParams(vmem_limit_bytes=vmem * 1024 * 1024),
        cost_estimate=pl.CostEstimate(flops=us * 5_000_000_000, bytes_accessed=us * 1_000_000, transcendentals=0),
        name=name,
    )(*scalars, *[v for v, _ in ins])


PAIRS = HEADS // 2
HP = PAIRS // 2


def fwd_pairs(q_ref, k_ref, v_ref, bias_s, o_ref, lse_ref):
    scale = (HEAD ** (-0.5)) * LOG2E

    def pair(p, _):
        q2 = q_ref[p]
        k2 = k_ref[p]
        v2 = v_ref[p]
        acc = None
        for h in range(2):
            m = pair_mask(h)
            s = mm_nt(q2, k2 * m) * scale + bias_s[...]
            top = jnp.max(s, axis=-1, keepdims=True)
            e = jnp.exp2(s - top)
            tot = jnp.sum(e, axis=-1, keepdims=True)
            oh = mm(e.astype(BF), v2 * m) * (1.0 / tot)
            acc = oh if acc is None else acc + oh
            lse_ref[2 * p + h, :, 0 : top.shape[0]] = (top + jnp.log2(tot)).reshape(1, -1)
        o_ref[p] = acc.astype(BF)
        return 0

    lse_ref[...] = jnp.zeros_like(lse_ref)
    lax.fori_loop(0, HP, pair, 0)


def half_heads(t, src, dst, sem):
    copies = []
    for i, (a, b) in enumerate(zip(src, dst)):
        n = min(a.shape[1], b.shape[1])
        copies.append(pltpu.make_async_copy(a.at[pl.ds(HP * t, HP), 0:n], b.at[:, 0:n], sem.at[i]))
    for c in copies:
        c.start()
    return copies


def attn_fwd1_kernel(nw, rows, rp, cp, ctl, dest, x_ref, segc_ref, segr_ref, ln_ref, qb_ref, *rest):
    w = rest[:nw]
    qh, kh, vh, o_ref, lse_ref, w_s, x_s, bias_s, q_ref, k_ref, v_ref, sem, osem = rest[nw:]
    copies = load_blocks(dest, w, w_s, sem)
    x_s[0:rows, :] = x_ref[...].astype(F32)
    x_s[rows:rp, :] = jnp.zeros((rp - rows, D), F32)
    bias_s[...] = jnp.where(segc_ref[...] == segr_ref[...], 0.0, NEG)
    xhat, _ = row_stats(x_s[...])
    n1 = (xhat * ln_ref[0:1] + ln_ref[1:2]).astype(BF)
    for c in copies:
        c.wait()
    half = D // 2
    k_ref[:, rp:cp, :] = jnp.zeros((PAIRS, cp - rp, 128), BF)
    v_ref[:, rp:cp, :] = jnp.zeros((PAIRS, cp - rp, 128), BF)
    x_s[...] = n1.astype(F32)

    def project(t, _):
        z = mm(x_s[...].astype(BF), w_s[pl.ds(pl.multiple_of(t * D, D), D), 0 : 3 * half]) + qb_ref[pl.ds(t, 1)]
        z = z.astype(BF)
        for i in range(HP):
            q_ref[HP * t + i] = z[:, i * 128 : (i + 1) * 128]
            k_ref[HP * t + i, 0:rp, :] = z[:, half + i * 128 : half + (i + 1) * 128]
            v_ref[HP * t + i, 0:rp, :] = z[:, 2 * half + i * 128 : 2 * half + (i + 1) * 128]
        return 0

    lax.fori_loop(0, 2, project, 0)
    out = [pltpu.make_async_copy(a, b, osem.at[i]) for i, (a, b) in enumerate(((q_ref, qh), (k_ref, kh), (v_ref, vh)))]
    for c in out:
        c.start()
    fwd_pairs(q_ref, k_ref, v_ref, bias_s, o_ref, lse_ref)
    for c in out:
        c.wait()


def attn_fwd2_kernel(nw, rows, rp, cp, ctl, dest, x_ref, segc_ref, segr_ref, ln_ref, ob_ref, qh, kh, vh, o1_ref, *rest):
    w = rest[:nw]
    x1_ref, attn_ref, o_ref, lse_ref, w_s, bias_s, q_s, k_s, v_s, sem, isem = rest[nw:]
    heads = half_heads(1, (qh, kh, vh), (q_s, k_s, v_s), isem)
    half = D // 2
    copies = load_blocks(dest, w, w_s, sem, slice(3 * half, 4 * half))
    bias_s[...] = jnp.where(segc_ref[...] == segr_ref[...], 0.0, NEG)
    for c in heads:
        c.wait()
    fwd_pairs(q_s, k_s, v_s, bias_s, o_ref, lse_ref)
    for c in copies:
        c.wait()
    a = ob_ref[0:1]
    for t, src in enumerate((o1_ref, o_ref)):
        o_t = jnp.concatenate([src[i] for i in range(HP)], axis=1)
        a = a + mm_nt(o_t, w_s[t * D : (t + 1) * D, :]).astype(BF).astype(F32)
    attn_ref[...] = a
    x1_ref[...] = ln_ref[2:3] * a
    x1_ref[0:rows, :] += x_ref[...].astype(F32)


def attn_fwd1(ctl, dest, tokens, segc, segr, ln, qb, weights):
    rows, rp, cp = tokens.shape[0], segc.shape[0], segr.shape[1]
    wcols = weights[0].shape[2]
    return call(
        functools.partial(attn_fwd1_kernel, len(weights), rows, rp, cp), "attn_fwd1", (ctl, dest),
        [(tokens, None), (segc, None), (segr, None), (ln, None), (qb, None)] + [(w, "hbm") for w in weights],
        [((PAIRS, rp, 128), BF, "far"), ((PAIRS, cp, 128), BF, "far"), ((PAIRS, cp, 128), BF, "far"), ((HP, rp, 128), BF, 0), ((HEADS // 2, 1, cp), F32, 0)],
        [
            pltpu.VMEM((2 * D, wcols), BF), pltpu.VMEM((rp, D), F32), pltpu.VMEM((rp, cp), F32), pltpu.VMEM((PAIRS, rp, 128), BF), pltpu.VMEM((PAIRS, cp, 128), BF), pltpu.VMEM((PAIRS, cp, 128), BF),
            pltpu.SemaphoreType.DMA((2 * BLOCKS,)), pltpu.SemaphoreType.DMA((3,)),
        ],
        14,
    )


def attn_fwd2(ctl, dest, tokens, segc, segr, ln, ob, q, k, v, o1, weights):
    rows, rp, cp = tokens.shape[0], segc.shape[0], segr.shape[1]
    wcols = weights[0].shape[2]
    return call(
        functools.partial(attn_fwd2_kernel, len(weights), rows, rp, cp), "attn_fwd2", (ctl, dest),
        [(tokens, None), (segc, None), (segr, None), (ln, None), (ob, None), (q, "far"), (k, "far"), (v, "far"), (o1, None)] + [(w, "hbm") for w in weights],
        [((rp, D), F32, 0), ((rp, D), F32, 0), ((HP, rp, 128), BF, 0), ((HEADS // 2, 1, cp), F32, 0)],
        [
            pltpu.VMEM((2 * D, wcols // 4), BF), pltpu.VMEM((rp, cp), F32), pltpu.VMEM((HP, rp, 128), BF), pltpu.VMEM((HP, cp, 128), BF), pltpu.VMEM((HP, cp, 128), BF),
            pltpu.SemaphoreType.DMA((2 * BLOCKS,)), pltpu.SemaphoreType.DMA((3,)),
        ],
        12,
    )


def gelu_parts(h):
    x = jnp.abs(h) * 0.7071067811865476
    t = 1.0 / (1.0 + 0.3275911 * x)
    e = jnp.exp2(h * h * (-0.5 * LOG2E))
    poly = t * (0.254829592 * 0.5 + t * (-0.284496736 * 0.5 + t * (1.421413741 * 0.5 + t * (-1.453152027 * 0.5 + t * (1.061405429 * 0.5)))))
    tail = poly * e
    phi = jnp.where(h < 0, tail, 1.0 - tail)
    return phi, phi + h * e * 0.3989422804014327


FCH = 768


def ffn_kernel(rows, rp, first, ctl, dest, slots, x1_ref, cot_ref, segc_ref, ln_ref, ub_ref, *rest):
    if first:
        nw = len(rest) - 14
        w = rest[:nw]
        (f_ref, dn_ref, dub_ref, keep, send, w_s, n2_s, n2t_s, dfr_s, dft_s, dy_s, stage, lsem, ssem) = rest[nw:]
    else:
        attn_ref, fin_ref, dnin_ref = rest[:3]
        nw = len(rest) - 3 - 18
        w = rest[3 : 3 + nw]
        (y0_ref, y1_ref, dx1_ref, vec_ref, dub_ref, keep, send, w_s, n2_s, n2t_s, dfr_s, dft_s, dy_s, stage, f_ref, dn_ref, lsem, ssem) = rest[3 + nw :]
    copies = load_blocks(dest, w, w_s, lsem)
    core = ctl[1]
    live = (segc_ref[...] != PAD_ID).astype(F32)
    xhat, rstd = row_stats(x1_ref[...])
    n2 = (xhat * ln_ref[0:1] + ln_ref[1:2]).astype(BF)
    n2_s[...] = n2
    n2t_s[...] = n2.T
    dy_s[rows:rp, :] = jnp.zeros((rp - rows, D), F32)
    dy_s[0:rows, :] = cot_ref[...].astype(F32)
    dy = dy_s[...] * live
    dy_s[...] = dy
    df = dy * ln_ref[2:3]
    dfr = df.astype(BF)
    dfr_s[...] = dfr
    dft_s[...] = dfr.T
    if not first:
        vec_ref[2:3] = col_sum(df)
    for c in copies:
        c.wait()
    if first:
        f_ref[...] = jnp.zeros((rp, D), F32)
        dn_ref[...] = jnp.zeros((rp, D), F32)
    else:
        f_ref[...] = fin_ref[...]
        dn_ref[...] = dnin_ref[...]
    copies_of = lambda t: store_copies(core, slots, t, stage.at[t], (keep, send), pl.ds(0, 2 * FCH), ssem.at[t])

    def half_units(t, _):
        rows_t = pl.ds(pl.multiple_of(t * D, D), D)
        wu = w_s[rows_t, 0:FCH]
        wd = w_s[rows_t, FCH:]
        hid = mm(n2_s[...], wu) + ub_ref[pl.ds(t, 1)]
        phi, slope = gelu_parts(hid)
        g = (hid * phi).astype(BF)
        dh = (mm(dfr_s[...], wd) * slope).astype(BF)
        dub_ref[pl.ds(t, 1)] = col_sum(dh.astype(F32))
        stage[t, :, 0:FCH] = mm(n2t_s[...], dh).astype(BF)
        stage[t, :, FCH:] = mm(dft_s[...], g).astype(BF)
        for c in copies_of(t):
            c.start()
        f_ref[...] += mm_nt(g, wd)
        dn_ref[...] += mm_nt(dh, wu)
        return 0

    lax.fori_loop(0, 2, half_units, 0)
    pending = copies_of(0) + copies_of(1)
    if not first:
        ffo = f_ref[...] + ln_ref[3:4]
        dy = dy_s[...]
        vec_ref[3:4] = col_sum(dy * ffo)
        y = (x1_ref[...] + ln_ref[2:3] * ffo).astype(BF)
        cut = y0_ref.shape[0]
        y0_ref[...] = y[0:cut]
        y1_ref[...] = y[cut:rows]
        dn2 = dn_ref[...]
        xhat, rstd = row_stats(x1_ref[...])
        vec_ref[0:1] = col_sum(dn2 * xhat)
        vec_ref[1:2] = col_sum(dn2)
        dx1 = dy + norm_back(xhat, rstd, dn2, ln_ref[0:1])
        dx1_ref[...] = dx1
        vec_ref[4:5] = col_sum(dx1 * ln_ref[4:5])
        vec_ref[5:6] = col_sum(dx1 * attn_ref[...])
        vec_ref[6:8] = jnp.zeros((2, D), F32)
    for c in pending:
        c.wait()


def ffn(first, ctl, dest, slots, x1, cotangent, segc, ln, ub, more, weights):
    rows, rp = cotangent.shape[0], x1.shape[0]
    wcols = weights[0].shape[2]
    if first:
        outs = [((rp, D), F32, 0), ((rp, D), F32, 0)]
    else:
        cut = -(-rows // 32) * 16
        outs = [((cut, D), BF, 0), ((rows - cut, D), BF, 0), ((rp, D), F32, 0), ((8, D), F32, 0)]
    outs += [((2, FCH), F32, 0)] + [((BLOCKS, BROWS, wcols), BF, 1)] * 2
    return call(
        functools.partial(ffn_kernel, rows, rp, first), "ffn_first" if first else "ffn_last", (ctl, dest, slots),
        [(x1, None), (cotangent, None), (segc, None), (ln, None), (ub, None)] + [(v, None) for v in more] + [(w, "hbm") for w in weights],
        outs,
        [
            pltpu.VMEM((2 * D, wcols), BF), pltpu.VMEM((rp, D), BF), pltpu.VMEM((D, rp), BF), pltpu.VMEM((rp, D), BF), pltpu.VMEM((D, rp), BF),
            pltpu.VMEM((rp, D), F32), pltpu.VMEM((2, D, 2 * FCH), BF),
        ]
        + ([] if first else [pltpu.VMEM((rp, D), F32)] * 2)
        + [pltpu.SemaphoreType.DMA((2 * BLOCKS,)), pltpu.SemaphoreType.DMA((2, BLOCKS))],
        20, 60,
    )


def attn_bwd_kernel(nw, rp, cp, which, ctl, dest, dx1_ref, qh, kh, vh, lse_ref, segc_ref, segr_ref, ln_ref, *rest):
    w = rest[:nw]
    dq_ref, dk_ref, dv_ref, w_s, do_s, q_s, k_s, v_s, bias_s, sem, isem = rest[nw:]
    t = which[0]
    heads = half_heads(t, (qh, kh, vh), (q_s, k_s, v_s), isem)
    half = D // 2
    copies = load_blocks(dest, w, w_s, sem, slice(3 * half, 4 * half))
    scale = HEAD ** (-0.5)
    bias_s[...] = jnp.where(segc_ref[...] == segr_ref[...], 0.0, NEG)
    q_s[:, rp:cp, :] = jnp.zeros((HP, cp - rp, 128), BF)
    do_s[:, rp:cp, :] = jnp.zeros((HP, cp - rp, 128), BF)
    dar = (dx1_ref[...] * ln_ref[2:3]).astype(BF)
    for c in copies:
        c.wait()
    z = mm(dar, w_s[pl.ds(pl.multiple_of(t * D, D), D), :]).astype(BF)
    for i in range(HP):
        do_s[i, 0:rp, :] = z[:, i * 128 : (i + 1) * 128]
    for c in heads:
        c.wait()

    def pair(p, _):
        q2 = q_s[p]
        do2 = do_s[p]
        k2 = k_s[p]
        v2 = v_s[p]
        dq = dk = dv = None
        for h in range(2):
            m = pair_mask(h)
            km = k2 * m
            st = mm_nt(km, q2) * (scale * LOG2E) + bias_s[...]
            pt = jnp.exp2(st - lse_ref[2 * p + h])
            dpt = mm_nt(v2 * m, do2)
            delta = jnp.sum(pt * dpt, axis=0, keepdims=True)
            dst = (pt * (dpt - delta)).astype(BF)
            a = mm(pt.astype(BF), do2 * m)
            b = mm(dst, q2 * m)
            c = mm_tn(dst, km)
            dv = a if dv is None else dv + a
            dk = b if dk is None else dk + b
            dq = c if dq is None else dq + c
        dq_ref[p] = (dq[0:rp] * scale).astype(BF)
        dk_ref[p] = (dk * scale).astype(BF)
        dv_ref[p] = dv.astype(BF)
        return 0

    lax.fori_loop(0, HP, pair, 0)


def attn_bwd(t, ctl, dest, dx1, q, k, v, lse, segc, segr, ln, weights):
    rp, cp = segc.shape[0], segr.shape[1]
    wcols = weights[0].shape[2]
    return call(
        functools.partial(attn_bwd_kernel, len(weights), rp, cp), "attn_bwd", (jnp.full((1,), t, jnp.int32), ctl, dest),
        [(dx1, None), (q, "far"), (k, "far"), (v, "far")] + [(e, None) for e in (lse, segc, segr, ln)] + [(w, "hbm") for w in weights],
        [((HP, rp, 128), BF, 0)] * 3,
        [
            pltpu.VMEM((2 * D, wcols // 4), BF), pltpu.VMEM((HP, cp, 128), BF), pltpu.VMEM((HP, cp, 128), BF), pltpu.VMEM((HP, rp, 128), BF), pltpu.VMEM((HP, rp, 128), BF),
            pltpu.VMEM((rp, cp), F32), pltpu.SemaphoreType.DMA((2 * BLOCKS,)), pltpu.SemaphoreType.DMA((3,)),
        ],
        15, 60,
    )


def attn_grad_kernel(rows, rp, ctl, slots, x_ref, dx1_ref, o1_ref, o2_ref, dq1, dk1, dv1, dq2, dk2, dv2, ln_ref, keep, send, stage, x_s, ssem):
    core = ctl[1]
    half = D // 2
    x_s[0:rows, :] = x_ref[...].astype(F32)
    x_s[rows:rp, :] = jnp.zeros((rp - rows, D), F32)
    dart = (dx1_ref[...] * ln_ref[2:3]).astype(BF).T
    xhat, _ = row_stats(x_s[...])
    n1t = (xhat * ln_ref[0:1] + ln_ref[1:2]).astype(BF).T
    pend = []
    for t, (o, dz) in enumerate(((o1_ref, (dq1, dk1, dv1)), (o2_ref, (dq2, dk2, dv2)))):
        o_t = jnp.concatenate([o[i] for i in range(HP)], axis=1)
        stage[t, :, 3 * half :] = mm(dart, o_t).astype(BF)
        z = jnp.concatenate([e[i] for e in dz for i in range(HP)], axis=1)
        stage[t, :, 0 : 3 * half] = mm(n1t, z).astype(BF)
        cps = store_copies(core, slots, t, stage.at[t], (keep, send), pl.ds(0, 4 * half), ssem.at[t])
        for c in cps:
            c.start()
        pend += cps
    for c in pend:
        c.wait()


def attn_grad(ctl, slots, tokens, dx1, o1, o2, dz1, dz2, ln):
    rows, rp = tokens.shape[0], dx1.shape[0]
    wcols = 2 * D
    return call(
        functools.partial(attn_grad_kernel, rows, rp), "attn_grad", (ctl, slots),
        [(tokens, None)] + [(e, None) for e in (dx1, o1, o2, *dz1, *dz2, ln)],
        [((BLOCKS, BROWS, wcols), BF, 1)] * 2,
        [pltpu.VMEM((2, D, wcols), BF), pltpu.VMEM((rp, D), F32), pltpu.SemaphoreType.DMA((2, BLOCKS))],
        10, 48,
    )


def input_grad_kernel(nw, rows, rp, ctl, dest, x_ref, dx1_ref, dq1, dk1, dv1, dq2, dk2, dv2, ln_ref, vecf_ref, dub1_ref, dub2_ref, *rest):
    w = rest[:nw]
    dx_ref, vec_ref, w_s, x_s, sem = rest[nw:]
    half = D // 2
    copies = load_blocks(dest, w, w_s, sem, slice(0, 3 * half))
    x_s[0:rows, :] = x_ref[...].astype(F32)
    x_s[rows:rp, :] = jnp.zeros((rp - rows, D), F32)
    xhat, rstd = row_stats(x_s[...])
    for c in copies:
        c.wait()
    dn1 = None
    for t, dz in enumerate(((dq1, dk1, dv1), (dq2, dk2, dv2))):
        z = jnp.concatenate([e[i] for e in dz for i in range(HP)], axis=1)
        part = mm_nt(z, w_s[t * D : (t + 1) * D, :])
        dn1 = part if dn1 is None else dn1 + part
        vec_ref[8:9, t * half : (t + 1) * half] = col_sum(z[:, 0:half].astype(F32))
        vec_ref[9:10, t * half : (t + 1) * half] = col_sum(z[:, 2 * half :].astype(F32))
        vec_ref[10 + 2 * t : 11 + 2 * t] = dub1_ref[t : t + 1]
        vec_ref[11 + 2 * t : 12 + 2 * t] = dub2_ref[t : t + 1]
    vec_ref[0:1] = col_sum(dn1 * xhat)
    vec_ref[2:3] = col_sum(dn1)
    for i, row in enumerate((1, 3, 5, 7, 4, 6)):
        vec_ref[row : row + 1] = vecf_ref[i : i + 1]
    vec_ref[14:16] = jnp.zeros((2, D), F32)
    dx = dx1_ref[...] + norm_back(xhat, rstd, dn1, ln_ref[0:1])
    dx_ref[...] = dx[0:rows].astype(BF)


def input_grad(ctl, dest, tokens, dx1, dz1, dz2, ln, vec_f, dub1, dub2, weights):
    rows, rp = tokens.shape[0], dx1.shape[0]
    wcols = weights[0].shape[2]
    return call(
        functools.partial(input_grad_kernel, len(weights), rows, rp), "input_grad", (ctl, dest),
        [(tokens, None)] + [(e, None) for e in (dx1, *dz1, *dz2, ln, vec_f, dub1, dub2)] + [(w, "hbm") for w in weights],
        [((rows, D), BF, 0), ((16, D), F32, 0)],
        [pltpu.VMEM((2 * D, wcols * 3 // 4), BF), pltpu.VMEM((rp, D), F32), pltpu.SemaphoreType.DMA((2 * BLOCKS,))],
        10,
    )


def prepare(segment, me, ln_gain, ln_shift, qb, out_bias, layer_scale):
    rows = segment.shape[1]
    rp = -(-rows // 16) * 16
    cp = -(-rp // 128) * 128
    seg = lax.dynamic_index_in_dim(segment, me, 0, keepdims=False)
    seg = jnp.concatenate([seg, jnp.full((rp - rows,), -2, jnp.int32), jnp.full((cp - rp,), -1, jnp.int32)])
    segr = seg.reshape(1, cp)
    segc = seg[:rp].reshape(rp, 1)
    half = D // 2
    ln1 = jnp.stack([ln_gain[0], ln_shift[0], layer_scale[0]])
    ln2 = jnp.stack([ln_gain[1], ln_shift[1], layer_scale[1], out_bias[1], layer_scale[0]])
    z = jnp.zeros((2, half), F32)
    qbt = jnp.concatenate([qb[0].reshape(2, half), z, qb[1].reshape(2, half)], axis=1)
    return segc, segr, ln1, ln2, qbt, out_bias[0:1]


def swap(v, n_tensor):
    return lax.ppermute(v, "tensor", [(i, (i + 1) % n_tensor) for i in range(n_tensor)])


def after(v, *done):
    return lax.optimization_barrier((v, done))[0]


class Grid:
    axes = ("dp", "tensor")
    places = [(z, y, c, t) for z in range(4) for y in range(2) for c in range(2) for t in range(2)]

    def number(self, p):
        return ((p[0] * 2 + p[1]) * 2 + p[2]) * 2 + p[3]

    def x(self, p):
        return p[0], p[1], p[2], 1 - p[3]

    def y(self, p):
        return p[0], 1 - p[1], p[2], p[3]

    def core(self, p):
        return p[0], p[1], 1 - p[2], p[3]

    def first(self, p):
        return self.y(p) if p[2] else self.x(p)

    def second(self, p):
        return self.x(p) if p[2] else self.y(p)

    def z1(self, p):
        return p[0] ^ 1, p[1], p[2], p[3]

    def z2(self, p):
        return p[0] ^ 2, p[1], p[2], p[3]

    def z3(self, p):
        return p[0] ^ 3, p[1], p[2], p[3]

    def along(self, v):
        return [self.send(e, to) for e, to in zip(v, (self.z1, self.z2, self.z3))]

    def send(self, v, to):
        return lax.ppermute(v, self.axes, [(self.number(p), self.number(to(p))) for p in self.places])

    def line(self, p):
        return [(p[0] ^ k, p[1], p[2], p[3]) for k in range(4)]

    def held(self, p, first, second):
        b = second(p)
        return self.line(p) + self.line(first(p)) + self.line(b) + self.line(first(b))

    def tables(self):
        where = lambda q: q[3] * BLOCKS + (q[0] * 2 + q[1]) * 2 + q[2]
        half = BLOCKS // 2
        rows = []
        for p in self.places:
            row = [where(q) for e in (p, self.core(p)) for q in self.held(e, self.first, self.second)]
            for route in ((self.first, self.second), (self.x, self.y)):
                at = {where(q): i for e in (p, self.core(p)) for i, q in enumerate(self.held(e, *route))}
                row += [at[t * BLOCKS + 2 * m + p[2]] for t in range(2) for m in range(half)]
                row += [at[t * BLOCKS + 2 * m + 1 - p[2]] for t in range(2) for m in range(half)]
            rows.append(row)
        return jnp.array(rows, jnp.int32)


def wide(v):
    return v.astype(F32)


class Reduce:
    def __init__(self, net, keep, sent, first, second):
        self.net, self.terms, self.sent, self.first, self.second = net, [keep], sent, first, second
        self.stage = 0
        self.got = net.send(sent, net.core)

    def total(self, at):
        return sum(wide(e[at]) for e in self.terms)

    def start(self, *dep):
        self.stage += 1
        n = self.stage
        self.terms.append(after(self.got, *dep))
        if n < 3:
            self.sent = self.total(slice(BLOCKS >> n, 2 * BLOCKS >> n)).astype(BF)
            self.got = self.net.send(self.sent, self.second if n == 1 else self.first)
        else:
            self.sent = [self.total(k).astype(BF) for k in (1, 2, 3)]
            self.got = self.net.along(self.sent)

    def result(self, *dep):
        return self.total(0) + sum(wide(e) for e in after(self.got, *dep))


class Plain:
    def __init__(self, n_tensor):
        self.n_tensor = n_tensor

    def gather(self, w):
        me = lax.axis_index("tensor")
        other = swap(w, self.n_tensor)
        both = jnp.where(me == 0, jnp.stack([w, other]), jnp.stack([other, w]))
        full = lax.all_gather(both, "dp", axis=1, tiled=True)
        return [full.reshape(2 * BLOCKS, BROWS, w.shape[1])]

    def settle(self, keep, sent):
        me = lax.axis_index("tensor")
        h = BLOCKS // 2
        g = jnp.stack([keep.reshape(2, h, BROWS, -1), sent.reshape(2, h, BROWS, -1)], axis=2).reshape(2, D, -1)
        part = lax.psum_scatter(g, "dp", scatter_dimension=1, tiled=True).astype(F32)
        return jnp.where(me == 0, part[0], part[1]) + swap(jnp.where(me == 0, part[1], part[0]), self.n_tensor)

    def total(self, v):
        return lax.psum(v, ("dp", "tensor"))


def make_on_device(n_dp, n_tensor):
    def on_device(
        tokens, segment, cotangent, ln_gain, ln_shift, qkv_weight, qv_bias, out_weight,
        out_bias, layer_scale, up_weight, up_bias, down_weight,
    ):
        me = lax.axis_index("tensor")
        own_first = lambda own, other, axis=0: jnp.where(me == 0, jnp.stack([own, other], axis), jnp.stack([other, own], axis))
        both = lambda own, other: own_first(own, other, 1).transpose(1, 0, 2)
        half = D // 2
        hid_half = up_weight.shape[1]
        wa = jnp.concatenate([qkv_weight[0], qkv_weight[1], qkv_weight[2], out_weight.T], axis=1)
        small = jnp.concatenate([qv_bias.reshape(-1), up_bias])

        def pack_ffn(up, down):
            down_t = down.T
            return [jnp.concatenate([up[:, lo : lo + FCH], down_t[:, lo : lo + FCH]], axis=1) for lo in range(0, hid_half, FCH)]

        def consts(small, segment):
            small = own_first(small, swap(small, n_tensor))
            qb = small[:, : 2 * half].reshape(2, 2, half).transpose(1, 0, 2).reshape(2, D)
            ub = small[:, 2 * half :]
            return (ub[:, :FCH], ub[:, FCH:]) + prepare(segment, me, ln_gain, ln_shift, qb, out_bias, layer_scale)

        def results(out, dxs, vec, ga, gup, gdown):
            qv = lax.dynamic_slice(vec, (8, me * half), (2, half))
            dubs = lax.dynamic_slice(vec, (10 + 2 * me, 0), (2, D)).reshape(hid_half)
            return (
                out, dxs, vec[0:2], vec[2:4],
                jnp.stack([ga[:, i * half : (i + 1) * half] for i in range(3)]),
                qv, ga[:, 3 * half :].T, vec[4:6], vec[6:8],
                gup, dubs, gdown.T,
            )

        pick = lambda v: lax.dynamic_index_in_dim(v, me, 0, keepdims=False)
        if n_dp != 16 or n_tensor != 2:
            tokens, cotangent = pick(tokens), pick(cotangent)
            net = Plain(n_tensor)
            dest = jnp.arange(2 * BLOCKS, dtype=jnp.int32)
            slots = jnp.concatenate([jnp.arange(BLOCKS, dtype=jnp.int32)] * 2)
            ctl = jnp.stack([me, 0]).astype(jnp.int32)
            wa = net.gather(wa)
            wf = [net.gather(w) for w in pack_ffn(up_weight, down_weight)]
            ub1, ub2, segc, segr, ln1, ln2, qbt, ob0 = consts(small, segment)
            q, k, v, o1, lse1 = attn_fwd1(ctl, dest, tokens, segc, segr, ln1, qbt, wa)
            x1, attn, o2, lse2 = attn_fwd2(ctl, dest, tokens, segc, segr, ln1, ob0, q, k, v, o1, wa)
            f, dn, dub1, k1, s1 = ffn(True, ctl, dest, slots, x1, cotangent, segc, ln2, ub1, (), wf[0])
            y0, y1, dx1, vec_f, dub2, k2, s2 = ffn(False, ctl, dest, slots, x1, cotangent, segc, ln2, ub2, (attn, f, dn), wf[1])
            dz1 = attn_bwd(0, ctl, dest, dx1, q, k, v, lse1, segc, segr, ln1, wa)
            dz2 = attn_bwd(1, ctl, dest, dx1, q, k, v, lse2, segc, segr, ln1, wa)
            ka, sa = attn_grad(ctl, slots, tokens, dx1, o1, o2, dz1, dz2, ln1)
            dx, vec = input_grad(ctl, dest, tokens, dx1, dz1, dz2, ln1, vec_f, dub1, dub2, wa)
            gf1, gf2, ga = net.settle(k1, s1), net.settle(k2, s2), net.settle(ka, sa)
            vec = net.total(vec)
            gup = jnp.concatenate([gf1[:, :FCH], gf2[:, :FCH]], axis=1)
            gdown = jnp.concatenate([gf1[:, FCH:], gf2[:, FCH:]], axis=1)
            y = jnp.concatenate([y0, y1])
            return results(both(y, swap(y, n_tensor)), both(dx, swap(dx, n_tensor)), vec, ga, gup, gdown)

        net = Grid()
        place = lax.axis_index("dp") * 2 + me
        bs = net.along([wa] * 3)
        up_weight, down_weight, segment, small, place = after((up_weight, down_weight, segment, small, place), bs[0])
        fs, es = pack_ffn(up_weight, down_weight)
        fs, bs = after((fs, bs))
        s = after(jnp.stack([wa, *bs]))
        ra = net.send(s, net.first)
        fz = net.along([after(fs, s)] * 3)
        tokens, small, segment, place = after((tokens, small, segment, place), s)
        tokens = pick(tokens)
        ub1, ub2, segc, segr, ln1, ln2, qbt, ob0 = consts(small, segment)
        table = lax.dynamic_index_in_dim(net.tables(), place, 0, keepdims=False)
        dest, slots, slots_f = (table[i : i + 2 * BLOCKS] for i in range(0, 6 * BLOCKS, 2 * BLOCKS))
        ctl = jnp.stack([me, lax.axis_index("dp") % 2]).astype(jnp.int32)
        ra = after(ra, segc, dest, qbt)
        s = jnp.concatenate([s, ra])
        r = net.send(s, net.second)
        sc = net.send(s, net.core)
        cotangent = pick(after(cotangent, s))
        fz = after(fz, s)
        fs = after(jnp.stack([fs, *fz]))
        ez = net.along([after(es, fs)] * 3)
        r = after(r, sc, fs, cotangent)
        rc = net.send(r, net.core)
        fs = after(fs, r)
        fr = net.send(fs, net.first)
        fr = after(fr, rc)
        fs = jnp.concatenate([fs, fr])
        r1 = net.send(fs, net.second)
        c1 = net.send(fs, net.core)
        wa = after([s, r, sc, rc], fs)
        q, k, v, o1, lse1 = attn_fwd1(ctl, dest, tokens, segc, segr, ln1, qbt, wa)
        r1, c1, ez = after((r1, c1, ez), o1)
        w1 = [fs, r1, c1, net.send(r1, net.core)]
        es = after(jnp.stack([es, *ez]), r1)
        er = net.send(es, net.first)
        q = after(q, es, r1)
        x1, attn, o2, lse2 = attn_fwd2(ctl, dest, tokens, segc, segr, ln1, ob0, q, k, v, o1, wa)
        w1, er = after((w1, er), x1)
        es = jnp.concatenate([es, er])
        r2 = net.send(es, net.second)
        c2 = net.send(es, net.core)
        w1 = after(w1, es)
        f, dn, dub1, k1, s1 = ffn(True, ctl, dest, slots, x1, cotangent, segc, ln2, ub1, (), w1)
        r2, c2 = after((r2, c2), f)
        w2 = [es, r2, c2, net.send(r2, net.core)]
        g1 = Reduce(net, k1, s1, net.first, net.second)
        y0, y1, dx1, vec_f, dub2, k2, s2 = ffn(False, ctl, dest, slots_f, x1, cotangent, segc, ln2, ub2, (attn, f, dn), w2)
        g2 = Reduce(net, k2, s2, net.x, net.y)
        g1.start(dx1)
        dx1 = after(dx1, g1.sent)
        dz1 = attn_bwd(0, ctl, dest, dx1, q, k, v, lse1, segc, segr, ln1, wa)
        g1.start(dz1[0])
        g2.start(dz1[0], g1.sent)
        z0 = swap(after(y0, g2.sent), n_tensor)
        dx1 = after(dx1, dz1[0], g1.sent, g2.sent)
        dz2 = attn_bwd(1, ctl, dest, dx1, q, k, v, lse2, segc, segr, ln1, wa)
        z1 = swap(after(y1, dz2[0]), n_tensor)
        dx1 = after(dx1, dz2[0], z0)
        ka, sa = attn_grad(ctl, slots, tokens, dx1, o1, o2, dz1, dz2, ln1)
        g = Reduce(net, ka, sa, net.first, net.second)
        g1.start(ka)
        g2.start(ka)
        dx1 = after(dx1, ka, g1.sent, g2.sent, z1)
        dx, vec = input_grad(ctl, dest, tokens, dx1, dz1, dz2, ln1, vec_f, dub1, dub2, wa)
        def add(v, to, *dep):
            v = after(v, *dep)
            return v + net.send(v, to)

        g.start(dx)
        vec = add(add(add(vec, net.first, g.sent), net.z1), net.z2)
        g2.start(g.sent, vec)
        y0, y1, z0, z1 = after((y0, y1, z0, z1), g.sent)
        out = both(jnp.concatenate([y0, y1]), jnp.concatenate([z0, z1]))
        gf1 = g1.result(g.sent)
        g.start(g2.sent, gf1, out)
        vec = add(vec, net.second, g.sent)
        dx_other = swap(after(dx, vec), n_tensor)
        g.start(vec)
        gf2 = g2.result(g.sent)
        vec = add(vec, net.core, g.sent)
        gup = jnp.concatenate([gf1[:, :FCH], gf2[:, :FCH]], axis=1)
        gdown = jnp.concatenate([gf1[:, FCH:], gf2[:, FCH:]], axis=1)
        dxs = both(dx, dx_other)
        return results(out, dxs, vec, g.result(), gup, gdown)

    return on_device


def solution(mesh):
    rows = P(None, "dp", None)
    wt = P("tensor", "dp")
    return jax.shard_map(
        make_on_device(mesh.shape["dp"], mesh.shape["tensor"]),
        mesh=mesh,
        in_specs=(
            rows, P(None, "dp"), rows, P(), P(), P(None, "dp", "tensor"), P(None, "tensor"), wt,
            P(), P(), P("dp", "tensor"), P("tensor"), wt,
        ),
        out_specs=(
            rows, rows, P(), P(), P(None, "dp", "tensor"), P(None, "tensor"), wt,
            P(), P(), P("dp", "tensor"), P("tensor"), wt,
        ),
        check_vma=False,
    )
```

```python
import functools

import jax
import jax.numpy as jnp
from jax import lax
from jax.experimental import pallas as pl
from jax.experimental.pallas import tpu as pltpu
from jax.sharding import PartitionSpec as P

D = 768
HEADS = 12
HEAD = D // HEADS
EPS = 1e-06
PAD_ID = 3
NEG = -1e30
BF = jnp.bfloat16
F32 = jnp.float32
LOG2E = 1.4426950408889634

BLOCKS = 16
BROWS = D // BLOCKS


def mm(a, b):
    return jnp.dot(a, b, preferred_element_type=F32)


def mm_nt(a, b):
    return lax.dot_general(a, b, (((1,), (1,)), ((), ())), preferred_element_type=F32)


def mm_tn(a, b):
    return lax.dot_general(a, b, (((0,), (0,)), ((), ())), preferred_element_type=F32)


def row_stats(v):
    mean = jnp.mean(v, axis=-1, keepdims=True)
    c = v - mean
    rstd = lax.rsqrt(jnp.mean(c * c, axis=-1, keepdims=True) + EPS)
    return c * rstd, rstd


def norm_back(xhat, rstd, dn, gain):
    dxh = dn * gain
    m1 = jnp.mean(dxh, axis=-1, keepdims=True)
    m2 = jnp.mean(dxh * xhat, axis=-1, keepdims=True)
    return rstd * (dxh - m1 - xhat * m2)


def col_sum(v):
    return jnp.sum(v, axis=0, keepdims=True)


def load_blocks(dest, parts, dst, sem, cols=slice(None)):
    copies = []
    n = 0
    for part in parts:
        for j in range(part.shape[0]):
            row = pl.multiple_of(dest[n] * BROWS, BROWS)
            copies.append(pltpu.make_async_copy(part.at[j, :, cols], dst.at[pl.ds(row, BROWS)], sem.at[n]))
            n += 1
    for c in copies:
        c.start()
    return copies


def store_copies(core, slots, t, stage, outs, cols, sem):
    keep, send = outs
    copies = []
    half = BLOCKS // 2
    for m in range(half):
        a = pl.multiple_of((2 * m + core) * BROWS, BROWS)
        b = pl.multiple_of((2 * m + 1 - core) * BROWS, BROWS)
        copies.append(pltpu.make_async_copy(stage.at[pl.ds(a, BROWS)], keep.at[slots[t * half + m], :, cols], sem.at[2 * m]))
        copies.append(pltpu.make_async_copy(stage.at[pl.ds(b, BROWS)], send.at[slots[BLOCKS + t * half + m], :, cols], sem.at[2 * m + 1]))
    return copies


def pair_mask(h, dtype=BF):
    lane = lax.broadcasted_iota(jnp.int32, (1, 2 * HEAD), 1)
    return (lane // HEAD == h).astype(dtype)


def call(kernel, name, scalars, ins, outs, scratch, us, vmem=32):
    spaces = {None: pltpu.VMEM, 0: pltpu.VMEM, 1: pl.ANY, "hbm": pl.ANY, "far": pltpu.HBM}
    at = lambda how: pl.BlockSpec(memory_space=spaces[how])
    return pl.pallas_call(
        kernel,
        in_specs=[pl.BlockSpec(memory_space=pltpu.SMEM)] * len(scalars) + [at(how) for _, how in ins],
        out_specs=[at(how) for _, _, how in outs],
        out_shape=[jax.ShapeDtypeStruct(shape, dtype) for shape, dtype, _ in outs],
        scratch_shapes=scratch,
        compiler_params=pltpu.CompilerParams(vmem_limit_bytes=vmem * 1024 * 1024),
        cost_estimate=pl.CostEstimate(flops=us * 5_000_000_000, bytes_accessed=us * 1_000_000, transcendentals=0),
        name=name,
    )(*scalars, *[v for v, _ in ins])


PAIRS = HEADS // 2
HP = PAIRS // 2


def fwd_pairs(q_ref, k_ref, v_ref, bias_s, o_ref, lse_ref):
    scale = (HEAD ** (-0.5)) * LOG2E

    def pair(p, _):
        q2 = q_ref[p]
        k2 = k_ref[p]
        v2 = v_ref[p]
        acc = None
        for h in range(2):
            m = pair_mask(h)
            s = mm_nt(q2, k2 * m) * scale + bias_s[...]
            top = jnp.max(s, axis=-1, keepdims=True)
            e = jnp.exp2(s - top)
            tot = jnp.sum(e, axis=-1, keepdims=True)
            oh = mm(e.astype(BF), v2 * m) * (1.0 / tot)
            acc = oh if acc is None else acc + oh
            lse_ref[2 * p + h, :, 0 : top.shape[0]] = (top + jnp.log2(tot)).reshape(1, -1)
        o_ref[p] = acc.astype(BF)
        return 0

    lse_ref[...] = jnp.zeros_like(lse_ref)
    lax.fori_loop(0, HP, pair, 0)


def half_heads(t, src, dst, sem):
    copies = []
    for i, (a, b) in enumerate(zip(src, dst)):
        n = min(a.shape[1], b.shape[1])
        copies.append(pltpu.make_async_copy(a.at[pl.ds(HP * t, HP), 0:n], b.at[:, 0:n], sem.at[i]))
    for c in copies:
        c.start()
    return copies


def attn_fwd1_kernel(nw, rows, rp, cp, ctl, dest, x_ref, segc_ref, segr_ref, ln_ref, qb_ref, *rest):
    w = rest[:nw]
    qh, kh, vh, o_ref, lse_ref, w_s, x_s, bias_s, q_ref, k_ref, v_ref, sem, osem = rest[nw:]
    copies = load_blocks(dest, w, w_s, sem)
    x_s[0:rows, :] = x_ref[...].astype(F32)
    x_s[rows:rp, :] = jnp.zeros((rp - rows, D), F32)
    bias_s[...] = jnp.where(segc_ref[...] == segr_ref[...], 0.0, NEG)
    xhat, _ = row_stats(x_s[...])
    n1 = (xhat * ln_ref[0:1] + ln_ref[1:2]).astype(BF)
    for c in copies:
        c.wait()
    half = D // 2
    k_ref[:, rp:cp, :] = jnp.zeros((PAIRS, cp - rp, 128), BF)
    v_ref[:, rp:cp, :] = jnp.zeros((PAIRS, cp - rp, 128), BF)
    x_s[...] = n1.astype(F32)

    def project(t, _):
        z = mm(x_s[...].astype(BF), w_s[pl.ds(pl.multiple_of(t * D, D), D), 0 : 3 * half]) + qb_ref[pl.ds(t, 1)]
        z = z.astype(BF)
        for i in range(HP):
            q_ref[HP * t + i] = z[:, i * 128 : (i + 1) * 128]
            k_ref[HP * t + i, 0:rp, :] = z[:, half + i * 128 : half + (i + 1) * 128]
            v_ref[HP * t + i, 0:rp, :] = z[:, 2 * half + i * 128 : 2 * half + (i + 1) * 128]
        return 0

    lax.fori_loop(0, 2, project, 0)
    out = [pltpu.make_async_copy(a, b, osem.at[i]) for i, (a, b) in enumerate(((q_ref, qh), (k_ref, kh), (v_ref, vh)))]
    for c in out:
        c.start()
    fwd_pairs(q_ref, k_ref, v_ref, bias_s, o_ref, lse_ref)
    for c in out:
        c.wait()


def attn_fwd2_kernel(nw, rows, rp, cp, ctl, dest, x_ref, segc_ref, segr_ref, ln_ref, ob_ref, qh, kh, vh, o1_ref, *rest):
    w = rest[:nw]
    x1_ref, attn_ref, o_ref, lse_ref, w_s, bias_s, q_s, k_s, v_s, sem, isem = rest[nw:]
    heads = half_heads(1, (qh, kh, vh), (q_s, k_s, v_s), isem)
    half = D // 2
    copies = load_blocks(dest, w, w_s, sem, slice(3 * half, 4 * half))
    bias_s[...] = jnp.where(segc_ref[...] == segr_ref[...], 0.0, NEG)
    for c in heads:
        c.wait()
    fwd_pairs(q_s, k_s, v_s, bias_s, o_ref, lse_ref)
    for c in copies:
        c.wait()
    a = ob_ref[0:1]
    for t, src in enumerate((o1_ref, o_ref)):
        o_t = jnp.concatenate([src[i] for i in range(HP)], axis=1)
        a = a + mm_nt(o_t, w_s[t * D : (t + 1) * D, :]).astype(BF).astype(F32)
    attn_ref[...] = a
    x1_ref[...] = ln_ref[2:3] * a
    x1_ref[0:rows, :] += x_ref[...].astype(F32)


def attn_fwd1(ctl, dest, tokens, segc, segr, ln, qb, weights):
    rows, rp, cp = tokens.shape[0], segc.shape[0], segr.shape[1]
    wcols = weights[0].shape[2]
    return call(
        functools.partial(attn_fwd1_kernel, len(weights), rows, rp, cp), "attn_fwd1", (ctl, dest),
        [(tokens, None), (segc, None), (segr, None), (ln, None), (qb, None)] + [(w, "hbm") for w in weights],
        [((PAIRS, rp, 128), BF, "far"), ((PAIRS, cp, 128), BF, "far"), ((PAIRS, cp, 128), BF, "far"), ((HP, rp, 128), BF, 0), ((HEADS // 2, 1, cp), F32, 0)],
        [
            pltpu.VMEM((2 * D, wcols), BF), pltpu.VMEM((rp, D), F32), pltpu.VMEM((rp, cp), F32), pltpu.VMEM((PAIRS, rp, 128), BF), pltpu.VMEM((PAIRS, cp, 128), BF), pltpu.VMEM((PAIRS, cp, 128), BF),
            pltpu.SemaphoreType.DMA((2 * BLOCKS,)), pltpu.SemaphoreType.DMA((3,)),
        ],
        14,
    )


def attn_fwd2(ctl, dest, tokens, segc, segr, ln, ob, q, k, v, o1, weights):
    rows, rp, cp = tokens.shape[0], segc.shape[0], segr.shape[1]
    wcols = weights[0].shape[2]
    return call(
        functools.partial(attn_fwd2_kernel, len(weights), rows, rp, cp), "attn_fwd2", (ctl, dest),
        [(tokens, None), (segc, None), (segr, None), (ln, None), (ob, None), (q, "far"), (k, "far"), (v, "far"), (o1, None)] + [(w, "hbm") for w in weights],
        [((rp, D), F32, 0), ((rp, D), F32, 0), ((HP, rp, 128), BF, 0), ((HEADS // 2, 1, cp), F32, 0)],
        [
            pltpu.VMEM((2 * D, wcols // 4), BF), pltpu.VMEM((rp, cp), F32), pltpu.VMEM((HP, rp, 128), BF), pltpu.VMEM((HP, cp, 128), BF), pltpu.VMEM((HP, cp, 128), BF),
            pltpu.SemaphoreType.DMA((2 * BLOCKS,)), pltpu.SemaphoreType.DMA((3,)),
        ],
        12,
    )


def gelu_parts(h):
    x = jnp.abs(h) * 0.7071067811865476
    t = 1.0 / (1.0 + 0.3275911 * x)
    e = jnp.exp2(h * h * (-0.5 * LOG2E))
    poly = t * (0.254829592 * 0.5 + t * (-0.284496736 * 0.5 + t * (1.421413741 * 0.5 + t * (-1.453152027 * 0.5 + t * (1.061405429 * 0.5)))))
    tail = poly * e
    phi = jnp.where(h < 0, tail, 1.0 - tail)
    return phi, phi + h * e * 0.3989422804014327


FCH = 768


def ffn_kernel(rows, rp, first, ctl, dest, slots, x1_ref, cot_ref, segc_ref, ln_ref, ub_ref, *rest):
    if first:
        nw = len(rest) - 14
        w = rest[:nw]
        (f_ref, dn_ref, dub_ref, keep, send, w_s, n2_s, n2t_s, dfr_s, dft_s, dy_s, stage, lsem, ssem) = rest[nw:]
    else:
        attn_ref, fin_ref, dnin_ref = rest[:3]
        nw = len(rest) - 3 - 18
        w = rest[3 : 3 + nw]
        (y0_ref, y1_ref, dx1_ref, vec_ref, dub_ref, keep, send, w_s, n2_s, n2t_s, dfr_s, dft_s, dy_s, stage, f_ref, dn_ref, lsem, ssem) = rest[3 + nw :]
    copies = load_blocks(dest, w, w_s, lsem)
    core = ctl[1]
    live = (segc_ref[...] != PAD_ID).astype(F32)
    xhat, rstd = row_stats(x1_ref[...])
    n2 = (xhat * ln_ref[0:1] + ln_ref[1:2]).astype(BF)
    n2_s[...] = n2
    n2t_s[...] = n2.T
    dy_s[rows:rp, :] = jnp.zeros((rp - rows, D), F32)
    dy_s[0:rows, :] = cot_ref[...].astype(F32)
    dy = dy_s[...] * live
    dy_s[...] = dy
    df = dy * ln_ref[2:3]
    dfr = df.astype(BF)
    dfr_s[...] = dfr
    dft_s[...] = dfr.T
    if not first:
        vec_ref[2:3] = col_sum(df)
    for c in copies:
        c.wait()
    if first:
        f_ref[...] = jnp.zeros((rp, D), F32)
        dn_ref[...] = jnp.zeros((rp, D), F32)
    else:
        f_ref[...] = fin_ref[...]
        dn_ref[...] = dnin_ref[...]
    copies_of = lambda t: store_copies(core, slots, t, stage.at[t], (keep, send), pl.ds(0, 2 * FCH), ssem.at[t])

    def half_units(t, _):
        rows_t = pl.ds(pl.multiple_of(t * D, D), D)
        wu = w_s[rows_t, 0:FCH]
        wd = w_s[rows_t, FCH:]
        hid = mm(n2_s[...], wu) + ub_ref[pl.ds(t, 1)]
        phi, slope = gelu_parts(hid)
        g = (hid * phi).astype(BF)
        dh = (mm(dfr_s[...], wd) * slope).astype(BF)
        dub_ref[pl.ds(t, 1)] = col_sum(dh.astype(F32))
        stage[t, :, 0:FCH] = mm(n2t_s[...], dh).astype(BF)
        stage[t, :, FCH:] = mm(dft_s[...], g).astype(BF)
        for c in copies_of(t):
            c.start()
        f_ref[...] += mm_nt(g, wd)
        dn_ref[...] += mm_nt(dh, wu)
        return 0

    lax.fori_loop(0, 2, half_units, 0)
    pending = copies_of(0) + copies_of(1)
    if not first:
        ffo = f_ref[...] + ln_ref[3:4]
        dy = dy_s[...]
        vec_ref[3:4] = col_sum(dy * ffo)
        y = (x1_ref[...] + ln_ref[2:3] * ffo).astype(BF)
        cut = y0_ref.shape[0]
        y0_ref[...] = y[0:cut]
        y1_ref[...] = y[cut:rows]
        dn2 = dn_ref[...]
        xhat, rstd = row_stats(x1_ref[...])
        vec_ref[0:1] = col_sum(dn2 * xhat)
        vec_ref[1:2] = col_sum(dn2)
        dx1 = dy + norm_back(xhat, rstd, dn2, ln_ref[0:1])
        dx1_ref[...] = dx1
        vec_ref[4:5] = col_sum(dx1 * ln_ref[4:5])
        vec_ref[5:6] = col_sum(dx1 * attn_ref[...])
        vec_ref[6:8] = jnp.zeros((2, D), F32)
    for c in pending:
        c.wait()


def ffn(first, ctl, dest, slots, x1, cotangent, segc, ln, ub, more, weights):
    rows, rp = cotangent.shape[0], x1.shape[0]
    wcols = weights[0].shape[2]
    if first:
        outs = [((rp, D), F32, 0), ((rp, D), F32, 0)]
    else:
        cut = -(-rows // 32) * 16
        outs = [((cut, D), BF, 0), ((rows - cut, D), BF, 0), ((rp, D), F32, 0), ((8, D), F32, 0)]
    outs += [((2, FCH), F32, 0)] + [((BLOCKS, BROWS, wcols), BF, 1)] * 2
    return call(
        functools.partial(ffn_kernel, rows, rp, first), "ffn_first" if first else "ffn_last", (ctl, dest, slots),
        [(x1, None), (cotangent, None), (segc, None), (ln, None), (ub, None)] + [(v, None) for v in more] + [(w, "hbm") for w in weights],
        outs,
        [
            pltpu.VMEM((2 * D, wcols), BF), pltpu.VMEM((rp, D), BF), pltpu.VMEM((D, rp), BF), pltpu.VMEM((rp, D), BF), pltpu.VMEM((D, rp), BF),
            pltpu.VMEM((rp, D), F32), pltpu.VMEM((2, D, 2 * FCH), BF),
        ]
        + ([] if first else [pltpu.VMEM((rp, D), F32)] * 2)
        + [pltpu.SemaphoreType.DMA((2 * BLOCKS,)), pltpu.SemaphoreType.DMA((2, BLOCKS))],
        20, 60,
    )


def attn_bwd_kernel(nw, rp, cp, which, ctl, dest, dx1_ref, qh, kh, vh, lse_ref, segc_ref, segr_ref, ln_ref, *rest):
    w = rest[:nw]
    dq_ref, dk_ref, dv_ref, w_s, do_s, q_s, k_s, v_s, bias_s, sem, isem = rest[nw:]
    t = which[0]
    heads = half_heads(t, (qh, kh, vh), (q_s, k_s, v_s), isem)
    half = D // 2
    copies = load_blocks(dest, w, w_s, sem, slice(3 * half, 4 * half))
    scale = HEAD ** (-0.5)
    bias_s[...] = jnp.where(segc_ref[...] == segr_ref[...], 0.0, NEG)
    q_s[:, rp:cp, :] = jnp.zeros((HP, cp - rp, 128), BF)
    do_s[:, rp:cp, :] = jnp.zeros((HP, cp - rp, 128), BF)
    dar = (dx1_ref[...] * ln_ref[2:3]).astype(BF)
    for c in copies:
        c.wait()
    z = mm(dar, w_s[pl.ds(pl.multiple_of(t * D, D), D), :]).astype(BF)
    for i in range(HP):
        do_s[i, 0:rp, :] = z[:, i * 128 : (i + 1) * 128]
    for c in heads:
        c.wait()

    def pair(p, _):
        q2 = q_s[p]
        do2 = do_s[p]
        k2 = k_s[p]
        v2 = v_s[p]
        dq = dk = dv = None
        for h in range(2):
            m = pair_mask(h)
            km = k2 * m
            st = mm_nt(km, q2) * (scale * LOG2E) + bias_s[...]
            pt = jnp.exp2(st - lse_ref[2 * p + h])
            dpt = mm_nt(v2 * m, do2)
            delta = jnp.sum(pt * dpt, axis=0, keepdims=True)
            dst = (pt * (dpt - delta)).astype(BF)
            a = mm(pt.astype(BF), do2 * m)
            b = mm(dst, q2 * m)
            c = mm_tn(dst, km)
            dv = a if dv is None else dv + a
            dk = b if dk is None else dk + b
            dq = c if dq is None else dq + c
        dq_ref[p] = (dq[0:rp] * scale).astype(BF)
        dk_ref[p] = (dk * scale).astype(BF)
        dv_ref[p] = dv.astype(BF)
        return 0

    lax.fori_loop(0, HP, pair, 0)


def attn_bwd(t, ctl, dest, dx1, q, k, v, lse, segc, segr, ln, weights):
    rp, cp = segc.shape[0], segr.shape[1]
    wcols = weights[0].shape[2]
    return call(
        functools.partial(attn_bwd_kernel, len(weights), rp, cp), "attn_bwd", (jnp.full((1,), t, jnp.int32), ctl, dest),
        [(dx1, None), (q, "far"), (k, "far"), (v, "far")] + [(e, None) for e in (lse, segc, segr, ln)] + [(w, "hbm") for w in weights],
        [((HP, rp, 128), BF, 0)] * 3,
        [
            pltpu.VMEM((2 * D, wcols // 4), BF), pltpu.VMEM((HP, cp, 128), BF), pltpu.VMEM((HP, cp, 128), BF), pltpu.VMEM((HP, rp, 128), BF), pltpu.VMEM((HP, rp, 128), BF),
            pltpu.VMEM((rp, cp), F32), pltpu.SemaphoreType.DMA((2 * BLOCKS,)), pltpu.SemaphoreType.DMA((3,)),
        ],
        15, 60,
    )


def attn_grad_kernel(rows, rp, ctl, slots, x_ref, dx1_ref, o1_ref, o2_ref, dq1, dk1, dv1, dq2, dk2, dv2, ln_ref, keep, send, stage, x_s, ssem):
    core = ctl[1]
    half = D // 2
    x_s[0:rows, :] = x_ref[...].astype(F32)
    x_s[rows:rp, :] = jnp.zeros((rp - rows, D), F32)
    dart = (dx1_ref[...] * ln_ref[2:3]).astype(BF).T
    xhat, _ = row_stats(x_s[...])
    n1t = (xhat * ln_ref[0:1] + ln_ref[1:2]).astype(BF).T
    pend = []
    for t, (o, dz) in enumerate(((o1_ref, (dq1, dk1, dv1)), (o2_ref, (dq2, dk2, dv2)))):
        o_t = jnp.concatenate([o[i] for i in range(HP)], axis=1)
        stage[t, :, 3 * half :] = mm(dart, o_t).astype(BF)
        z = jnp.concatenate([e[i] for e in dz for i in range(HP)], axis=1)
        stage[t, :, 0 : 3 * half] = mm(n1t, z).astype(BF)
        cps = store_copies(core, slots, t, stage.at[t], (keep, send), pl.ds(0, 4 * half), ssem.at[t])
        for c in cps:
            c.start()
        pend += cps
    for c in pend:
        c.wait()


def attn_grad(ctl, slots, tokens, dx1, o1, o2, dz1, dz2, ln):
    rows, rp = tokens.shape[0], dx1.shape[0]
    wcols = 2 * D
    return call(
        functools.partial(attn_grad_kernel, rows, rp), "attn_grad", (ctl, slots),
        [(tokens, None)] + [(e, None) for e in (dx1, o1, o2, *dz1, *dz2, ln)],
        [((BLOCKS, BROWS, wcols), BF, 1)] * 2,
        [pltpu.VMEM((2, D, wcols), BF), pltpu.VMEM((rp, D), F32), pltpu.SemaphoreType.DMA((2, BLOCKS))],
        10, 48,
    )


def input_grad_kernel(nw, rows, rp, ctl, dest, x_ref, dx1_ref, dq1, dk1, dv1, dq2, dk2, dv2, ln_ref, vecf_ref, dub1_ref, dub2_ref, *rest):
    w = rest[:nw]
    dx_ref, vec_ref, w_s, x_s, sem = rest[nw:]
    half = D // 2
    copies = load_blocks(dest, w, w_s, sem, slice(0, 3 * half))
    x_s[0:rows, :] = x_ref[...].astype(F32)
    x_s[rows:rp, :] = jnp.zeros((rp - rows, D), F32)
    xhat, rstd = row_stats(x_s[...])
    for c in copies:
        c.wait()
    dn1 = None
    for t, dz in enumerate(((dq1, dk1, dv1), (dq2, dk2, dv2))):
        z = jnp.concatenate([e[i] for e in dz for i in range(HP)], axis=1)
        part = mm_nt(z, w_s[t * D : (t + 1) * D, :])
        dn1 = part if dn1 is None else dn1 + part
        vec_ref[8:9, t * half : (t + 1) * half] = col_sum(z[:, 0:half].astype(F32))
        vec_ref[9:10, t * half : (t + 1) * half] = col_sum(z[:, 2 * half :].astype(F32))
        vec_ref[10 + 2 * t : 11 + 2 * t] = dub1_ref[t : t + 1]
        vec_ref[11 + 2 * t : 12 + 2 * t] = dub2_ref[t : t + 1]
    vec_ref[0:1] = col_sum(dn1 * xhat)
    vec_ref[2:3] = col_sum(dn1)
    for i, row in enumerate((1, 3, 5, 7, 4, 6)):
        vec_ref[row : row + 1] = vecf_ref[i : i + 1]
    vec_ref[14:16] = jnp.zeros((2, D), F32)
    dx = dx1_ref[...] + norm_back(xhat, rstd, dn1, ln_ref[0:1])
    dx_ref[...] = dx[0:rows].astype(BF)


def input_grad(ctl, dest, tokens, dx1, dz1, dz2, ln, vec_f, dub1, dub2, weights):
    rows, rp = tokens.shape[0], dx1.shape[0]
    wcols = weights[0].shape[2]
    return call(
        functools.partial(input_grad_kernel, len(weights), rows, rp), "input_grad", (ctl, dest),
        [(tokens, None)] + [(e, None) for e in (dx1, *dz1, *dz2, ln, vec_f, dub1, dub2)] + [(w, "hbm") for w in weights],
        [((rows, D), BF, 0), ((16, D), F32, 0)],
        [pltpu.VMEM((2 * D, wcols * 3 // 4), BF), pltpu.VMEM((rp, D), F32), pltpu.SemaphoreType.DMA((2 * BLOCKS,))],
        10,
    )


def prepare(segment, me, ln_gain, ln_shift, qb, out_bias, layer_scale):
    rows = segment.shape[1]
    rp = -(-rows // 16) * 16
    cp = -(-rp // 128) * 128
    seg = lax.dynamic_index_in_dim(segment, me, 0, keepdims=False)
    seg = jnp.concatenate([seg, jnp.full((rp - rows,), -2, jnp.int32), jnp.full((cp - rp,), -1, jnp.int32)])
    segr = seg.reshape(1, cp)
    segc = seg[:rp].reshape(rp, 1)
    half = D // 2
    ln1 = jnp.stack([ln_gain[0], ln_shift[0], layer_scale[0]])
    ln2 = jnp.stack([ln_gain[1], ln_shift[1], layer_scale[1], out_bias[1], layer_scale[0]])
    z = jnp.zeros((2, half), F32)
    qbt = jnp.concatenate([qb[0].reshape(2, half), z, qb[1].reshape(2, half)], axis=1)
    return segc, segr, ln1, ln2, qbt, out_bias[0:1]


def swap(v, n_tensor):
    return lax.ppermute(v, "tensor", [(i, (i + 1) % n_tensor) for i in range(n_tensor)])


def after(v, *done):
    return lax.optimization_barrier((v, done))[0]


class Grid:
    axes = ("dp", "tensor")
    places = [(z, y, c, t) for z in range(4) for y in range(2) for c in range(2) for t in range(2)]

    def number(self, p):
        return ((p[0] * 2 + p[1]) * 2 + p[2]) * 2 + p[3]

    def x(self, p):
        return p[0], p[1], p[2], 1 - p[3]

    def y(self, p):
        return p[0], 1 - p[1], p[2], p[3]

    def core(self, p):
        return p[0], p[1], 1 - p[2], p[3]

    def first(self, p):
        return self.y(p) if p[2] else self.x(p)

    def second(self, p):
        return self.x(p) if p[2] else self.y(p)

    def z1(self, p):
        return p[0] ^ 1, p[1], p[2], p[3]

    def z2(self, p):
        return p[0] ^ 2, p[1], p[2], p[3]

    def z3(self, p):
        return p[0] ^ 3, p[1], p[2], p[3]

    def along(self, v):
        return [self.send(e, to) for e, to in zip(v, (self.z1, self.z2, self.z3))]

    def send(self, v, to):
        return lax.ppermute(v, self.axes, [(self.number(p), self.number(to(p))) for p in self.places])

    def line(self, p):
        return [(p[0] ^ k, p[1], p[2], p[3]) for k in range(4)]

    def held(self, p, first, second):
        b = second(p)
        return self.line(p) + self.line(first(p)) + self.line(b) + self.line(first(b))

    def tables(self):
        where = lambda q: q[3] * BLOCKS + (q[0] * 2 + q[1]) * 2 + q[2]
        half = BLOCKS // 2
        rows = []
        for p in self.places:
            row = [where(q) for e in (p, self.core(p)) for q in self.held(e, self.first, self.second)]
            for route in ((self.first, self.second), (self.x, self.y)):
                at = {where(q): i for e in (p, self.core(p)) for i, q in enumerate(self.held(e, *route))}
                row += [at[t * BLOCKS + 2 * m + p[2]] for t in range(2) for m in range(half)]
                row += [at[t * BLOCKS + 2 * m + 1 - p[2]] for t in range(2) for m in range(half)]
            rows.append(row)
        return jnp.array(rows, jnp.int32)


def wide(v):
    return v.astype(F32)


class Reduce:
    def __init__(self, net, keep, sent, first, second):
        self.net, self.terms, self.sent, self.first, self.second = net, [keep], sent, first, second
        self.stage = 0
        self.got = net.send(sent, net.core)

    def total(self, at):
        return sum(wide(e[at]) for e in self.terms)

    def start(self, *dep):
        self.stage += 1
        n = self.stage
        self.terms.append(after(self.got, *dep))
        if n < 3:
            self.sent = self.total(slice(BLOCKS >> n, 2 * BLOCKS >> n)).astype(BF)
            self.got = self.net.send(self.sent, self.second if n == 1 else self.first)
        else:
            self.sent = [self.total(k).astype(BF) for k in (1, 2, 3)]
            self.got = self.net.along(self.sent)

    def result(self, *dep):
        return self.total(0) + sum(wide(e) for e in after(self.got, *dep))


class Plain:
    def __init__(self, n_tensor):
        self.n_tensor = n_tensor

    def gather(self, w):
        me = lax.axis_index("tensor")
        other = swap(w, self.n_tensor)
        both = jnp.where(me == 0, jnp.stack([w, other]), jnp.stack([other, w]))
        full = lax.all_gather(both, "dp", axis=1, tiled=True)
        return [full.reshape(2 * BLOCKS, BROWS, w.shape[1])]

    def settle(self, keep, sent):
        me = lax.axis_index("tensor")
        h = BLOCKS // 2
        g = jnp.stack([keep.reshape(2, h, BROWS, -1), sent.reshape(2, h, BROWS, -1)], axis=2).reshape(2, D, -1)
        part = lax.psum_scatter(g, "dp", scatter_dimension=1, tiled=True).astype(F32)
        return jnp.where(me == 0, part[0], part[1]) + swap(jnp.where(me == 0, part[1], part[0]), self.n_tensor)

    def total(self, v):
        return lax.psum(v, ("dp", "tensor"))


def make_on_device(n_dp, n_tensor):
    def on_device(
        tokens, segment, cotangent, ln_gain, ln_shift, qkv_weight, qv_bias, out_weight,
        out_bias, layer_scale, up_weight, up_bias, down_weight,
    ):
        me = lax.axis_index("tensor")
        own_first = lambda own, other, axis=0: jnp.where(me == 0, jnp.stack([own, other], axis), jnp.stack([other, own], axis))
        both = lambda own, other: own_first(own, other, 1).transpose(1, 0, 2)
        half = D // 2
        hid_half = up_weight.shape[1]
        wa = jnp.concatenate([qkv_weight[0], qkv_weight[1], qkv_weight[2], out_weight.T], axis=1)
        small = jnp.concatenate([qv_bias.reshape(-1), up_bias])

        def pack_ffn(up, down):
            down_t = down.T
            return [jnp.concatenate([up[:, lo : lo + FCH], down_t[:, lo : lo + FCH]], axis=1) for lo in range(0, hid_half, FCH)]

        def consts(small, segment):
            small = own_first(small, swap(small, n_tensor))
            qb = small[:, : 2 * half].reshape(2, 2, half).transpose(1, 0, 2).reshape(2, D)
            ub = small[:, 2 * half :]
            return (ub[:, :FCH], ub[:, FCH:]) + prepare(segment, me, ln_gain, ln_shift, qb, out_bias, layer_scale)

        def results(out, dxs, vec, ga, gup, gdown):
            qv = lax.dynamic_slice(vec, (8, me * half), (2, half))
            dubs = lax.dynamic_slice(vec, (10 + 2 * me, 0), (2, D)).reshape(hid_half)
            return (
                out, dxs, vec[0:2], vec[2:4],
                jnp.stack([ga[:, i * half : (i + 1) * half] for i in range(3)]),
                qv, ga[:, 3 * half :].T, vec[4:6], vec[6:8],
                gup, dubs, gdown.T,
            )

        pick = lambda v: lax.dynamic_index_in_dim(v, me, 0, keepdims=False)
        if n_dp != 16 or n_tensor != 2:
            tokens, cotangent = pick(tokens), pick(cotangent)
            net = Plain(n_tensor)
            dest = jnp.arange(2 * BLOCKS, dtype=jnp.int32)
            slots = jnp.concatenate([jnp.arange(BLOCKS, dtype=jnp.int32)] * 2)
            ctl = jnp.stack([me, 0]).astype(jnp.int32)
            wa = net.gather(wa)
            wf = [net.gather(w) for w in pack_ffn(up_weight, down_weight)]
            ub1, ub2, segc, segr, ln1, ln2, qbt, ob0 = consts(small, segment)
            q, k, v, o1, lse1 = attn_fwd1(ctl, dest, tokens, segc, segr, ln1, qbt, wa)
            x1, attn, o2, lse2 = attn_fwd2(ctl, dest, tokens, segc, segr, ln1, ob0, q, k, v, o1, wa)
            f, dn, dub1, k1, s1 = ffn(True, ctl, dest, slots, x1, cotangent, segc, ln2, ub1, (), wf[0])
            y0, y1, dx1, vec_f, dub2, k2, s2 = ffn(False, ctl, dest, slots, x1, cotangent, segc, ln2, ub2, (attn, f, dn), wf[1])
            dz1 = attn_bwd(0, ctl, dest, dx1, q, k, v, lse1, segc, segr, ln1, wa)
            dz2 = attn_bwd(1, ctl, dest, dx1, q, k, v, lse2, segc, segr, ln1, wa)
            ka, sa = attn_grad(ctl, slots, tokens, dx1, o1, o2, dz1, dz2, ln1)
            dx, vec = input_grad(ctl, dest, tokens, dx1, dz1, dz2, ln1, vec_f, dub1, dub2, wa)
            gf1, gf2, ga = net.settle(k1, s1), net.settle(k2, s2), net.settle(ka, sa)
            vec = net.total(vec)
            gup = jnp.concatenate([gf1[:, :FCH], gf2[:, :FCH]], axis=1)
            gdown = jnp.concatenate([gf1[:, FCH:], gf2[:, FCH:]], axis=1)
            y = jnp.concatenate([y0, y1])
            return results(both(y, swap(y, n_tensor)), both(dx, swap(dx, n_tensor)), vec, ga, gup, gdown)

        net = Grid()
        place = lax.axis_index("dp") * 2 + me
        bs = net.along([wa] * 3)
        tokens, cotangent, segment, small, place = after((tokens, cotangent, segment, small, place), wa)
        tokens, cotangent = pick(tokens), pick(cotangent)
        ub1, ub2, segc, segr, ln1, ln2, qbt, ob0 = consts(small, segment)
        table = lax.dynamic_index_in_dim(net.tables(), place, 0, keepdims=False)
        bs = after(bs, tokens, cotangent, segc, table)
        up_weight, down_weight = after((up_weight, down_weight), bs[0])
        fs, es = pack_ffn(up_weight, down_weight)
        fs, bs = after((fs, bs))
        s = after(jnp.stack([wa, *bs]))
        ra = net.send(s, net.first)
        fz = net.along([after(fs, s)] * 3)
        dest, slots, slots_f = (table[i : i + 2 * BLOCKS] for i in range(0, 6 * BLOCKS, 2 * BLOCKS))
        ctl = jnp.stack([me, lax.axis_index("dp") % 2]).astype(jnp.int32)
        ra = after(ra, dest, qbt)
        s = jnp.concatenate([s, ra])
        r = net.send(s, net.second)
        sc = net.send(s, net.core)
        fz = after(fz, s)
        fs = after(jnp.stack([fs, *fz]))
        ez = net.along([after(es, fs)] * 3)
        r = after(r, sc, fs)
        rc = net.send(r, net.core)
        fs = after(fs, r)
        fr = net.send(fs, net.first)
        fr = after(fr, rc)
        fs = jnp.concatenate([fs, fr])
        r1 = net.send(fs, net.second)
        c1 = net.send(fs, net.core)
        wa = after([s, r, sc, rc], fs)
        q, k, v, o1, lse1 = attn_fwd1(ctl, dest, tokens, segc, segr, ln1, qbt, wa)
        r1, c1, ez = after((r1, c1, ez), o1)
        w1 = [fs, r1, c1, net.send(r1, net.core)]
        es = after(jnp.stack([es, *ez]), r1)
        er = net.send(es, net.first)
        q = after(q, es, r1)
        x1, attn, o2, lse2 = attn_fwd2(ctl, dest, tokens, segc, segr, ln1, ob0, q, k, v, o1, wa)
        w1, er = after((w1, er), x1)
        es = jnp.concatenate([es, er])
        r2 = net.send(es, net.second)
        c2 = net.send(es, net.core)
        w1 = after(w1, es)
        f, dn, dub1, k1, s1 = ffn(True, ctl, dest, slots, x1, cotangent, segc, ln2, ub1, (), w1)
        r2, c2 = after((r2, c2), f)
        w2 = [es, r2, c2, net.send(r2, net.core)]
        g1 = Reduce(net, k1, s1, net.first, net.second)
        y0, y1, dx1, vec_f, dub2, k2, s2 = ffn(False, ctl, dest, slots_f, x1, cotangent, segc, ln2, ub2, (attn, f, dn), w2)
        g2 = Reduce(net, k2, s2, net.x, net.y)
        g1.start(dx1)
        dx1 = after(dx1, g1.sent)
        dz1 = attn_bwd(0, ctl, dest, dx1, q, k, v, lse1, segc, segr, ln1, wa)
        g1.start(dz1[0])
        g2.start(dz1[0], g1.sent)
        z0 = swap(after(y0, g2.sent), n_tensor)
        dx1 = after(dx1, dz1[0], g1.sent, g2.sent)
        dz2 = attn_bwd(1, ctl, dest, dx1, q, k, v, lse2, segc, segr, ln1, wa)
        z1 = swap(after(y1, dz2[0]), n_tensor)
        dx1 = after(dx1, dz2[0], z0)
        ka, sa = attn_grad(ctl, slots, tokens, dx1, o1, o2, dz1, dz2, ln1)
        g = Reduce(net, ka, sa, net.first, net.second)
        g1.start(ka)
        g2.start(ka)
        dx1 = after(dx1, ka, g1.sent, g2.sent, z1)
        dx, vec = input_grad(ctl, dest, tokens, dx1, dz1, dz2, ln1, vec_f, dub1, dub2, wa)
        def add(v, to, *dep):
            v = after(v, *dep)
            return v + net.send(v, to)

        g.start(dx)
        vec = add(add(vec, net.z1, g.sent), net.z2)
        g2.start(g.sent, vec)
        vec = add(vec, net.first)
        y0, y1, z0, z1 = after((y0, y1, z0, z1), g.sent)
        out = both(jnp.concatenate([y0, y1]), jnp.concatenate([z0, z1]))
        gf1 = g1.result(g.sent)
        g.start(g2.sent, gf1, out, vec)
        vec = add(vec, net.second, g.sent)
        dx_other = swap(after(dx, vec), n_tensor)
        g.start(vec)
        gf2 = g2.result(g.sent)
        vec = add(vec, net.core, g.sent)
        gup = jnp.concatenate([gf1[:, :FCH], gf2[:, :FCH]], axis=1)
        gdown = jnp.concatenate([gf1[:, FCH:], gf2[:, FCH:]], axis=1)
        dxs = both(dx, dx_other)
        return results(out, dxs, vec, g.result(), gup, gdown)

    return on_device


def solution(mesh):
    rows = P(None, "dp", None)
    wt = P("tensor", "dp")
    return jax.shard_map(
        make_on_device(mesh.shape["dp"], mesh.shape["tensor"]),
        mesh=mesh,
        in_specs=(
            rows, P(None, "dp"), rows, P(), P(), P(None, "dp", "tensor"), P(None, "tensor"), wt,
            P(), P(), P("dp", "tensor"), P("tensor"), wt,
        ),
        out_specs=(
            rows, rows, P(), P(), P(None, "dp", "tensor"), P(None, "tensor"), wt,
            P(), P(), P("dp", "tensor"), P("tensor"), wt,
        ),
        check_vma=False,
    )
```

```python
import functools

import jax
import jax.numpy as jnp
from jax import lax
from jax.experimental import pallas as pl
from jax.experimental.pallas import tpu as pltpu
from jax.sharding import PartitionSpec as P

D = 768
HEADS = 12
HEAD = D // HEADS
EPS = 1e-06
PAD_ID = 3
NEG = -1e30
BF = jnp.bfloat16
F32 = jnp.float32
LOG2E = 1.4426950408889634

BLOCKS = 16
BROWS = D // BLOCKS


def mm(a, b):
    return jnp.dot(a, b, preferred_element_type=F32)


def mm_nt(a, b):
    return lax.dot_general(a, b, (((1,), (1,)), ((), ())), preferred_element_type=F32)


def mm_tn(a, b):
    return lax.dot_general(a, b, (((0,), (0,)), ((), ())), preferred_element_type=F32)


def row_stats(v):
    mean = jnp.mean(v, axis=-1, keepdims=True)
    c = v - mean
    rstd = lax.rsqrt(jnp.mean(c * c, axis=-1, keepdims=True) + EPS)
    return c * rstd, rstd


def norm_back(xhat, rstd, dn, gain):
    dxh = dn * gain
    m1 = jnp.mean(dxh, axis=-1, keepdims=True)
    m2 = jnp.mean(dxh * xhat, axis=-1, keepdims=True)
    return rstd * (dxh - m1 - xhat * m2)


def col_sum(v):
    return jnp.sum(v, axis=0, keepdims=True)


def load_blocks(dest, parts, dst, sem, cols=slice(None)):
    copies = []
    n = 0
    for part in parts:
        for j in range(part.shape[0]):
            row = pl.multiple_of(dest[n] * BROWS, BROWS)
            copies.append(pltpu.make_async_copy(part.at[j, :, cols], dst.at[pl.ds(row, BROWS)], sem.at[n]))
            n += 1
    for c in copies:
        c.start()
    return copies


def store_copies(core, slots, t, stage, outs, cols, sem):
    keep, send = outs
    copies = []
    half = BLOCKS // 2
    for m in range(half):
        a = pl.multiple_of((2 * m + core) * BROWS, BROWS)
        b = pl.multiple_of((2 * m + 1 - core) * BROWS, BROWS)
        copies.append(pltpu.make_async_copy(stage.at[pl.ds(a, BROWS)], keep.at[slots[t * half + m], :, cols], sem.at[2 * m]))
        copies.append(pltpu.make_async_copy(stage.at[pl.ds(b, BROWS)], send.at[slots[BLOCKS + t * half + m], :, cols], sem.at[2 * m + 1]))
    return copies


def pair_mask(h, dtype=BF):
    lane = lax.broadcasted_iota(jnp.int32, (1, 2 * HEAD), 1)
    return (lane // HEAD == h).astype(dtype)


def call(kernel, name, scalars, ins, outs, scratch, us, vmem=32):
    spaces = {None: pltpu.VMEM, 0: pltpu.VMEM, 1: pl.ANY, "hbm": pl.ANY, "far": pltpu.HBM}
    at = lambda how: pl.BlockSpec(memory_space=spaces[how])
    return pl.pallas_call(
        kernel,
        in_specs=[pl.BlockSpec(memory_space=pltpu.SMEM)] * len(scalars) + [at(how) for _, how in ins],
        out_specs=[at(how) for _, _, how in outs],
        out_shape=[jax.ShapeDtypeStruct(shape, dtype) for shape, dtype, _ in outs],
        scratch_shapes=scratch,
        compiler_params=pltpu.CompilerParams(vmem_limit_bytes=vmem * 1024 * 1024),
        cost_estimate=pl.CostEstimate(flops=us * 5_000_000_000, bytes_accessed=us * 1_000_000, transcendentals=0),
        name=name,
    )(*scalars, *[v for v, _ in ins])


PAIRS = HEADS // 2
HP = PAIRS // 2


def fwd_pairs(q_ref, k_ref, v_ref, bias_s, o_ref, lse_ref):
    scale = (HEAD ** (-0.5)) * LOG2E

    def pair(p, _):
        q2 = q_ref[p]
        k2 = k_ref[p]
        v2 = v_ref[p]
        acc = None
        for h in range(2):
            m = pair_mask(h)
            s = mm_nt(q2, k2 * m) * scale + bias_s[...]
            top = jnp.max(s, axis=-1, keepdims=True)
            e = jnp.exp2(s - top)
            tot = jnp.sum(e, axis=-1, keepdims=True)
            oh = mm(e.astype(BF), v2 * m) * (1.0 / tot)
            acc = oh if acc is None else acc + oh
            lse_ref[2 * p + h, :, 0 : top.shape[0]] = (top + jnp.log2(tot)).reshape(1, -1)
        o_ref[p] = acc.astype(BF)
        return 0

    lse_ref[...] = jnp.zeros_like(lse_ref)
    lax.fori_loop(0, HP, pair, 0)


def half_heads(t, src, dst, sem):
    copies = []
    for i, (a, b) in enumerate(zip(src, dst)):
        n = min(a.shape[1], b.shape[1])
        copies.append(pltpu.make_async_copy(a.at[pl.ds(HP * t, HP), 0:n], b.at[:, 0:n], sem.at[i]))
    for c in copies:
        c.start()
    return copies


def attn_fwd1_kernel(nw, rows, rp, cp, ctl, dest, x_ref, segc_ref, segr_ref, ln_ref, qb_ref, *rest):
    w = rest[:nw]
    qh, kh, vh, o_ref, lse_ref, w_s, x_s, bias_s, q_ref, k_ref, v_ref, sem, osem = rest[nw:]
    copies = load_blocks(dest, w, w_s, sem)
    x_s[0:rows, :] = x_ref[...].astype(F32)
    x_s[rows:rp, :] = jnp.zeros((rp - rows, D), F32)
    bias_s[...] = jnp.where(segc_ref[...] == segr_ref[...], 0.0, NEG)
    xhat, _ = row_stats(x_s[...])
    n1 = (xhat * ln_ref[0:1] + ln_ref[1:2]).astype(BF)
    for c in copies:
        c.wait()
    half = D // 2
    k_ref[:, rp:cp, :] = jnp.zeros((PAIRS, cp - rp, 128), BF)
    v_ref[:, rp:cp, :] = jnp.zeros((PAIRS, cp - rp, 128), BF)
    x_s[...] = n1.astype(F32)

    def project(t, _):
        z = mm(x_s[...].astype(BF), w_s[pl.ds(pl.multiple_of(t * D, D), D), 0 : 3 * half]) + qb_ref[pl.ds(t, 1)]
        z = z.astype(BF)
        for i in range(HP):
            q_ref[HP * t + i] = z[:, i * 128 : (i + 1) * 128]
            k_ref[HP * t + i, 0:rp, :] = z[:, half + i * 128 : half + (i + 1) * 128]
            v_ref[HP * t + i, 0:rp, :] = z[:, 2 * half + i * 128 : 2 * half + (i + 1) * 128]
        return 0

    lax.fori_loop(0, 2, project, 0)
    out = [pltpu.make_async_copy(a, b, osem.at[i]) for i, (a, b) in enumerate(((q_ref, qh), (k_ref, kh), (v_ref, vh)))]
    for c in out:
        c.start()
    fwd_pairs(q_ref, k_ref, v_ref, bias_s, o_ref, lse_ref)
    for c in out:
        c.wait()


def attn_fwd2_kernel(nw, rows, rp, cp, ctl, dest, x_ref, segc_ref, segr_ref, ln_ref, ob_ref, qh, kh, vh, o1_ref, *rest):
    w = rest[:nw]
    x1_ref, attn_ref, o_ref, lse_ref, w_s, bias_s, q_s, k_s, v_s, sem, isem = rest[nw:]
    heads = half_heads(1, (qh, kh, vh), (q_s, k_s, v_s), isem)
    half = D // 2
    copies = load_blocks(dest, w, w_s, sem, slice(3 * half, 4 * half))
    bias_s[...] = jnp.where(segc_ref[...] == segr_ref[...], 0.0, NEG)
    for c in heads:
        c.wait()
    fwd_pairs(q_s, k_s, v_s, bias_s, o_ref, lse_ref)
    for c in copies:
        c.wait()
    a = ob_ref[0:1]
    for t, src in enumerate((o1_ref, o_ref)):
        o_t = jnp.concatenate([src[i] for i in range(HP)], axis=1)
        a = a + mm_nt(o_t, w_s[t * D : (t + 1) * D, :]).astype(BF).astype(F32)
    attn_ref[...] = a.astype(BF)
    x1_ref[...] = ln_ref[2:3] * a
    x1_ref[0:rows, :] += x_ref[...].astype(F32)


def attn_fwd1(ctl, dest, tokens, segc, segr, ln, qb, weights):
    rows, rp, cp = tokens.shape[0], segc.shape[0], segr.shape[1]
    wcols = weights[0].shape[2]
    return call(
        functools.partial(attn_fwd1_kernel, len(weights), rows, rp, cp), "attn_fwd1", (ctl, dest),
        [(tokens, None), (segc, None), (segr, None), (ln, None), (qb, None)] + [(w, "hbm") for w in weights],
        [((PAIRS, rp, 128), BF, "far"), ((PAIRS, cp, 128), BF, "far"), ((PAIRS, cp, 128), BF, "far"), ((HP, rp, 128), BF, 0), ((HEADS // 2, 1, cp), F32, 0)],
        [
            pltpu.VMEM((2 * D, wcols), BF), pltpu.VMEM((rp, D), F32), pltpu.VMEM((rp, cp), F32), pltpu.VMEM((PAIRS, rp, 128), BF), pltpu.VMEM((PAIRS, cp, 128), BF), pltpu.VMEM((PAIRS, cp, 128), BF),
            pltpu.SemaphoreType.DMA((2 * BLOCKS,)), pltpu.SemaphoreType.DMA((3,)),
        ],
        14, 48,
    )


def attn_fwd2(ctl, dest, tokens, segc, segr, ln, ob, q, k, v, o1, weights):
    rows, rp, cp = tokens.shape[0], segc.shape[0], segr.shape[1]
    wcols = weights[0].shape[2]
    return call(
        functools.partial(attn_fwd2_kernel, len(weights), rows, rp, cp), "attn_fwd2", (ctl, dest),
        [(tokens, None), (segc, None), (segr, None), (ln, None), (ob, None), (q, "far"), (k, "far"), (v, "far"), (o1, None)] + [(w, "hbm") for w in weights],
        [((rp, D), F32, 0), ((rp, D), BF, 0), ((HP, rp, 128), BF, 0), ((HEADS // 2, 1, cp), F32, 0)],
        [
            pltpu.VMEM((2 * D, wcols // 4), BF), pltpu.VMEM((rp, cp), F32), pltpu.VMEM((HP, rp, 128), BF), pltpu.VMEM((HP, cp, 128), BF), pltpu.VMEM((HP, cp, 128), BF),
            pltpu.SemaphoreType.DMA((2 * BLOCKS,)), pltpu.SemaphoreType.DMA((3,)),
        ],
        12,
    )


def gelu_parts(h):
    x = jnp.abs(h) * 0.7071067811865476
    t = 1.0 / (1.0 + 0.3275911 * x)
    e = jnp.exp2(h * h * (-0.5 * LOG2E))
    poly = t * (0.254829592 * 0.5 + t * (-0.284496736 * 0.5 + t * (1.421413741 * 0.5 + t * (-1.453152027 * 0.5 + t * (1.061405429 * 0.5)))))
    tail = poly * e
    phi = jnp.where(h < 0, tail, 1.0 - tail)
    return phi, phi + h * e * 0.3989422804014327


FCH = 768


def ffn_kernel(rows, rp, first, ctl, dest, slots, x1_ref, cot_ref, segc_ref, ln_ref, ub_ref, *rest):
    if first:
        nw = len(rest) - 16
        w = rest[:nw]
        (f_out, dn_out, dub_ref, keep, send, w_s, n2_s, n2t_s, dfr_s, dft_s, dy_s, stage, f_ref, dn_ref, lsem, ssem) = rest[nw:]
    else:
        attn_ref, fin_ref, dnin_ref = rest[:3]
        nw = len(rest) - 3 - 18
        w = rest[3 : 3 + nw]
        (y0_ref, y1_ref, dx1_ref, vec_ref, dub_ref, keep, send, w_s, n2_s, n2t_s, dfr_s, dft_s, dy_s, stage, f_ref, dn_ref, lsem, ssem) = rest[3 + nw :]
    copies = load_blocks(dest, w, w_s, lsem)
    core = ctl[1]
    live = (segc_ref[...] != PAD_ID).astype(F32)
    xhat, rstd = row_stats(x1_ref[...])
    n2 = (xhat * ln_ref[0:1] + ln_ref[1:2]).astype(BF)
    n2_s[...] = n2
    n2t_s[...] = n2.T
    dy_s[rows:rp, :] = jnp.zeros((rp - rows, D), F32)
    dy_s[0:rows, :] = cot_ref[...].astype(F32)
    dy = dy_s[...] * live
    dy_s[...] = dy
    df = dy * ln_ref[2:3]
    dfr = df.astype(BF)
    dfr_s[...] = dfr
    dft_s[...] = dfr.T
    if not first:
        vec_ref[2:3] = col_sum(df)
    for c in copies:
        c.wait()
    if first:
        f_ref[...] = jnp.zeros((rp, D), F32)
        dn_ref[...] = jnp.zeros((rp, D), F32)
    else:
        f_ref[...] = fin_ref[...].astype(F32)
        dn_ref[...] = dnin_ref[...].astype(F32)
    copies_of = lambda t: store_copies(core, slots, t, stage.at[t], (keep, send), pl.ds(0, 2 * FCH), ssem.at[t])

    def half_units(t, _):
        rows_t = pl.ds(pl.multiple_of(t * D, D), D)
        wu = w_s[rows_t, 0:FCH]
        wd = w_s[rows_t, FCH:]
        hid = mm(n2_s[...], wu) + ub_ref[pl.ds(t, 1)]
        phi, slope = gelu_parts(hid)
        g = (hid * phi).astype(BF)
        dh = (mm(dfr_s[...], wd) * slope).astype(BF)
        dub_ref[pl.ds(t, 1)] = col_sum(dh.astype(F32))
        stage[t, :, 0:FCH] = mm(n2t_s[...], dh).astype(BF)
        stage[t, :, FCH:] = mm(dft_s[...], g).astype(BF)
        for c in copies_of(t):
            c.start()
        f_ref[...] += mm_nt(g, wd)
        dn_ref[...] += mm_nt(dh, wu)
        return 0

    lax.fori_loop(0, 2, half_units, 0)
    pending = copies_of(0) + copies_of(1)
    if first:
        f_out[...] = f_ref[...].astype(BF)
        dn_out[...] = dn_ref[...].astype(BF)
    else:
        ffo = f_ref[...] + ln_ref[3:4]
        dy = dy_s[...]
        vec_ref[3:4] = col_sum(dy * ffo)
        y = (x1_ref[...] + ln_ref[2:3] * ffo).astype(BF)
        cut = y0_ref.shape[0]
        y0_ref[...] = y[0:cut]
        y1_ref[...] = y[cut:rows]
        dn2 = dn_ref[...]
        xhat, rstd = row_stats(x1_ref[...])
        vec_ref[0:1] = col_sum(dn2 * xhat)
        vec_ref[1:2] = col_sum(dn2)
        dx1 = dy + norm_back(xhat, rstd, dn2, ln_ref[0:1])
        dx1_ref[...] = dx1
        vec_ref[4:5] = col_sum(dx1 * ln_ref[4:5])
        vec_ref[5:6] = col_sum(dx1 * attn_ref[...].astype(F32))
        vec_ref[6:8] = jnp.zeros((2, D), F32)
    for c in pending:
        c.wait()


def ffn(first, ctl, dest, slots, x1, cotangent, segc, ln, ub, more, weights):
    rows, rp = cotangent.shape[0], x1.shape[0]
    wcols = weights[0].shape[2]
    if first:
        outs = [((rp, D), BF, 0), ((rp, D), BF, 0)]
    else:
        cut = -(-rows // 32) * 16
        outs = [((cut, D), BF, 0), ((rows - cut, D), BF, 0), ((rp, D), F32, 0), ((8, D), F32, 0)]
    outs += [((2, FCH), F32, 0)] + [((BLOCKS, BROWS, wcols), BF, 1)] * 2
    return call(
        functools.partial(ffn_kernel, rows, rp, first), "ffn_first" if first else "ffn_last", (ctl, dest, slots),
        [(x1, None), (cotangent, None), (segc, None), (ln, None), (ub, None)] + [(v, None) for v in more] + [(w, "hbm") for w in weights],
        outs,
        [
            pltpu.VMEM((2 * D, wcols), BF), pltpu.VMEM((rp, D), BF), pltpu.VMEM((D, rp), BF), pltpu.VMEM((rp, D), BF), pltpu.VMEM((D, rp), BF),
            pltpu.VMEM((rp, D), F32), pltpu.VMEM((2, D, 2 * FCH), BF),
        ]
        + [pltpu.VMEM((rp, D), F32)] * 2
        + [pltpu.SemaphoreType.DMA((2 * BLOCKS,)), pltpu.SemaphoreType.DMA((2, BLOCKS))],
        20, 56,
    )


def attn_bwd_kernel(nw, rp, cp, which, ctl, dest, dx1_ref, qh, kh, vh, lse_ref, segc_ref, segr_ref, ln_ref, *rest):
    w = rest[:nw]
    dq_ref, dk_ref, dv_ref, w_s, do_s, q_s, k_s, v_s, bias_s, sem, isem = rest[nw:]
    t = which[0]
    heads = half_heads(t, (qh, kh, vh), (q_s, k_s, v_s), isem)
    half = D // 2
    copies = load_blocks(dest, w, w_s, sem, slice(3 * half, 4 * half))
    scale = HEAD ** (-0.5)
    bias_s[...] = jnp.where(segc_ref[...] == segr_ref[...], 0.0, NEG)
    q_s[:, rp:cp, :] = jnp.zeros((HP, cp - rp, 128), BF)
    do_s[:, rp:cp, :] = jnp.zeros((HP, cp - rp, 128), BF)
    dar = (dx1_ref[...] * ln_ref[2:3]).astype(BF)
    for c in copies:
        c.wait()
    z = mm(dar, w_s[pl.ds(pl.multiple_of(t * D, D), D), :]).astype(BF)
    for i in range(HP):
        do_s[i, 0:rp, :] = z[:, i * 128 : (i + 1) * 128]
    for c in heads:
        c.wait()

    def pair(p, _):
        q2 = q_s[p]
        do2 = do_s[p]
        k2 = k_s[p]
        v2 = v_s[p]
        dq = dk = dv = None
        for h in range(2):
            m = pair_mask(h)
            km = k2 * m
            st = mm_nt(km, q2) * (scale * LOG2E) + bias_s[...]
            pt = jnp.exp2(st - lse_ref[2 * p + h])
            dpt = mm_nt(v2 * m, do2)
            delta = jnp.sum(pt * dpt, axis=0, keepdims=True)
            dst = (pt * (dpt - delta)).astype(BF)
            a = mm(pt.astype(BF), do2 * m)
            b = mm(dst, q2 * m)
            c = mm_tn(dst, km)
            dv = a if dv is None else dv + a
            dk = b if dk is None else dk + b
            dq = c if dq is None else dq + c
        dq_ref[p] = (dq[0:rp] * scale).astype(BF)
        dk_ref[p] = (dk * scale).astype(BF)
        dv_ref[p] = dv.astype(BF)
        return 0

    lax.fori_loop(0, HP, pair, 0)


def attn_bwd(t, ctl, dest, dx1, q, k, v, lse, segc, segr, ln, weights):
    rp, cp = segc.shape[0], segr.shape[1]
    wcols = weights[0].shape[2]
    return call(
        functools.partial(attn_bwd_kernel, len(weights), rp, cp), "attn_bwd", (jnp.full((1,), t, jnp.int32), ctl, dest),
        [(dx1, None), (q, "far"), (k, "far"), (v, "far")] + [(e, None) for e in (lse, segc, segr, ln)] + [(w, "hbm") for w in weights],
        [((HP, rp, 128), BF, 0)] * 3,
        [
            pltpu.VMEM((2 * D, wcols // 4), BF), pltpu.VMEM((HP, cp, 128), BF), pltpu.VMEM((HP, cp, 128), BF), pltpu.VMEM((HP, rp, 128), BF), pltpu.VMEM((HP, rp, 128), BF),
            pltpu.VMEM((rp, cp), F32), pltpu.SemaphoreType.DMA((2 * BLOCKS,)), pltpu.SemaphoreType.DMA((3,)),
        ],
        15, 52,
    )


def attn_grad_kernel(rows, rp, ctl, slots, x_ref, dx1_ref, o1_ref, o2_ref, dq1, dk1, dv1, dq2, dk2, dv2, ln_ref, keep, send, stage, x_s, ssem):
    core = ctl[1]
    half = D // 2
    x_s[0:rows, :] = x_ref[...].astype(F32)
    x_s[rows:rp, :] = jnp.zeros((rp - rows, D), F32)
    dart = (dx1_ref[...] * ln_ref[2:3]).astype(BF).T
    xhat, _ = row_stats(x_s[...])
    n1t = (xhat * ln_ref[0:1] + ln_ref[1:2]).astype(BF).T
    pend = []
    for t, (o, dz) in enumerate(((o1_ref, (dq1, dk1, dv1)), (o2_ref, (dq2, dk2, dv2)))):
        o_t = jnp.concatenate([o[i] for i in range(HP)], axis=1)
        stage[t, :, 3 * half :] = mm(dart, o_t).astype(BF)
        z = jnp.concatenate([e[i] for e in dz for i in range(HP)], axis=1)
        stage[t, :, 0 : 3 * half] = mm(n1t, z).astype(BF)
        cps = store_copies(core, slots, t, stage.at[t], (keep, send), pl.ds(0, 4 * half), ssem.at[t])
        for c in cps:
            c.start()
        pend += cps
    for c in pend:
        c.wait()


def attn_grad(ctl, slots, tokens, dx1, o1, o2, dz1, dz2, ln):
    rows, rp = tokens.shape[0], dx1.shape[0]
    wcols = 2 * D
    return call(
        functools.partial(attn_grad_kernel, rows, rp), "attn_grad", (ctl, slots),
        [(tokens, None)] + [(e, None) for e in (dx1, o1, o2, *dz1, *dz2, ln)],
        [((BLOCKS, BROWS, wcols), BF, 1)] * 2,
        [pltpu.VMEM((2, D, wcols), BF), pltpu.VMEM((rp, D), F32), pltpu.SemaphoreType.DMA((2, BLOCKS))],
        10, 48,
    )


def input_grad_kernel(nw, rows, rp, ctl, dest, x_ref, dx1_ref, dq1, dk1, dv1, dq2, dk2, dv2, ln_ref, vecf_ref, dub1_ref, dub2_ref, *rest):
    w = rest[:nw]
    dx_ref, vec_ref, w_s, x_s, sem = rest[nw:]
    half = D // 2
    copies = load_blocks(dest, w, w_s, sem, slice(0, 3 * half))
    x_s[0:rows, :] = x_ref[...].astype(F32)
    x_s[rows:rp, :] = jnp.zeros((rp - rows, D), F32)
    xhat, rstd = row_stats(x_s[...])
    for c in copies:
        c.wait()
    dn1 = None
    for t, dz in enumerate(((dq1, dk1, dv1), (dq2, dk2, dv2))):
        z = jnp.concatenate([e[i] for e in dz for i in range(HP)], axis=1)
        part = mm_nt(z, w_s[t * D : (t + 1) * D, :])
        dn1 = part if dn1 is None else dn1 + part
        vec_ref[8:9, t * half : (t + 1) * half] = col_sum(z[:, 0:half].astype(F32))
        vec_ref[9:10, t * half : (t + 1) * half] = col_sum(z[:, 2 * half :].astype(F32))
        vec_ref[10 + 2 * t : 11 + 2 * t] = dub1_ref[t : t + 1]
        vec_ref[11 + 2 * t : 12 + 2 * t] = dub2_ref[t : t + 1]
    vec_ref[0:1] = col_sum(dn1 * xhat)
    vec_ref[2:3] = col_sum(dn1)
    for i, row in enumerate((1, 3, 5, 7, 4, 6)):
        vec_ref[row : row + 1] = vecf_ref[i : i + 1]
    vec_ref[14:16] = jnp.zeros((2, D), F32)
    dx = dx1_ref[...] + norm_back(xhat, rstd, dn1, ln_ref[0:1])
    dx_ref[...] = dx[0:rows].astype(BF)


def input_grad(ctl, dest, tokens, dx1, dz1, dz2, ln, vec_f, dub1, dub2, weights):
    rows, rp = tokens.shape[0], dx1.shape[0]
    wcols = weights[0].shape[2]
    return call(
        functools.partial(input_grad_kernel, len(weights), rows, rp), "input_grad", (ctl, dest),
        [(tokens, None)] + [(e, None) for e in (dx1, *dz1, *dz2, ln, vec_f, dub1, dub2)] + [(w, "hbm") for w in weights],
        [((rows, D), BF, 0), ((16, D), F32, 0)],
        [pltpu.VMEM((2 * D, wcols * 3 // 4), BF), pltpu.VMEM((rp, D), F32), pltpu.SemaphoreType.DMA((2 * BLOCKS,))],
        10,
    )


def prepare(segment, me, ln_gain, ln_shift, qb, out_bias, layer_scale):
    rows = segment.shape[1]
    rp = -(-rows // 16) * 16
    cp = -(-rp // 128) * 128
    seg = lax.dynamic_index_in_dim(segment, me, 0, keepdims=False)
    seg = jnp.concatenate([seg, jnp.full((rp - rows,), -2, jnp.int32), jnp.full((cp - rp,), -1, jnp.int32)])
    segr = seg.reshape(1, cp)
    segc = seg[:rp].reshape(rp, 1)
    half = D // 2
    ln1 = jnp.stack([ln_gain[0], ln_shift[0], layer_scale[0]])
    ln2 = jnp.stack([ln_gain[1], ln_shift[1], layer_scale[1], out_bias[1], layer_scale[0]])
    z = jnp.zeros((2, half), F32)
    qbt = jnp.concatenate([qb[0].reshape(2, half), z, qb[1].reshape(2, half)], axis=1)
    return segc, segr, ln1, ln2, qbt, out_bias[0:1]


def swap(v, n_tensor):
    return lax.ppermute(v, "tensor", [(i, (i + 1) % n_tensor) for i in range(n_tensor)])


def after(v, *done):
    return lax.optimization_barrier((v, done))[0]


class Grid:
    axes = ("dp", "tensor")
    places = [(z, y, c, t) for z in range(4) for y in range(2) for c in range(2) for t in range(2)]

    def number(self, p):
        return ((p[0] * 2 + p[1]) * 2 + p[2]) * 2 + p[3]

    def x(self, p):
        return p[0], p[1], p[2], 1 - p[3]

    def y(self, p):
        return p[0], 1 - p[1], p[2], p[3]

    def core(self, p):
        return p[0], p[1], 1 - p[2], p[3]

    def first(self, p):
        return self.y(p) if p[2] else self.x(p)

    def second(self, p):
        return self.x(p) if p[2] else self.y(p)

    def z1(self, p):
        return p[0] ^ 1, p[1], p[2], p[3]

    def z2(self, p):
        return p[0] ^ 2, p[1], p[2], p[3]

    def z3(self, p):
        return p[0] ^ 3, p[1], p[2], p[3]

    def along(self, v):
        return [self.send(e, to) for e, to in zip(v, (self.z1, self.z2, self.z3))]

    def send(self, v, to):
        return lax.ppermute(v, self.axes, [(self.number(p), self.number(to(p))) for p in self.places])

    def line(self, p):
        return [(p[0] ^ k, p[1], p[2], p[3]) for k in range(4)]

    def held(self, p, first, second):
        b = second(p)
        return self.line(p) + self.line(first(p)) + self.line(b) + self.line(first(b))

    def tables(self):
        where = lambda q: q[3] * BLOCKS + (q[0] * 2 + q[1]) * 2 + q[2]
        half = BLOCKS // 2
        rows = []
        for p in self.places:
            row = [where(q) for e in (p, self.core(p)) for q in self.held(e, self.first, self.second)]
            for route in ((self.first, self.second), (self.x, self.y)):
                at = {where(q): i for e in (p, self.core(p)) for i, q in enumerate(self.held(e, *route))}
                row += [at[t * BLOCKS + 2 * m + p[2]] for t in range(2) for m in range(half)]
                row += [at[t * BLOCKS + 2 * m + 1 - p[2]] for t in range(2) for m in range(half)]
            rows.append(row)
        return jnp.array(rows, jnp.int32)


def wide(v):
    return v.astype(F32)


class Reduce:
    def __init__(self, net, keep, sent, first, second):
        self.net, self.terms, self.sent, self.first, self.second = net, [keep], sent, first, second
        self.stage = 0
        self.got = net.send(sent, net.core)

    def total(self, at):
        return sum(wide(e[at]) for e in self.terms)

    def start(self, *dep):
        self.stage += 1
        n = self.stage
        self.terms.append(after(self.got, *dep))
        if n < 3:
            self.sent = self.total(slice(BLOCKS >> n, 2 * BLOCKS >> n)).astype(BF)
            self.got = self.net.send(self.sent, self.second if n == 1 else self.first)
        else:
            self.sent = [self.total(k).astype(BF) for k in (1, 2, 3)]
            self.got = self.net.along(self.sent)

    def result(self, *dep):
        return self.total(0) + sum(wide(e) for e in after(self.got, *dep))


class Plain:
    def __init__(self, n_tensor):
        self.n_tensor = n_tensor

    def gather(self, w):
        me = lax.axis_index("tensor")
        other = swap(w, self.n_tensor)
        both = jnp.where(me == 0, jnp.stack([w, other]), jnp.stack([other, w]))
        full = lax.all_gather(both, "dp", axis=1, tiled=True)
        return [full.reshape(2 * BLOCKS, BROWS, w.shape[1])]

    def settle(self, keep, sent):
        me = lax.axis_index("tensor")
        h = BLOCKS // 2
        g = jnp.stack([keep.reshape(2, h, BROWS, -1), sent.reshape(2, h, BROWS, -1)], axis=2).reshape(2, D, -1)
        part = lax.psum_scatter(g, "dp", scatter_dimension=1, tiled=True).astype(F32)
        return jnp.where(me == 0, part[0], part[1]) + swap(jnp.where(me == 0, part[1], part[0]), self.n_tensor)

    def total(self, v):
        return lax.psum(v, ("dp", "tensor"))


def make_on_device(n_dp, n_tensor):
    def on_device(
        tokens, segment, cotangent, ln_gain, ln_shift, qkv_weight, qv_bias, out_weight,
        out_bias, layer_scale, up_weight, up_bias, down_weight,
    ):
        me = lax.axis_index("tensor")
        own_first = lambda own, other, axis=0: jnp.where(me == 0, jnp.stack([own, other], axis), jnp.stack([other, own], axis))
        both = lambda own, other: own_first(own, other, 1).transpose(1, 0, 2)
        half = D // 2
        hid_half = up_weight.shape[1]
        wa = jnp.concatenate([qkv_weight[0], qkv_weight[1], qkv_weight[2], out_weight.T], axis=1)
        small = jnp.concatenate([qv_bias.reshape(-1), up_bias])

        def pack_ffn(up, down):
            down_t = down.T
            return [jnp.concatenate([up[:, lo : lo + FCH], down_t[:, lo : lo + FCH]], axis=1) for lo in range(0, hid_half, FCH)]

        def consts(small, segment):
            small = own_first(small, swap(small, n_tensor))
            qb = small[:, : 2 * half].reshape(2, 2, half).transpose(1, 0, 2).reshape(2, D)
            ub = small[:, 2 * half :]
            return (ub[:, :FCH], ub[:, FCH:]) + prepare(segment, me, ln_gain, ln_shift, qb, out_bias, layer_scale)

        def results(out, dxs, vec, ga, gup, gdown):
            qv = lax.dynamic_slice(vec, (8, me * half), (2, half))
            dubs = lax.dynamic_slice(vec, (10 + 2 * me, 0), (2, D)).reshape(hid_half)
            return (
                out, dxs, vec[0:2], vec[2:4],
                jnp.stack([ga[:, i * half : (i + 1) * half] for i in range(3)]),
                qv, ga[:, 3 * half :].T, vec[4:6], vec[6:8],
                gup, dubs, gdown.T,
            )

        pick = lambda v: lax.dynamic_index_in_dim(v, me, 0, keepdims=False)
        if n_dp != 16 or n_tensor != 2:
            tokens, cotangent = pick(tokens), pick(cotangent)
            net = Plain(n_tensor)
            dest = jnp.arange(2 * BLOCKS, dtype=jnp.int32)
            slots = jnp.concatenate([jnp.arange(BLOCKS, dtype=jnp.int32)] * 2)
            ctl = jnp.stack([me, 0]).astype(jnp.int32)
            wa = net.gather(wa)
            wf = [net.gather(w) for w in pack_ffn(up_weight, down_weight)]
            ub1, ub2, segc, segr, ln1, ln2, qbt, ob0 = consts(small, segment)
            q, k, v, o1, lse1 = attn_fwd1(ctl, dest, tokens, segc, segr, ln1, qbt, wa)
            x1, attn, o2, lse2 = attn_fwd2(ctl, dest, tokens, segc, segr, ln1, ob0, q, k, v, o1, wa)
            f, dn, dub1, k1, s1 = ffn(True, ctl, dest, slots, x1, cotangent, segc, ln2, ub1, (), wf[0])
            y0, y1, dx1, vec_f, dub2, k2, s2 = ffn(False, ctl, dest, slots, x1, cotangent, segc, ln2, ub2, (attn, f, dn), wf[1])
            dz1 = attn_bwd(0, ctl, dest, dx1, q, k, v, lse1, segc, segr, ln1, wa)
            dz2 = attn_bwd(1, ctl, dest, dx1, q, k, v, lse2, segc, segr, ln1, wa)
            ka, sa = attn_grad(ctl, slots, tokens, dx1, o1, o2, dz1, dz2, ln1)
            dx, vec = input_grad(ctl, dest, tokens, dx1, dz1, dz2, ln1, vec_f, dub1, dub2, wa)
            gf1, gf2, ga = net.settle(k1, s1), net.settle(k2, s2), net.settle(ka, sa)
            vec = net.total(vec)
            gup = jnp.concatenate([gf1[:, :FCH], gf2[:, :FCH]], axis=1)
            gdown = jnp.concatenate([gf1[:, FCH:], gf2[:, FCH:]], axis=1)
            y = jnp.concatenate([y0, y1])
            return results(both(y, swap(y, n_tensor)), both(dx, swap(dx, n_tensor)), vec, ga, gup, gdown)

        net = Grid()
        place = lax.axis_index("dp") * 2 + me
        bs = net.along([wa] * 3)
        tokens, cotangent, segment, small, place = after((tokens, cotangent, segment, small, place), wa)
        tokens, cotangent = pick(tokens), pick(cotangent)
        ub1, ub2, segc, segr, ln1, ln2, qbt, ob0 = consts(small, segment)
        table = lax.dynamic_index_in_dim(net.tables(), place, 0, keepdims=False)
        bs = after(bs, tokens, cotangent, segc, table)
        s = after(jnp.stack([wa, *bs]))
        fs, es = pack_ffn(*after((up_weight, down_weight), s))
        ra = net.send(s, net.first)
        fz = net.along([after(fs, s)] * 3)
        dest, slots, slots_f = (table[i : i + 2 * BLOCKS] for i in range(0, 6 * BLOCKS, 2 * BLOCKS))
        ctl = jnp.stack([me, lax.axis_index("dp") % 2]).astype(jnp.int32)
        ra = after(ra, dest, qbt)
        s = jnp.concatenate([s, ra])
        r = net.send(s, net.second)
        sc = net.send(s, net.core)
        fz = after(fz, s)
        fs = after(jnp.stack([fs, *fz]))
        ez = net.along([after(es, fs)] * 3)
        r = after(r, sc, fs)
        rc = net.send(r, net.core)
        fs = after(fs, r)
        fr = net.send(fs, net.first)
        fr = after(fr, rc)
        fs = jnp.concatenate([fs, fr])
        r1 = net.send(fs, net.second)
        c1 = net.send(fs, net.core)
        wa = after([s, r, sc, rc], fs)
        q, k, v, o1, lse1 = attn_fwd1(ctl, dest, tokens, segc, segr, ln1, qbt, wa)
        r1, c1, ez = after((r1, c1, ez), o1)
        w1 = [fs, r1, c1, net.send(r1, net.core)]
        es = after(jnp.stack([es, *ez]), r1)
        er = net.send(es, net.first)
        q = after(q, es, r1)
        x1, attn, o2, lse2 = attn_fwd2(ctl, dest, tokens, segc, segr, ln1, ob0, q, k, v, o1, wa)
        w1, er = after((w1, er), x1)
        es = jnp.concatenate([es, er])
        r2 = net.send(es, net.second)
        c2 = net.send(es, net.core)
        w1 = after(w1, es)
        f, dn, dub1, k1, s1 = ffn(True, ctl, dest, slots, x1, cotangent, segc, ln2, ub1, (), w1)
        r2, c2 = after((r2, c2), f)
        w2 = [es, r2, c2, net.send(r2, net.core)]
        g1 = Reduce(net, k1, s1, net.first, net.second)
        y0, y1, dx1, vec_f, dub2, k2, s2 = ffn(False, ctl, dest, slots_f, x1, cotangent, segc, ln2, ub2, (attn, f, dn), w2)
        g2 = Reduce(net, k2, s2, net.x, net.y)
        g1.start(dx1)
        dx1 = after(dx1, g1.sent)
        dz1 = attn_bwd(0, ctl, dest, dx1, q, k, v, lse1, segc, segr, ln1, wa)
        g1.start(dz1[0])
        g2.start(dz1[0], g1.sent)
        z0 = swap(after(y0, g2.sent), n_tensor)
        dx1 = after(dx1, dz1[0], g1.sent, g2.sent)
        dz2 = attn_bwd(1, ctl, dest, dx1, q, k, v, lse2, segc, segr, ln1, wa)
        z1 = swap(after(y1, dz2[0]), n_tensor)
        dx1 = after(dx1, dz2[0], z0)
        ka, sa = attn_grad(ctl, slots, tokens, dx1, o1, o2, dz1, dz2, ln1)
        g = Reduce(net, ka, sa, net.first, net.second)
        g1.start(ka)
        g2.start(ka)
        dx1 = after(dx1, ka, g1.sent, g2.sent, z1)
        dx, vec = input_grad(ctl, dest, tokens, dx1, dz1, dz2, ln1, vec_f, dub1, dub2, wa)
        def add(v, to, *dep):
            v = after(v, *dep)
            return v + net.send(v, to)

        g.start(dx)
        vec = add(add(vec, net.z1, g.sent), net.z2)
        g2.start(g.sent, vec)
        vec = add(vec, net.first)
        y0, y1, z0, z1 = after((y0, y1, z0, z1), g.sent)
        out = both(jnp.concatenate([y0, y1]), jnp.concatenate([z0, z1]))
        gf1 = g1.result(g.sent)
        g.start(g2.sent, gf1, out, vec)
        vec = add(vec, net.second, g.sent)
        dx_other = swap(after(dx, vec), n_tensor)
        g.start(vec)
        gf2 = g2.result(g.sent)
        vec = add(vec, net.core, g.sent)
        gup = jnp.concatenate([gf1[:, :FCH], gf2[:, :FCH]], axis=1)
        gdown = jnp.concatenate([gf1[:, FCH:], gf2[:, FCH:]], axis=1)
        dxs = both(dx, dx_other)
        return results(out, dxs, vec, g.result(), gup, gdown)

    return on_device


def solution(mesh):
    rows = P(None, "dp", None)
    wt = P("tensor", "dp")
    return jax.shard_map(
        make_on_device(mesh.shape["dp"], mesh.shape["tensor"]),
        mesh=mesh,
        in_specs=(
            rows, P(None, "dp"), rows, P(), P(), P(None, "dp", "tensor"), P(None, "tensor"), wt,
            P(), P(), P("dp", "tensor"), P("tensor"), wt,
        ),
        out_specs=(
            rows, rows, P(), P(), P(None, "dp", "tensor"), P(None, "tensor"), wt,
            P(), P(), P("dp", "tensor"), P("tensor"), wt,
        ),
        check_vma=False,
    )
```

```python
import functools

import jax
import jax.numpy as jnp
from jax import lax
from jax.experimental import pallas as pl
from jax.experimental.pallas import tpu as pltpu
from jax.sharding import PartitionSpec as P

D = 768
HEADS = 12
HEAD = D // HEADS
EPS = 1e-06
PAD_ID = 3
NEG = -1e30
BF = jnp.bfloat16
F32 = jnp.float32
LOG2E = 1.4426950408889634

BLOCKS = 16
BROWS = D // BLOCKS


def mm(a, b):
    return jnp.dot(a, b, preferred_element_type=F32)


def mm_nt(a, b):
    return lax.dot_general(a, b, (((1,), (1,)), ((), ())), preferred_element_type=F32)


def mm_tn(a, b):
    return lax.dot_general(a, b, (((0,), (0,)), ((), ())), preferred_element_type=F32)


def row_stats(v):
    mean = jnp.mean(v, axis=-1, keepdims=True)
    c = v - mean
    rstd = lax.rsqrt(jnp.mean(c * c, axis=-1, keepdims=True) + EPS)
    return c * rstd, rstd


def norm_back(xhat, rstd, dn, gain):
    dxh = dn * gain
    m1 = jnp.mean(dxh, axis=-1, keepdims=True)
    m2 = jnp.mean(dxh * xhat, axis=-1, keepdims=True)
    return rstd * (dxh - m1 - xhat * m2)


def col_sum(v):
    return jnp.sum(v, axis=0, keepdims=True)


def load_blocks(dest, parts, dst, sem, cols=slice(None)):
    copies = []
    n = 0
    for part in parts:
        for j in range(part.shape[0]):
            row = pl.multiple_of(dest[n] * BROWS, BROWS)
            copies.append(pltpu.make_async_copy(part.at[j, :, cols], dst.at[pl.ds(row, BROWS)], sem.at[n]))
            n += 1
    for c in copies:
        c.start()
    return copies


def store_copies(core, slots, t, stage, outs, cols, sem):
    keep, send = outs
    copies = []
    half = BLOCKS // 2
    for m in range(half):
        a = pl.multiple_of((2 * m + core) * BROWS, BROWS)
        b = pl.multiple_of((2 * m + 1 - core) * BROWS, BROWS)
        copies.append(pltpu.make_async_copy(stage.at[pl.ds(a, BROWS)], keep.at[slots[t * half + m], :, cols], sem.at[2 * m]))
        copies.append(pltpu.make_async_copy(stage.at[pl.ds(b, BROWS)], send.at[slots[BLOCKS + t * half + m], :, cols], sem.at[2 * m + 1]))
    return copies


def pair_mask(h, dtype=BF):
    lane = lax.broadcasted_iota(jnp.int32, (1, 2 * HEAD), 1)
    return (lane // HEAD == h).astype(dtype)


def call(kernel, name, scalars, ins, outs, scratch, us, vmem=32):
    spaces = {None: pltpu.VMEM, 0: pltpu.VMEM, 1: pl.ANY, "hbm": pl.ANY, "far": pltpu.HBM}
    at = lambda how: pl.BlockSpec(memory_space=spaces[how])
    return pl.pallas_call(
        kernel,
        in_specs=[pl.BlockSpec(memory_space=pltpu.SMEM)] * len(scalars) + [at(how) for _, how in ins],
        out_specs=[at(how) for _, _, how in outs],
        out_shape=[jax.ShapeDtypeStruct(shape, dtype) for shape, dtype, _ in outs],
        scratch_shapes=scratch,
        compiler_params=pltpu.CompilerParams(vmem_limit_bytes=vmem * 1024 * 1024),
        cost_estimate=pl.CostEstimate(flops=us * 5_000_000_000, bytes_accessed=us * 1_000_000, transcendentals=0),
        name=name,
    )(*scalars, *[v for v, _ in ins])


PAIRS = HEADS // 2
HP = PAIRS // 2


def fwd_pairs(q_ref, k_ref, v_ref, bias_s, o_ref, lse_ref):
    scale = (HEAD ** (-0.5)) * LOG2E

    def pair(p, _):
        q2 = q_ref[p]
        k2 = k_ref[p]
        v2 = v_ref[p]
        acc = None
        for h in range(2):
            m = pair_mask(h)
            s = mm_nt(q2, k2 * m) * scale + bias_s[...]
            top = jnp.max(s, axis=-1, keepdims=True)
            e = jnp.exp2(s - top)
            tot = jnp.sum(e, axis=-1, keepdims=True)
            oh = mm(e.astype(BF), v2 * m) * (1.0 / tot)
            acc = oh if acc is None else acc + oh
            lse_ref[2 * p + h, :, 0 : top.shape[0]] = (top + jnp.log2(tot)).reshape(1, -1)
        o_ref[p] = acc.astype(BF)
        return 0

    lse_ref[...] = jnp.zeros_like(lse_ref)
    lax.fori_loop(0, HP, pair, 0)


def half_heads(t, src, dst, sem):
    copies = []
    for i, (a, b) in enumerate(zip(src, dst)):
        n = min(a.shape[1], b.shape[1])
        copies.append(pltpu.make_async_copy(a.at[pl.ds(HP * t, HP), 0:n], b.at[:, 0:n], sem.at[i]))
    for c in copies:
        c.start()
    return copies


def attn_fwd1_kernel(nw, rows, rp, cp, ctl, dest, x_ref, segc_ref, segr_ref, ln_ref, qb_ref, *rest):
    w = rest[:nw]
    qh, kh, vh, o_ref, lse_ref, w_s, x_s, bias_s, q_ref, k_ref, v_ref, sem, osem = rest[nw:]
    copies = load_blocks(dest, w, w_s, sem)
    x_s[0:rows, :] = x_ref[...].astype(F32)
    x_s[rows:rp, :] = jnp.zeros((rp - rows, D), F32)
    bias_s[...] = jnp.where(segc_ref[...] == segr_ref[...], 0.0, NEG)
    xhat, _ = row_stats(x_s[...])
    n1 = (xhat * ln_ref[0:1] + ln_ref[1:2]).astype(BF)
    for c in copies:
        c.wait()
    half = D // 2
    k_ref[:, rp:cp, :] = jnp.zeros((PAIRS, cp - rp, 128), BF)
    v_ref[:, rp:cp, :] = jnp.zeros((PAIRS, cp - rp, 128), BF)
    x_s[...] = n1.astype(F32)

    def project(t, _):
        z = mm(x_s[...].astype(BF), w_s[pl.ds(pl.multiple_of(t * D, D), D), 0 : 3 * half]) + qb_ref[pl.ds(t, 1)]
        z = z.astype(BF)
        for i in range(HP):
            q_ref[HP * t + i] = z[:, i * 128 : (i + 1) * 128]
            k_ref[HP * t + i, 0:rp, :] = z[:, half + i * 128 : half + (i + 1) * 128]
            v_ref[HP * t + i, 0:rp, :] = z[:, 2 * half + i * 128 : 2 * half + (i + 1) * 128]
        return 0

    lax.fori_loop(0, 2, project, 0)
    out = [pltpu.make_async_copy(a, b, osem.at[i]) for i, (a, b) in enumerate(((q_ref, qh), (k_ref, kh), (v_ref, vh)))]
    for c in out:
        c.start()
    fwd_pairs(q_ref, k_ref, v_ref, bias_s, o_ref, lse_ref)
    for c in out:
        c.wait()


def attn_fwd2_kernel(nw, rows, rp, cp, ctl, dest, x_ref, segc_ref, segr_ref, ln_ref, ob_ref, qh, kh, vh, o1_ref, *rest):
    w = rest[:nw]
    x1_ref, attn_ref, o_ref, lse_ref, w_s, bias_s, q_s, k_s, v_s, sem, isem = rest[nw:]
    heads = half_heads(1, (qh, kh, vh), (q_s, k_s, v_s), isem)
    half = D // 2
    copies = load_blocks(dest, w, w_s, sem, slice(3 * half, 4 * half))
    bias_s[...] = jnp.where(segc_ref[...] == segr_ref[...], 0.0, NEG)
    for c in heads:
        c.wait()
    fwd_pairs(q_s, k_s, v_s, bias_s, o_ref, lse_ref)
    for c in copies:
        c.wait()
    a = ob_ref[0:1]
    for t, src in enumerate((o1_ref, o_ref)):
        o_t = jnp.concatenate([src[i] for i in range(HP)], axis=1)
        a = a + mm_nt(o_t, w_s[t * D : (t + 1) * D, :]).astype(BF).astype(F32)
    attn_ref[...] = a.astype(BF)
    x1_ref[...] = ln_ref[2:3] * a
    x1_ref[0:rows, :] += x_ref[...].astype(F32)


def attn_fwd1(ctl, dest, tokens, segc, segr, ln, qb, weights):
    rows, rp, cp = tokens.shape[0], segc.shape[0], segr.shape[1]
    wcols = weights[0].shape[2]
    return call(
        functools.partial(attn_fwd1_kernel, len(weights), rows, rp, cp), "attn_fwd1", (ctl, dest),
        [(tokens, None), (segc, None), (segr, None), (ln, None), (qb, None)] + [(w, "hbm") for w in weights],
        [((PAIRS, rp, 128), BF, "far"), ((PAIRS, cp, 128), BF, "far"), ((PAIRS, cp, 128), BF, "far"), ((HP, rp, 128), BF, 0), ((HEADS // 2, 1, cp), F32, 0)],
        [
            pltpu.VMEM((2 * D, wcols), BF), pltpu.VMEM((rp, D), F32), pltpu.VMEM((rp, cp), F32), pltpu.VMEM((PAIRS, rp, 128), BF), pltpu.VMEM((PAIRS, cp, 128), BF), pltpu.VMEM((PAIRS, cp, 128), BF),
            pltpu.SemaphoreType.DMA((2 * BLOCKS,)), pltpu.SemaphoreType.DMA((3,)),
        ],
        14, 48,
    )


def attn_fwd2(ctl, dest, tokens, segc, segr, ln, ob, q, k, v, o1, weights):
    rows, rp, cp = tokens.shape[0], segc.shape[0], segr.shape[1]
    wcols = weights[0].shape[2]
    return call(
        functools.partial(attn_fwd2_kernel, len(weights), rows, rp, cp), "attn_fwd2", (ctl, dest),
        [(tokens, None), (segc, None), (segr, None), (ln, None), (ob, None), (q, "far"), (k, "far"), (v, "far"), (o1, None)] + [(w, "hbm") for w in weights],
        [((rp, D), F32, 0), ((rp, D), BF, 0), ((HP, rp, 128), BF, 0), ((HEADS // 2, 1, cp), F32, 0)],
        [
            pltpu.VMEM((2 * D, wcols // 4), BF), pltpu.VMEM((rp, cp), F32), pltpu.VMEM((HP, rp, 128), BF), pltpu.VMEM((HP, cp, 128), BF), pltpu.VMEM((HP, cp, 128), BF),
            pltpu.SemaphoreType.DMA((2 * BLOCKS,)), pltpu.SemaphoreType.DMA((3,)),
        ],
        12,
    )


def gelu_parts(h):
    x = jnp.abs(h) * 0.7071067811865476
    t = 1.0 / (1.0 + 0.3275911 * x)
    e = jnp.exp2(h * h * (-0.5 * LOG2E))
    poly = t * (0.254829592 * 0.5 + t * (-0.284496736 * 0.5 + t * (1.421413741 * 0.5 + t * (-1.453152027 * 0.5 + t * (1.061405429 * 0.5)))))
    tail = poly * e
    phi = jnp.where(h < 0, tail, 1.0 - tail)
    return phi, phi + h * e * 0.3989422804014327


FCH = 768


def ffn_kernel(rows, rp, first, ctl, dest, slots, x1_ref, cot_ref, segc_ref, ln_ref, ub_ref, *rest):
    if first:
        nw = len(rest) - 16
        w = rest[:nw]
        (f_out, dn_out, dub_ref, keep, send, w_s, n2_s, n2t_s, dfr_s, dft_s, dy_s, stage, f_ref, dn_ref, lsem, ssem) = rest[nw:]
    else:
        attn_ref, fin_ref, dnin_ref = rest[:3]
        nw = len(rest) - 3 - 18
        w = rest[3 : 3 + nw]
        (y0_ref, y1_ref, dx1_ref, vec_ref, dub_ref, keep, send, w_s, n2_s, n2t_s, dfr_s, dft_s, dy_s, stage, f_ref, dn_ref, lsem, ssem) = rest[3 + nw :]
    copies = load_blocks(dest, w, w_s, lsem)
    core = ctl[1]
    live = (segc_ref[...] != PAD_ID).astype(F32)
    xhat, rstd = row_stats(x1_ref[...])
    n2 = (xhat * ln_ref[0:1] + ln_ref[1:2]).astype(BF)
    n2_s[...] = n2
    n2t_s[...] = n2.T
    dy_s[rows:rp, :] = jnp.zeros((rp - rows, D), F32)
    dy_s[0:rows, :] = cot_ref[...].astype(F32)
    dy = dy_s[...] * live
    dy_s[...] = dy
    df = dy * ln_ref[2:3]
    dfr = df.astype(BF)
    dfr_s[...] = dfr
    dft_s[...] = dfr.T
    if not first:
        vec_ref[2:3] = col_sum(df)
    for c in copies:
        c.wait()
    if first:
        f_ref[...] = jnp.zeros((rp, D), F32)
        dn_ref[...] = jnp.zeros((rp, D), F32)
    else:
        f_ref[...] = fin_ref[...].astype(F32)
        dn_ref[...] = dnin_ref[...].astype(F32)
    copies_of = lambda t: store_copies(core, slots, t, stage.at[t], (keep, send), pl.ds(0, 2 * FCH), ssem.at[t])

    def half_units(t, _):
        rows_t = pl.ds(pl.multiple_of(t * D, D), D)
        wu = w_s[rows_t, 0:FCH]
        wd = w_s[rows_t, FCH:]
        hid = mm(n2_s[...], wu) + ub_ref[pl.ds(t, 1)]
        phi, slope = gelu_parts(hid)
        g = (hid * phi).astype(BF)
        dh = (mm(dfr_s[...], wd) * slope).astype(BF)
        dub_ref[pl.ds(t, 1)] = col_sum(dh.astype(F32))
        stage[t, :, 0:FCH] = mm(n2t_s[...], dh).astype(BF)
        stage[t, :, FCH:] = mm(dft_s[...], g).astype(BF)
        for c in copies_of(t):
            c.start()
        f_ref[...] += mm_nt(g, wd)
        dn_ref[...] += mm_nt(dh, wu)
        return 0

    lax.fori_loop(0, 2, half_units, 0)
    pending = copies_of(0) + copies_of(1)
    if first:
        f_out[...] = f_ref[...].astype(BF)
        dn_out[...] = dn_ref[...].astype(BF)
    else:
        ffo = f_ref[...] + ln_ref[3:4]
        dy = dy_s[...]
        vec_ref[3:4] = col_sum(dy * ffo)
        y = (x1_ref[...] + ln_ref[2:3] * ffo).astype(BF)
        cut = y0_ref.shape[0]
        y0_ref[...] = y[0:cut]
        y1_ref[...] = y[cut:rows]
        dn2 = dn_ref[...]
        xhat, rstd = row_stats(x1_ref[...])
        vec_ref[0:1] = col_sum(dn2 * xhat)
        vec_ref[1:2] = col_sum(dn2)
        dx1 = dy + norm_back(xhat, rstd, dn2, ln_ref[0:1])
        dx1_ref[...] = dx1
        vec_ref[4:5] = col_sum(dx1 * ln_ref[4:5])
        vec_ref[5:6] = col_sum(dx1 * attn_ref[...].astype(F32))
        vec_ref[6:8] = jnp.zeros((2, D), F32)
    for c in pending:
        c.wait()


def ffn(first, ctl, dest, slots, x1, cotangent, segc, ln, ub, more, weights):
    rows, rp = cotangent.shape[0], x1.shape[0]
    wcols = weights[0].shape[2]
    if first:
        outs = [((rp, D), BF, 0), ((rp, D), BF, 0)]
    else:
        cut = -(-rows // 32) * 16
        outs = [((cut, D), BF, 0), ((rows - cut, D), BF, 0), ((rp, D), F32, 0), ((8, D), F32, 0)]
    outs += [((2, FCH), F32, 0)] + [((BLOCKS, BROWS, wcols), BF, 1)] * 2
    return call(
        functools.partial(ffn_kernel, rows, rp, first), "ffn_first" if first else "ffn_last", (ctl, dest, slots),
        [(x1, None), (cotangent, None), (segc, None), (ln, None), (ub, None)] + [(v, None) for v in more] + [(w, "hbm") for w in weights],
        outs,
        [
            pltpu.VMEM((2 * D, wcols), BF), pltpu.VMEM((rp, D), BF), pltpu.VMEM((D, rp), BF), pltpu.VMEM((rp, D), BF), pltpu.VMEM((D, rp), BF),
            pltpu.VMEM((rp, D), F32), pltpu.VMEM((2, D, 2 * FCH), BF),
        ]
        + [pltpu.VMEM((rp, D), F32)] * 2
        + [pltpu.SemaphoreType.DMA((2 * BLOCKS,)), pltpu.SemaphoreType.DMA((2, BLOCKS))],
        20, 56,
    )


def attn_bwd_kernel(nw, rp, cp, which, ctl, dest, dx1_ref, qh, kh, vh, lse_ref, segc_ref, segr_ref, ln_ref, *rest):
    w = rest[:nw]
    dq_ref, dk_ref, dv_ref, w_s, do_s, q_s, k_s, v_s, bias_s, sem, isem = rest[nw:]
    t = which[0]
    heads = half_heads(t, (qh, kh, vh), (q_s, k_s, v_s), isem)
    half = D // 2
    copies = load_blocks(dest, w, w_s, sem, slice(3 * half, 4 * half))
    scale = HEAD ** (-0.5)
    bias_s[...] = jnp.where(segc_ref[...] == segr_ref[...], 0.0, NEG)
    q_s[:, rp:cp, :] = jnp.zeros((HP, cp - rp, 128), BF)
    do_s[:, rp:cp, :] = jnp.zeros((HP, cp - rp, 128), BF)
    dar = (dx1_ref[...] * ln_ref[2:3]).astype(BF)
    for c in copies:
        c.wait()
    z = mm(dar, w_s[pl.ds(pl.multiple_of(t * D, D), D), :]).astype(BF)
    for i in range(HP):
        do_s[i, 0:rp, :] = z[:, i * 128 : (i + 1) * 128]
    for c in heads:
        c.wait()

    def pair(p, _):
        q2 = q_s[p]
        do2 = do_s[p]
        k2 = k_s[p]
        v2 = v_s[p]
        dq = dk = dv = None
        for h in range(2):
            m = pair_mask(h)
            km = k2 * m
            st = mm_nt(km, q2) * (scale * LOG2E) + bias_s[...]
            pt = jnp.exp2(st - lse_ref[2 * p + h])
            dpt = mm_nt(v2 * m, do2)
            delta = jnp.sum(pt * dpt, axis=0, keepdims=True)
            dst = (pt * (dpt - delta)).astype(BF)
            a = mm(pt.astype(BF), do2 * m)
            b = mm(dst, q2 * m)
            c = mm_tn(dst, km)
            dv = a if dv is None else dv + a
            dk = b if dk is None else dk + b
            dq = c if dq is None else dq + c
        dq_ref[p] = (dq[0:rp] * scale).astype(BF)
        dk_ref[p] = (dk * scale).astype(BF)
        dv_ref[p] = dv.astype(BF)
        return 0

    lax.fori_loop(0, HP, pair, 0)


def attn_bwd(t, ctl, dest, dx1, q, k, v, lse, segc, segr, ln, weights):
    rp, cp = segc.shape[0], segr.shape[1]
    wcols = weights[0].shape[2]
    return call(
        functools.partial(attn_bwd_kernel, len(weights), rp, cp), "attn_bwd", (jnp.full((1,), t, jnp.int32), ctl, dest),
        [(dx1, None), (q, "far"), (k, "far"), (v, "far")] + [(e, None) for e in (lse, segc, segr, ln)] + [(w, "hbm") for w in weights],
        [((HP, rp, 128), BF, 0)] * 3,
        [
            pltpu.VMEM((2 * D, wcols // 4), BF), pltpu.VMEM((HP, cp, 128), BF), pltpu.VMEM((HP, cp, 128), BF), pltpu.VMEM((HP, rp, 128), BF), pltpu.VMEM((HP, rp, 128), BF),
            pltpu.VMEM((rp, cp), F32), pltpu.SemaphoreType.DMA((2 * BLOCKS,)), pltpu.SemaphoreType.DMA((3,)),
        ],
        15, 52,
    )


def attn_grad_kernel(rows, rp, ctl, slots, x_ref, dx1_ref, o1_ref, o2_ref, dq1, dk1, dv1, dq2, dk2, dv2, ln_ref, keep, send, stage, x_s, ssem):
    core = ctl[1]
    half = D // 2
    x_s[0:rows, :] = x_ref[...].astype(F32)
    x_s[rows:rp, :] = jnp.zeros((rp - rows, D), F32)
    dart = (dx1_ref[...] * ln_ref[2:3]).astype(BF).T
    xhat, _ = row_stats(x_s[...])
    n1t = (xhat * ln_ref[0:1] + ln_ref[1:2]).astype(BF).T
    pend = []
    for t, (o, dz) in enumerate(((o1_ref, (dq1, dk1, dv1)), (o2_ref, (dq2, dk2, dv2)))):
        o_t = jnp.concatenate([o[i] for i in range(HP)], axis=1)
        stage[t, :, 3 * half :] = mm(dart, o_t).astype(BF)
        z = jnp.concatenate([e[i] for e in dz for i in range(HP)], axis=1)
        stage[t, :, 0 : 3 * half] = mm(n1t, z).astype(BF)
        cps = store_copies(core, slots, t, stage.at[t], (keep, send), pl.ds(0, 4 * half), ssem.at[t])
        for c in cps:
            c.start()
        pend += cps
    for c in pend:
        c.wait()


def attn_grad(ctl, slots, tokens, dx1, o1, o2, dz1, dz2, ln):
    rows, rp = tokens.shape[0], dx1.shape[0]
    wcols = 2 * D
    return call(
        functools.partial(attn_grad_kernel, rows, rp), "attn_grad", (ctl, slots),
        [(tokens, None)] + [(e, None) for e in (dx1, o1, o2, *dz1, *dz2, ln)],
        [((BLOCKS, BROWS, wcols), BF, 1)] * 2,
        [pltpu.VMEM((2, D, wcols), BF), pltpu.VMEM((rp, D), F32), pltpu.SemaphoreType.DMA((2, BLOCKS))],
        10, 48,
    )


def input_grad_kernel(nw, rows, rp, ctl, dest, x_ref, dx1_ref, dq1, dk1, dv1, dq2, dk2, dv2, ln_ref, vecf_ref, dub1_ref, dub2_ref, *rest):
    w = rest[:nw]
    dx_ref, vec_ref, w_s, x_s, sem = rest[nw:]
    half = D // 2
    copies = load_blocks(dest, w, w_s, sem, slice(0, 3 * half))
    x_s[0:rows, :] = x_ref[...].astype(F32)
    x_s[rows:rp, :] = jnp.zeros((rp - rows, D), F32)
    xhat, rstd = row_stats(x_s[...])
    for c in copies:
        c.wait()
    dn1 = None
    for t, dz in enumerate(((dq1, dk1, dv1), (dq2, dk2, dv2))):
        z = jnp.concatenate([e[i] for e in dz for i in range(HP)], axis=1)
        part = mm_nt(z, w_s[t * D : (t + 1) * D, :])
        dn1 = part if dn1 is None else dn1 + part
        vec_ref[8:9, t * half : (t + 1) * half] = col_sum(z[:, 0:half].astype(F32))
        vec_ref[9:10, t * half : (t + 1) * half] = col_sum(z[:, 2 * half :].astype(F32))
        vec_ref[10 + 2 * t : 11 + 2 * t] = dub1_ref[t : t + 1]
        vec_ref[11 + 2 * t : 12 + 2 * t] = dub2_ref[t : t + 1]
    vec_ref[0:1] = col_sum(dn1 * xhat)
    vec_ref[2:3] = col_sum(dn1)
    for i, row in enumerate((1, 3, 5, 7, 4, 6)):
        vec_ref[row : row + 1] = vecf_ref[i : i + 1]
    vec_ref[14:16] = jnp.zeros((2, D), F32)
    dx = dx1_ref[...] + norm_back(xhat, rstd, dn1, ln_ref[0:1])
    dx_ref[...] = dx[0:rows].astype(BF)


def input_grad(ctl, dest, tokens, dx1, dz1, dz2, ln, vec_f, dub1, dub2, weights):
    rows, rp = tokens.shape[0], dx1.shape[0]
    wcols = weights[0].shape[2]
    return call(
        functools.partial(input_grad_kernel, len(weights), rows, rp), "input_grad", (ctl, dest),
        [(tokens, None)] + [(e, None) for e in (dx1, *dz1, *dz2, ln, vec_f, dub1, dub2)] + [(w, "hbm") for w in weights],
        [((rows, D), BF, 0), ((16, D), F32, 0)],
        [pltpu.VMEM((2 * D, wcols * 3 // 4), BF), pltpu.VMEM((rp, D), F32), pltpu.SemaphoreType.DMA((2 * BLOCKS,))],
        10,
    )


def prepare(segment, me, ln_gain, ln_shift, qb, out_bias, layer_scale):
    rows = segment.shape[1]
    rp = -(-rows // 16) * 16
    cp = -(-rp // 128) * 128
    seg = lax.dynamic_index_in_dim(segment, me, 0, keepdims=False)
    seg = jnp.concatenate([seg, jnp.full((rp - rows,), -2, jnp.int32), jnp.full((cp - rp,), -1, jnp.int32)])
    segr = seg.reshape(1, cp)
    segc = seg[:rp].reshape(rp, 1)
    half = D // 2
    ln1 = jnp.stack([ln_gain[0], ln_shift[0], layer_scale[0]])
    ln2 = jnp.stack([ln_gain[1], ln_shift[1], layer_scale[1], out_bias[1], layer_scale[0]])
    z = jnp.zeros((2, half), F32)
    qbt = jnp.concatenate([qb[0].reshape(2, half), z, qb[1].reshape(2, half)], axis=1)
    return segc, segr, ln1, ln2, qbt, out_bias[0:1]


def swap(v, n_tensor):
    return lax.ppermute(v, "tensor", [(i, (i + 1) % n_tensor) for i in range(n_tensor)])


def after(v, *done):
    return lax.optimization_barrier((v, done))[0]


class Grid:
    axes = ("dp", "tensor")
    places = [(z, y, c, t) for z in range(4) for y in range(2) for c in range(2) for t in range(2)]

    def number(self, p):
        return ((p[0] * 2 + p[1]) * 2 + p[2]) * 2 + p[3]

    def x(self, p):
        return p[0], p[1], p[2], 1 - p[3]

    def y(self, p):
        return p[0], 1 - p[1], p[2], p[3]

    def core(self, p):
        return p[0], p[1], 1 - p[2], p[3]

    def first(self, p):
        return self.y(p) if p[2] else self.x(p)

    def second(self, p):
        return self.x(p) if p[2] else self.y(p)

    def z1(self, p):
        return p[0] ^ 1, p[1], p[2], p[3]

    def z2(self, p):
        return p[0] ^ 2, p[1], p[2], p[3]

    def z3(self, p):
        return p[0] ^ 3, p[1], p[2], p[3]

    def along(self, v):
        return [self.send(e, to) for e, to in zip(v, (self.z1, self.z2, self.z3))]

    def send(self, v, to):
        return lax.ppermute(v, self.axes, [(self.number(p), self.number(to(p))) for p in self.places])

    def line(self, p):
        return [(p[0] ^ k, p[1], p[2], p[3]) for k in range(4)]

    def held(self, p, first, second):
        b = second(p)
        return self.line(p) + self.line(first(p)) + self.line(b) + self.line(first(b))

    def tables(self):
        where = lambda q: q[3] * BLOCKS + (q[0] * 2 + q[1]) * 2 + q[2]
        half = BLOCKS // 2
        rows = []
        for p in self.places:
            row = [where(q) for e in (p, self.core(p)) for q in self.held(e, self.first, self.second)]
            for route in ((self.first, self.second), (self.x, self.y)):
                at = {where(q): i for e in (p, self.core(p)) for i, q in enumerate(self.held(e, *route))}
                row += [at[t * BLOCKS + 2 * m + p[2]] for t in range(2) for m in range(half)]
                row += [at[t * BLOCKS + 2 * m + 1 - p[2]] for t in range(2) for m in range(half)]
            rows.append(row)
        return jnp.array(rows, jnp.int32)


def wide(v):
    return v.astype(F32)


class Reduce:
    def __init__(self, net, keep, sent, first, second):
        self.net, self.terms, self.sent, self.first, self.second = net, [keep], sent, first, second
        self.stage = 0
        self.got = net.send(sent, net.core)

    def total(self, at):
        return sum(wide(e[at]) for e in self.terms)

    def start(self, *dep):
        self.stage += 1
        n = self.stage
        self.terms.append(after(self.got, *dep))
        if n < 3:
            self.sent = self.total(slice(BLOCKS >> n, 2 * BLOCKS >> n)).astype(BF)
            self.got = self.net.send(self.sent, self.second if n == 1 else self.first)
        else:
            self.sent = [self.total(k).astype(BF) for k in (1, 2, 3)]
            self.got = self.net.along(self.sent)

    def result(self, *dep):
        return self.total(0) + sum(wide(e) for e in after(self.got, *dep))


class Plain:
    def __init__(self, n_tensor):
        self.n_tensor = n_tensor

    def gather(self, w):
        me = lax.axis_index("tensor")
        other = swap(w, self.n_tensor)
        both = jnp.where(me == 0, jnp.stack([w, other]), jnp.stack([other, w]))
        full = lax.all_gather(both, "dp", axis=1, tiled=True)
        return [full.reshape(2 * BLOCKS, BROWS, w.shape[1])]

    def settle(self, keep, sent):
        me = lax.axis_index("tensor")
        h = BLOCKS // 2
        g = jnp.stack([keep.reshape(2, h, BROWS, -1), sent.reshape(2, h, BROWS, -1)], axis=2).reshape(2, D, -1)
        part = lax.psum_scatter(g, "dp", scatter_dimension=1, tiled=True).astype(F32)
        return jnp.where(me == 0, part[0], part[1]) + swap(jnp.where(me == 0, part[1], part[0]), self.n_tensor)

    def total(self, v):
        return lax.psum(v, ("dp", "tensor"))


def make_on_device(n_dp, n_tensor):
    def on_device(
        tokens, segment, cotangent, ln_gain, ln_shift, qkv_weight, qv_bias, out_weight,
        out_bias, layer_scale, up_weight, up_bias, down_weight,
    ):
        me = lax.axis_index("tensor")
        own_first = lambda own, other, axis=0: jnp.where(me == 0, jnp.stack([own, other], axis), jnp.stack([other, own], axis))
        both = lambda own, other: own_first(own, other, 1).transpose(1, 0, 2)
        half = D // 2
        hid_half = up_weight.shape[1]
        wa = jnp.concatenate([qkv_weight[0], qkv_weight[1], qkv_weight[2], out_weight.T], axis=1)
        small = jnp.concatenate([qv_bias.reshape(-1), up_bias])

        def pack_ffn(up, down):
            down_t = down.T
            return [jnp.concatenate([up[:, lo : lo + FCH], down_t[:, lo : lo + FCH]], axis=1) for lo in range(0, hid_half, FCH)]

        def consts(small, segment):
            small = own_first(small, swap(small, n_tensor))
            qb = small[:, : 2 * half].reshape(2, 2, half).transpose(1, 0, 2).reshape(2, D)
            ub = small[:, 2 * half :]
            return (ub[:, :FCH], ub[:, FCH:]) + prepare(segment, me, ln_gain, ln_shift, qb, out_bias, layer_scale)

        def results(out, dxs, vec, ga, gup, gdown):
            qv = lax.dynamic_slice(vec, (8, me * half), (2, half))
            dubs = lax.dynamic_slice(vec, (10 + 2 * me, 0), (2, D)).reshape(hid_half)
            return (
                out, dxs, vec[0:2], vec[2:4],
                jnp.stack([ga[:, i * half : (i + 1) * half] for i in range(3)]),
                qv, ga[:, 3 * half :].T, vec[4:6], vec[6:8],
                gup, dubs, gdown.T,
            )

        pick = lambda v: lax.dynamic_index_in_dim(v, me, 0, keepdims=False)
        if n_dp != 16 or n_tensor != 2:
            tokens, cotangent = pick(tokens), pick(cotangent)
            net = Plain(n_tensor)
            dest = jnp.arange(2 * BLOCKS, dtype=jnp.int32)
            slots = jnp.concatenate([jnp.arange(BLOCKS, dtype=jnp.int32)] * 2)
            ctl = jnp.stack([me, 0]).astype(jnp.int32)
            wa = net.gather(wa)
            wf = [net.gather(w) for w in pack_ffn(up_weight, down_weight)]
            ub1, ub2, segc, segr, ln1, ln2, qbt, ob0 = consts(small, segment)
            q, k, v, o1, lse1 = attn_fwd1(ctl, dest, tokens, segc, segr, ln1, qbt, wa)
            x1, attn, o2, lse2 = attn_fwd2(ctl, dest, tokens, segc, segr, ln1, ob0, q, k, v, o1, wa)
            f, dn, dub1, k1, s1 = ffn(True, ctl, dest, slots, x1, cotangent, segc, ln2, ub1, (), wf[0])
            y0, y1, dx1, vec_f, dub2, k2, s2 = ffn(False, ctl, dest, slots, x1, cotangent, segc, ln2, ub2, (attn, f, dn), wf[1])
            dz1 = attn_bwd(0, ctl, dest, dx1, q, k, v, lse1, segc, segr, ln1, wa)
            dz2 = attn_bwd(1, ctl, dest, dx1, q, k, v, lse2, segc, segr, ln1, wa)
            ka, sa = attn_grad(ctl, slots, tokens, dx1, o1, o2, dz1, dz2, ln1)
            dx, vec = input_grad(ctl, dest, tokens, dx1, dz1, dz2, ln1, vec_f, dub1, dub2, wa)
            gf1, gf2, ga = net.settle(k1, s1), net.settle(k2, s2), net.settle(ka, sa)
            vec = net.total(vec)
            gup = jnp.concatenate([gf1[:, :FCH], gf2[:, :FCH]], axis=1)
            gdown = jnp.concatenate([gf1[:, FCH:], gf2[:, FCH:]], axis=1)
            y = jnp.concatenate([y0, y1])
            return results(both(y, swap(y, n_tensor)), both(dx, swap(dx, n_tensor)), vec, ga, gup, gdown)

        net = Grid()
        place = lax.axis_index("dp") * 2 + me
        bs = net.along([wa] * 3)
        tokens, cotangent, segment, small, place = after((tokens, cotangent, segment, small, place), wa)
        tokens, cotangent = pick(tokens), pick(cotangent)
        ub1, ub2, segc, segr, ln1, ln2, qbt, ob0 = consts(small, segment)
        table = lax.dynamic_index_in_dim(net.tables(), place, 0, keepdims=False)
        bs = after(bs, tokens, cotangent, segc, table)
        s = after(jnp.stack([wa, *bs]))
        fs, es = pack_ffn(*after((up_weight, down_weight), s))
        ra = net.send(s, net.first)
        fz = net.along([after(fs, s)] * 3)
        dest, slots, slots_f = (table[i : i + 2 * BLOCKS] for i in range(0, 6 * BLOCKS, 2 * BLOCKS))
        ctl = jnp.stack([me, lax.axis_index("dp") % 2]).astype(jnp.int32)
        ra = after(ra, dest, qbt)
        s = jnp.concatenate([s, ra])
        r = net.send(s, net.second)
        sc = net.send(s, net.core)
        fz = after(fz, s)
        fs = after(jnp.stack([fs, *fz]))
        ez = net.along([after(es, fs)] * 3)
        r = after(r, sc, fs)
        rc = net.send(r, net.core)
        fs = after(fs, r)
        fr = net.send(fs, net.first)
        fr = after(fr, rc)
        fs = jnp.concatenate([fs, fr])
        r1 = net.send(fs, net.second)
        c1 = net.send(fs, net.core)
        wa = after([s, r, sc, rc], fs)
        q, k, v, o1, lse1 = attn_fwd1(ctl, dest, tokens, segc, segr, ln1, qbt, wa)
        r1, c1, ez = after((r1, c1, ez), o1)
        w1 = [fs, r1, c1, net.send(r1, net.core)]
        es = after(jnp.stack([es, *ez]), r1)
        er = net.send(es, net.first)
        q = after(q, es, r1)
        x1, attn, o2, lse2 = attn_fwd2(ctl, dest, tokens, segc, segr, ln1, ob0, q, k, v, o1, wa)
        w1, er = after((w1, er), x1)
        es = jnp.concatenate([es, er])
        r2 = net.send(es, net.second)
        c2 = net.send(es, net.core)
        w1 = after(w1, es)
        f, dn, dub1, k1, s1 = ffn(True, ctl, dest, slots, x1, cotangent, segc, ln2, ub1, (), w1)
        r2, c2 = after((r2, c2), f)
        w2 = [es, r2, c2, net.send(r2, net.core)]
        g1 = Reduce(net, k1, s1, net.first, net.second)
        y0, y1, dx1, vec_f, dub2, k2, s2 = ffn(False, ctl, dest, slots_f, x1, cotangent, segc, ln2, ub2, (attn, f, dn), w2)
        g2 = Reduce(net, k2, s2, net.x, net.y)
        g1.start(dx1)
        dx1 = after(dx1, g1.sent)
        dz1 = attn_bwd(0, ctl, dest, dx1, q, k, v, lse1, segc, segr, ln1, wa)
        g1.start(dz1[0])
        g2.start(dz1[0], g1.sent)
        z0 = swap(after(y0, g2.sent), n_tensor)
        dx1 = after(dx1, dz1[0], g1.sent, g2.sent)
        dz2 = attn_bwd(1, ctl, dest, dx1, q, k, v, lse2, segc, segr, ln1, wa)
        z1 = swap(after(y1, dz2[0]), n_tensor)
        dx1 = after(dx1, dz2[0], z0)
        ka, sa = attn_grad(ctl, slots, tokens, dx1, o1, o2, dz1, dz2, ln1)
        g = Reduce(net, ka, sa, net.first, net.second)
        g1.start(ka)
        g2.start(ka)
        dx1 = after(dx1, ka, g1.sent, g2.sent, z1)
        dx, vec = input_grad(ctl, dest, tokens, dx1, dz1, dz2, ln1, vec_f, dub1, dub2, wa)
        def add(v, to, *dep):
            v = after(v, *dep)
            return v + net.send(v, to)

        g.start(dx)
        vec = add(add(vec, net.z1, g.sent), net.z2)
        g2.start(g.sent, vec)
        vec = add(vec, net.first)
        y0, y1, z0, z1 = after((y0, y1, z0, z1), g.sent)
        out = both(jnp.concatenate([y0, y1]), jnp.concatenate([z0, z1]))
        gf1 = g1.result(g.sent)
        g.start(g2.sent, gf1, out, vec)
        vec = add(vec, net.second, g.sent)
        dx_other = swap(after(dx, vec), n_tensor)
        g.start(vec)
        gf2 = g2.result(g.sent)
        vec = add(vec, net.core, g.sent)
        gup = jnp.concatenate([gf1[:, :FCH], gf2[:, :FCH]], axis=1)
        gdown = jnp.concatenate([gf1[:, FCH:], gf2[:, FCH:]], axis=1)
        dxs = both(dx, dx_other)
        return results(out, dxs, vec, g.result(dxs), gup, gdown)

    return on_device


def solution(mesh):
    rows = P(None, "dp", None)
    wt = P("tensor", "dp")
    return jax.shard_map(
        make_on_device(mesh.shape["dp"], mesh.shape["tensor"]),
        mesh=mesh,
        in_specs=(
            rows, P(None, "dp"), rows, P(), P(), P(None, "dp", "tensor"), P(None, "tensor"), wt,
            P(), P(), P("dp", "tensor"), P("tensor"), wt,
        ),
        out_specs=(
            rows, rows, P(), P(), P(None, "dp", "tensor"), P(None, "tensor"), wt,
            P(), P(), P("dp", "tensor"), P("tensor"), wt,
        ),
        check_vma=False,
    )
```

```python
import functools

import jax
import jax.numpy as jnp
from jax import lax
from jax.experimental import pallas as pl
from jax.experimental.pallas import tpu as pltpu
from jax.sharding import PartitionSpec as P

D = 768
HEADS = 12
HEAD = D // HEADS
EPS = 1e-06
PAD_ID = 3
NEG = -1e30
BF = jnp.bfloat16
F32 = jnp.float32
LOG2E = 1.4426950408889634

BLOCKS = 16
BROWS = D // BLOCKS


def mm(a, b):
    return jnp.dot(a, b, preferred_element_type=F32)


def mm_nt(a, b):
    return lax.dot_general(a, b, (((1,), (1,)), ((), ())), preferred_element_type=F32)


def mm_tn(a, b):
    return lax.dot_general(a, b, (((0,), (0,)), ((), ())), preferred_element_type=F32)


def row_stats(v):
    mean = jnp.mean(v, axis=-1, keepdims=True)
    c = v - mean
    rstd = lax.rsqrt(jnp.mean(c * c, axis=-1, keepdims=True) + EPS)
    return c * rstd, rstd


def norm_back(xhat, rstd, dn, gain):
    dxh = dn * gain
    m1 = jnp.mean(dxh, axis=-1, keepdims=True)
    m2 = jnp.mean(dxh * xhat, axis=-1, keepdims=True)
    return rstd * (dxh - m1 - xhat * m2)


def col_sum(v):
    return jnp.sum(v, axis=0, keepdims=True)


def load_blocks(dest, parts, dst, sem, cols=slice(None)):
    copies = []
    n = 0
    for part in parts:
        for j in range(part.shape[0]):
            row = pl.multiple_of(dest[n] * BROWS, BROWS)
            copies.append(pltpu.make_async_copy(part.at[j, :, cols], dst.at[pl.ds(row, BROWS)], sem.at[n]))
            n += 1
    for c in copies:
        c.start()
    return copies


def store_copies(core, slots, t, stage, outs, cols, sem):
    keep, send = outs
    copies = []
    half = BLOCKS // 2
    for m in range(half):
        a = pl.multiple_of((2 * m + core) * BROWS, BROWS)
        b = pl.multiple_of((2 * m + 1 - core) * BROWS, BROWS)
        copies.append(pltpu.make_async_copy(stage.at[pl.ds(a, BROWS)], keep.at[slots[t * half + m], :, cols], sem.at[2 * m]))
        copies.append(pltpu.make_async_copy(stage.at[pl.ds(b, BROWS)], send.at[slots[BLOCKS + t * half + m], :, cols], sem.at[2 * m + 1]))
    return copies


def pair_mask(h, dtype=BF):
    lane = lax.broadcasted_iota(jnp.int32, (1, 2 * HEAD), 1)
    return (lane // HEAD == h).astype(dtype)


def call(kernel, name, scalars, ins, outs, scratch, us, vmem=32):
    spaces = {None: pltpu.VMEM, 0: pltpu.VMEM, 1: pl.ANY, "hbm": pl.ANY, "far": pltpu.HBM}
    at = lambda how: pl.BlockSpec(memory_space=spaces[how])
    return pl.pallas_call(
        kernel,
        in_specs=[pl.BlockSpec(memory_space=pltpu.SMEM)] * len(scalars) + [at(how) for _, how in ins],
        out_specs=[at(how) for _, _, how in outs],
        out_shape=[jax.ShapeDtypeStruct(shape, dtype) for shape, dtype, _ in outs],
        scratch_shapes=scratch,
        compiler_params=pltpu.CompilerParams(vmem_limit_bytes=vmem * 1024 * 1024),
        cost_estimate=pl.CostEstimate(flops=us * 5_000_000_000, bytes_accessed=us * 1_000_000, transcendentals=0),
        name=name,
    )(*scalars, *[v for v, _ in ins])


PAIRS = HEADS // 2
HP = PAIRS // 2


def fwd_pairs(q_ref, k_ref, v_ref, bias_s, o_ref, lse_ref):
    scale = (HEAD ** (-0.5)) * LOG2E

    def pair(p, _):
        q2 = q_ref[p]
        k2 = k_ref[p]
        v2 = v_ref[p]
        acc = None
        for h in range(2):
            m = pair_mask(h)
            s = mm_nt(q2, k2 * m) * scale + bias_s[...]
            top = jnp.max(s, axis=-1, keepdims=True)
            e = jnp.exp2(s - top)
            tot = jnp.sum(e, axis=-1, keepdims=True)
            oh = mm(e.astype(BF), v2 * m) * (1.0 / tot)
            acc = oh if acc is None else acc + oh
            lse_ref[2 * p + h, :, 0 : top.shape[0]] = (top + jnp.log2(tot)).reshape(1, -1)
        o_ref[p] = acc.astype(BF)
        return 0

    lse_ref[...] = jnp.zeros_like(lse_ref)
    lax.fori_loop(0, HP, pair, 0)


def half_heads(t, src, dst, sem):
    copies = []
    for i, (a, b) in enumerate(zip(src, dst)):
        n = min(a.shape[1], b.shape[1])
        copies.append(pltpu.make_async_copy(a.at[pl.ds(HP * t, HP), 0:n], b.at[:, 0:n], sem.at[i]))
    for c in copies:
        c.start()
    return copies


def attn_fwd1_kernel(nw, rows, rp, cp, ctl, dest, x_ref, segc_ref, segr_ref, ln_ref, qb_ref, *rest):
    w = rest[:nw]
    qh, kh, vh, o_ref, lse_ref, w_s, x_s, bias_s, q_ref, k_ref, v_ref, sem, osem = rest[nw:]
    copies = load_blocks(dest, w, w_s, sem)
    x_s[0:rows, :] = x_ref[...].astype(F32)
    x_s[rows:rp, :] = jnp.zeros((rp - rows, D), F32)
    bias_s[...] = jnp.where(segc_ref[...] == segr_ref[...], 0.0, NEG)
    xhat, _ = row_stats(x_s[...])
    n1 = (xhat * ln_ref[0:1] + ln_ref[1:2]).astype(BF)
    for c in copies:
        c.wait()
    half = D // 2
    k_ref[:, rp:cp, :] = jnp.zeros((PAIRS, cp - rp, 128), BF)
    v_ref[:, rp:cp, :] = jnp.zeros((PAIRS, cp - rp, 128), BF)
    x_s[...] = n1.astype(F32)

    def project(t, _):
        z = mm(x_s[...].astype(BF), w_s[pl.ds(pl.multiple_of(t * D, D), D), 0 : 3 * half]) + qb_ref[pl.ds(t, 1)]
        z = z.astype(BF)
        for i in range(HP):
            q_ref[HP * t + i] = z[:, i * 128 : (i + 1) * 128]
            k_ref[HP * t + i, 0:rp, :] = z[:, half + i * 128 : half + (i + 1) * 128]
            v_ref[HP * t + i, 0:rp, :] = z[:, 2 * half + i * 128 : 2 * half + (i + 1) * 128]
        return 0

    lax.fori_loop(0, 2, project, 0)
    out = [pltpu.make_async_copy(a, b, osem.at[i]) for i, (a, b) in enumerate(((q_ref, qh), (k_ref, kh), (v_ref, vh)))]
    for c in out:
        c.start()
    fwd_pairs(q_ref, k_ref, v_ref, bias_s, o_ref, lse_ref)
    for c in out:
        c.wait()


def attn_fwd2_kernel(nw, rows, rp, cp, ctl, dest, x_ref, segc_ref, segr_ref, ln_ref, ob_ref, qh, kh, vh, o1_ref, *rest):
    w = rest[:nw]
    x1_ref, attn_ref, o_ref, lse_ref, w_s, bias_s, q_s, k_s, v_s, sem, isem = rest[nw:]
    heads = half_heads(1, (qh, kh, vh), (q_s, k_s, v_s), isem)
    half = D // 2
    copies = load_blocks(dest, w, w_s, sem, slice(3 * half, 4 * half))
    bias_s[...] = jnp.where(segc_ref[...] == segr_ref[...], 0.0, NEG)
    for c in heads:
        c.wait()
    fwd_pairs(q_s, k_s, v_s, bias_s, o_ref, lse_ref)
    for c in copies:
        c.wait()
    a = ob_ref[0:1]
    for t, src in enumerate((o1_ref, o_ref)):
        o_t = jnp.concatenate([src[i] for i in range(HP)], axis=1)
        a = a + mm_nt(o_t, w_s[t * D : (t + 1) * D, :]).astype(BF).astype(F32)
    attn_ref[...] = a.astype(BF)
    x1_ref[...] = ln_ref[2:3] * a
    x1_ref[0:rows, :] += x_ref[...].astype(F32)


def attn_fwd1(ctl, dest, tokens, segc, segr, ln, qb, weights):
    rows, rp, cp = tokens.shape[0], segc.shape[0], segr.shape[1]
    wcols = weights[0].shape[2]
    return call(
        functools.partial(attn_fwd1_kernel, len(weights), rows, rp, cp), "attn_fwd1", (ctl, dest),
        [(tokens, None), (segc, None), (segr, None), (ln, None), (qb, None)] + [(w, "hbm") for w in weights],
        [((PAIRS, rp, 128), BF, "far"), ((PAIRS, cp, 128), BF, "far"), ((PAIRS, cp, 128), BF, "far"), ((HP, rp, 128), BF, 0), ((HEADS // 2, 1, cp), F32, 0)],
        [
            pltpu.VMEM((2 * D, wcols), BF), pltpu.VMEM((rp, D), F32), pltpu.VMEM((rp, cp), F32), pltpu.VMEM((PAIRS, rp, 128), BF), pltpu.VMEM((PAIRS, cp, 128), BF), pltpu.VMEM((PAIRS, cp, 128), BF),
            pltpu.SemaphoreType.DMA((2 * BLOCKS,)), pltpu.SemaphoreType.DMA((3,)),
        ],
        14, 48,
    )


def attn_fwd2(ctl, dest, tokens, segc, segr, ln, ob, q, k, v, o1, weights):
    rows, rp, cp = tokens.shape[0], segc.shape[0], segr.shape[1]
    wcols = weights[0].shape[2]
    return call(
        functools.partial(attn_fwd2_kernel, len(weights), rows, rp, cp), "attn_fwd2", (ctl, dest),
        [(tokens, None), (segc, None), (segr, None), (ln, None), (ob, None), (q, "far"), (k, "far"), (v, "far"), (o1, None)] + [(w, "hbm") for w in weights],
        [((rp, D), F32, 0), ((rp, D), BF, 0), ((HP, rp, 128), BF, 0), ((HEADS // 2, 1, cp), F32, 0)],
        [
            pltpu.VMEM((2 * D, wcols // 4), BF), pltpu.VMEM((rp, cp), F32), pltpu.VMEM((HP, rp, 128), BF), pltpu.VMEM((HP, cp, 128), BF), pltpu.VMEM((HP, cp, 128), BF),
            pltpu.SemaphoreType.DMA((2 * BLOCKS,)), pltpu.SemaphoreType.DMA((3,)),
        ],
        12,
    )


def gelu_parts(h):
    x = jnp.abs(h) * 0.7071067811865476
    t = 1.0 / (1.0 + 0.3275911 * x)
    e = jnp.exp2(h * h * (-0.5 * LOG2E))
    poly = t * (0.254829592 * 0.5 + t * (-0.284496736 * 0.5 + t * (1.421413741 * 0.5 + t * (-1.453152027 * 0.5 + t * (1.061405429 * 0.5)))))
    tail = poly * e
    phi = jnp.where(h < 0, tail, 1.0 - tail)
    return phi, phi + h * e * 0.3989422804014327


FCH = 768


def ffn_kernel(rows, rp, first, ctl, dest, slots, x1_ref, cot_ref, segc_ref, ln_ref, ub_ref, *rest):
    if first:
        nw = len(rest) - 16
        w = rest[:nw]
        (f_out, dn_out, dub_ref, keep, send, w_s, n2_s, n2t_s, dfr_s, dft_s, dy_s, stage, f_ref, dn_ref, lsem, ssem) = rest[nw:]
    else:
        attn_ref, fin_ref, dnin_ref = rest[:3]
        nw = len(rest) - 3 - 18
        w = rest[3 : 3 + nw]
        (y0_ref, y1_ref, dx1_ref, vec_ref, dub_ref, keep, send, w_s, n2_s, n2t_s, dfr_s, dft_s, dy_s, stage, f_ref, dn_ref, lsem, ssem) = rest[3 + nw :]
    copies = load_blocks(dest, w, w_s, lsem)
    core = ctl[1]
    live = (segc_ref[...] != PAD_ID).astype(F32)
    xhat, rstd = row_stats(x1_ref[...])
    n2 = (xhat * ln_ref[0:1] + ln_ref[1:2]).astype(BF)
    n2_s[...] = n2
    n2t_s[...] = n2.T
    dy_s[rows:rp, :] = jnp.zeros((rp - rows, D), F32)
    dy_s[0:rows, :] = cot_ref[...].astype(F32)
    dy = dy_s[...] * live
    dy_s[...] = dy
    df = dy * ln_ref[2:3]
    dfr = df.astype(BF)
    dfr_s[...] = dfr
    dft_s[...] = dfr.T
    if not first:
        vec_ref[2:3] = col_sum(df)
    for c in copies:
        c.wait()
    if first:
        f_ref[...] = jnp.zeros((rp, D), F32)
        dn_ref[...] = jnp.zeros((rp, D), F32)
    else:
        f_ref[...] = fin_ref[...].astype(F32)
        dn_ref[...] = dnin_ref[...].astype(F32)
    copies_of = lambda t: store_copies(core, slots, t, stage.at[t], (keep, send), pl.ds(0, 2 * FCH), ssem.at[t])

    def half_units(t, _):
        rows_t = pl.ds(pl.multiple_of(t * D, D), D)
        wu = w_s[rows_t, 0:FCH]
        wd = w_s[rows_t, FCH:]
        hid = mm(n2_s[...], wu) + ub_ref[pl.ds(t, 1)]
        phi, slope = gelu_parts(hid)
        g = (hid * phi).astype(BF)
        dh = (mm(dfr_s[...], wd) * slope).astype(BF)
        dub_ref[pl.ds(t, 1)] = col_sum(dh.astype(F32))
        stage[t, :, 0:FCH] = mm(n2t_s[...], dh).astype(BF)
        stage[t, :, FCH:] = mm(dft_s[...], g).astype(BF)
        for c in copies_of(t):
            c.start()
        f_ref[...] += mm_nt(g, wd)
        dn_ref[...] += mm_nt(dh, wu)
        return 0

    lax.fori_loop(0, 2, half_units, 0)
    pending = copies_of(0) + copies_of(1)
    if first:
        f_out[...] = f_ref[...].astype(BF)
        dn_out[...] = dn_ref[...].astype(BF)
    else:
        ffo = f_ref[...] + ln_ref[3:4]
        dy = dy_s[...]
        vec_ref[3:4] = col_sum(dy * ffo)
        y = (x1_ref[...] + ln_ref[2:3] * ffo).astype(BF)
        cut = y0_ref.shape[0]
        y0_ref[...] = y[0:cut]
        y1_ref[...] = y[cut:rows]
        dn2 = dn_ref[...]
        xhat, rstd = row_stats(x1_ref[...])
        vec_ref[0:1] = col_sum(dn2 * xhat)
        vec_ref[1:2] = col_sum(dn2)
        dx1 = dy + norm_back(xhat, rstd, dn2, ln_ref[0:1])
        dx1_ref[...] = dx1
        vec_ref[4:5] = col_sum(dx1 * ln_ref[4:5])
        vec_ref[5:6] = col_sum(dx1 * attn_ref[...].astype(F32))
        vec_ref[6:8] = jnp.zeros((2, D), F32)
    for c in pending:
        c.wait()


def ffn(first, ctl, dest, slots, x1, cotangent, segc, ln, ub, more, weights):
    rows, rp = cotangent.shape[0], x1.shape[0]
    wcols = weights[0].shape[2]
    if first:
        outs = [((rp, D), BF, 0), ((rp, D), BF, 0)]
    else:
        cut = -(-rows // 32) * 16
        outs = [((cut, D), BF, 0), ((rows - cut, D), BF, 0), ((rp, D), F32, 0), ((8, D), F32, 0)]
    outs += [((2, FCH), F32, 0)] + [((BLOCKS, BROWS, wcols), BF, 1)] * 2
    return call(
        functools.partial(ffn_kernel, rows, rp, first), "ffn_first" if first else "ffn_last", (ctl, dest, slots),
        [(x1, None), (cotangent, None), (segc, None), (ln, None), (ub, None)] + [(v, None) for v in more] + [(w, "hbm") for w in weights],
        outs,
        [
            pltpu.VMEM((2 * D, wcols), BF), pltpu.VMEM((rp, D), BF), pltpu.VMEM((D, rp), BF), pltpu.VMEM((rp, D), BF), pltpu.VMEM((D, rp), BF),
            pltpu.VMEM((rp, D), F32), pltpu.VMEM((2, D, 2 * FCH), BF),
        ]
        + [pltpu.VMEM((rp, D), F32)] * 2
        + [pltpu.SemaphoreType.DMA((2 * BLOCKS,)), pltpu.SemaphoreType.DMA((2, BLOCKS))],
        20, 56,
    )


def attn_bwd_kernel(nw, rp, cp, which, ctl, dest, dx1_ref, qh, kh, vh, lse_ref, segc_ref, segr_ref, ln_ref, *rest):
    w = rest[:nw]
    dq_ref, dk_ref, dv_ref, w_s, do_s, q_s, k_s, v_s, bias_s, sem, isem = rest[nw:]
    t = which[0]
    heads = half_heads(t, (qh, kh, vh), (q_s, k_s, v_s), isem)
    half = D // 2
    copies = load_blocks(dest, w, w_s, sem, slice(3 * half, 4 * half))
    scale = HEAD ** (-0.5)
    bias_s[...] = jnp.where(segc_ref[...] == segr_ref[...], 0.0, NEG)
    q_s[:, rp:cp, :] = jnp.zeros((HP, cp - rp, 128), BF)
    do_s[:, rp:cp, :] = jnp.zeros((HP, cp - rp, 128), BF)
    dar = (dx1_ref[...] * ln_ref[2:3]).astype(BF)
    for c in copies:
        c.wait()
    z = mm(dar, w_s[pl.ds(pl.multiple_of(t * D, D), D), :]).astype(BF)
    for i in range(HP):
        do_s[i, 0:rp, :] = z[:, i * 128 : (i + 1) * 128]
    for c in heads:
        c.wait()

    def pair(p, _):
        q2 = q_s[p]
        do2 = do_s[p]
        k2 = k_s[p]
        v2 = v_s[p]
        def head(h, sums):
            dq, dk, dv = sums
            m = pair_mask(h)
            km = k2 * m
            st = mm_nt(km, q2) * (scale * LOG2E) + bias_s[...]
            pt = jnp.exp2(st - lse_ref[2 * p + h])
            dpt = mm_nt(v2 * m, do2)
            delta = jnp.sum(pt * dpt, axis=0, keepdims=True)
            dst = (pt * (dpt - delta)).astype(BF)
            return dq + mm_tn(dst, km), dk + mm(dst, q2 * m), dv + mm(pt.astype(BF), do2 * m)

        zero = jnp.zeros((rp, 128), F32)
        dq, dk, dv = lax.fori_loop(0, 2, head, (jnp.zeros((cp, 128), F32), zero, zero))
        dq_ref[p] = (dq[0:rp] * scale).astype(BF)
        dk_ref[p] = (dk * scale).astype(BF)
        dv_ref[p] = dv.astype(BF)
        return 0

    lax.fori_loop(0, HP, pair, 0)


def attn_bwd(t, ctl, dest, dx1, q, k, v, lse, segc, segr, ln, weights):
    rp, cp = segc.shape[0], segr.shape[1]
    wcols = weights[0].shape[2]
    return call(
        functools.partial(attn_bwd_kernel, len(weights), rp, cp), "attn_bwd", (jnp.full((1,), t, jnp.int32), ctl, dest),
        [(dx1, None), (q, "far"), (k, "far"), (v, "far")] + [(e, None) for e in (lse, segc, segr, ln)] + [(w, "hbm") for w in weights],
        [((HP, rp, 128), BF, 0)] * 3,
        [
            pltpu.VMEM((2 * D, wcols // 4), BF), pltpu.VMEM((HP, cp, 128), BF), pltpu.VMEM((HP, cp, 128), BF), pltpu.VMEM((HP, rp, 128), BF), pltpu.VMEM((HP, rp, 128), BF),
            pltpu.VMEM((rp, cp), F32), pltpu.SemaphoreType.DMA((2 * BLOCKS,)), pltpu.SemaphoreType.DMA((3,)),
        ],
        15, 52,
    )


def attn_grad_kernel(rows, rp, ctl, slots, x_ref, dx1_ref, o1_ref, o2_ref, dq1, dk1, dv1, dq2, dk2, dv2, ln_ref, keep, send, stage, x_s, ssem):
    core = ctl[1]
    half = D // 2
    x_s[0:rows, :] = x_ref[...].astype(F32)
    x_s[rows:rp, :] = jnp.zeros((rp - rows, D), F32)
    dart = (dx1_ref[...] * ln_ref[2:3]).astype(BF).T
    xhat, _ = row_stats(x_s[...])
    n1t = (xhat * ln_ref[0:1] + ln_ref[1:2]).astype(BF).T
    pend = []
    for t, (o, dz) in enumerate(((o1_ref, (dq1, dk1, dv1)), (o2_ref, (dq2, dk2, dv2)))):
        o_t = jnp.concatenate([o[i] for i in range(HP)], axis=1)
        stage[t, :, 3 * half :] = mm(dart, o_t).astype(BF)
        z = jnp.concatenate([e[i] for e in dz for i in range(HP)], axis=1)
        stage[t, :, 0 : 3 * half] = mm(n1t, z).astype(BF)
        cps = store_copies(core, slots, t, stage.at[t], (keep, send), pl.ds(0, 4 * half), ssem.at[t])
        for c in cps:
            c.start()
        pend += cps
    for c in pend:
        c.wait()


def attn_grad(ctl, slots, tokens, dx1, o1, o2, dz1, dz2, ln):
    rows, rp = tokens.shape[0], dx1.shape[0]
    wcols = 2 * D
    return call(
        functools.partial(attn_grad_kernel, rows, rp), "attn_grad", (ctl, slots),
        [(tokens, None)] + [(e, None) for e in (dx1, o1, o2, *dz1, *dz2, ln)],
        [((BLOCKS, BROWS, wcols), BF, 1)] * 2,
        [pltpu.VMEM((2, D, wcols), BF), pltpu.VMEM((rp, D), F32), pltpu.SemaphoreType.DMA((2, BLOCKS))],
        10, 48,
    )


def input_grad_kernel(nw, rows, rp, ctl, dest, x_ref, dx1_ref, dq1, dk1, dv1, dq2, dk2, dv2, ln_ref, vecf_ref, dub1_ref, dub2_ref, *rest):
    w = rest[:nw]
    dx_ref, vec_ref, w_s, x_s, sem = rest[nw:]
    half = D // 2
    copies = load_blocks(dest, w, w_s, sem, slice(0, 3 * half))
    x_s[0:rows, :] = x_ref[...].astype(F32)
    x_s[rows:rp, :] = jnp.zeros((rp - rows, D), F32)
    xhat, rstd = row_stats(x_s[...])
    for c in copies:
        c.wait()
    dn1 = None
    for t, dz in enumerate(((dq1, dk1, dv1), (dq2, dk2, dv2))):
        z = jnp.concatenate([e[i] for e in dz for i in range(HP)], axis=1)
        part = mm_nt(z, w_s[t * D : (t + 1) * D, :])
        dn1 = part if dn1 is None else dn1 + part
        vec_ref[8:9, t * half : (t + 1) * half] = col_sum(z[:, 0:half].astype(F32))
        vec_ref[9:10, t * half : (t + 1) * half] = col_sum(z[:, 2 * half :].astype(F32))
        vec_ref[10 + 2 * t : 11 + 2 * t] = dub1_ref[t : t + 1]
        vec_ref[11 + 2 * t : 12 + 2 * t] = dub2_ref[t : t + 1]
    vec_ref[0:1] = col_sum(dn1 * xhat)
    vec_ref[2:3] = col_sum(dn1)
    for i, row in enumerate((1, 3, 5, 7, 4, 6)):
        vec_ref[row : row + 1] = vecf_ref[i : i + 1]
    vec_ref[14:16] = jnp.zeros((2, D), F32)
    dx = dx1_ref[...] + norm_back(xhat, rstd, dn1, ln_ref[0:1])
    dx_ref[...] = dx[0:rows].astype(BF)


def input_grad(ctl, dest, tokens, dx1, dz1, dz2, ln, vec_f, dub1, dub2, weights):
    rows, rp = tokens.shape[0], dx1.shape[0]
    wcols = weights[0].shape[2]
    return call(
        functools.partial(input_grad_kernel, len(weights), rows, rp), "input_grad", (ctl, dest),
        [(tokens, None)] + [(e, None) for e in (dx1, *dz1, *dz2, ln, vec_f, dub1, dub2)] + [(w, "hbm") for w in weights],
        [((rows, D), BF, 0), ((16, D), F32, 0)],
        [pltpu.VMEM((2 * D, wcols * 3 // 4), BF), pltpu.VMEM((rp, D), F32), pltpu.SemaphoreType.DMA((2 * BLOCKS,))],
        10,
    )


def prepare(segment, me, ln_gain, ln_shift, qb, out_bias, layer_scale):
    rows = segment.shape[1]
    rp = -(-rows // 16) * 16
    cp = -(-rp // 128) * 128
    seg = lax.dynamic_index_in_dim(segment, me, 0, keepdims=False)
    seg = jnp.concatenate([seg, jnp.full((rp - rows,), -2, jnp.int32), jnp.full((cp - rp,), -1, jnp.int32)])
    segr = seg.reshape(1, cp)
    segc = seg[:rp].reshape(rp, 1)
    half = D // 2
    ln1 = jnp.stack([ln_gain[0], ln_shift[0], layer_scale[0]])
    ln2 = jnp.stack([ln_gain[1], ln_shift[1], layer_scale[1], out_bias[1], layer_scale[0]])
    z = jnp.zeros((2, half), F32)
    qbt = jnp.concatenate([qb[0].reshape(2, half), z, qb[1].reshape(2, half)], axis=1)
    return segc, segr, ln1, ln2, qbt, out_bias[0:1]


def swap(v, n_tensor):
    return lax.ppermute(v, "tensor", [(i, (i + 1) % n_tensor) for i in range(n_tensor)])


def after(v, *done):
    return lax.optimization_barrier((v, done))[0]


class Grid:
    axes = ("dp", "tensor")
    places = [(z, y, c, t) for z in range(4) for y in range(2) for c in range(2) for t in range(2)]

    def number(self, p):
        return ((p[0] * 2 + p[1]) * 2 + p[2]) * 2 + p[3]

    def x(self, p):
        return p[0], p[1], p[2], 1 - p[3]

    def y(self, p):
        return p[0], 1 - p[1], p[2], p[3]

    def core(self, p):
        return p[0], p[1], 1 - p[2], p[3]

    def first(self, p):
        return self.y(p) if p[2] else self.x(p)

    def second(self, p):
        return self.x(p) if p[2] else self.y(p)

    def z1(self, p):
        return p[0] ^ 1, p[1], p[2], p[3]

    def z2(self, p):
        return p[0] ^ 2, p[1], p[2], p[3]

    def z3(self, p):
        return p[0] ^ 3, p[1], p[2], p[3]

    def along(self, v):
        return [self.send(e, to) for e, to in zip(v, (self.z1, self.z2, self.z3))]

    def send(self, v, to):
        return lax.ppermute(v, self.axes, [(self.number(p), self.number(to(p))) for p in self.places])

    def line(self, p):
        return [(p[0] ^ k, p[1], p[2], p[3]) for k in range(4)]

    def held(self, p, first, second):
        b = second(p)
        return self.line(p) + self.line(first(p)) + self.line(b) + self.line(first(b))

    def tables(self):
        where = lambda q: q[3] * BLOCKS + (q[0] * 2 + q[1]) * 2 + q[2]
        half = BLOCKS // 2
        rows = []
        for p in self.places:
            row = [where(q) for e in (p, self.core(p)) for q in self.held(e, self.first, self.second)]
            for route in ((self.first, self.second), (self.x, self.y)):
                at = {where(q): i for e in (p, self.core(p)) for i, q in enumerate(self.held(e, *route))}
                row += [at[t * BLOCKS + 2 * m + p[2]] for t in range(2) for m in range(half)]
                row += [at[t * BLOCKS + 2 * m + 1 - p[2]] for t in range(2) for m in range(half)]
            rows.append(row)
        return jnp.array(rows, jnp.int32)


def wide(v):
    return v.astype(F32)


class Reduce:
    def __init__(self, net, keep, sent, first, second):
        self.net, self.terms, self.sent, self.first, self.second = net, [keep], sent, first, second
        self.stage = 0
        self.got = net.send(sent, net.core)

    def total(self, at):
        return sum(wide(e[at]) for e in self.terms)

    def start(self, *dep):
        self.stage += 1
        n = self.stage
        self.terms.append(after(self.got, *dep))
        if n < 3:
            self.sent = self.total(slice(BLOCKS >> n, 2 * BLOCKS >> n)).astype(BF)
            self.got = self.net.send(self.sent, self.second if n == 1 else self.first)
        else:
            self.sent = [self.total(k).astype(BF) for k in (1, 2, 3)]
            self.got = self.net.along(self.sent)

    def result(self, *dep):
        return self.total(0) + sum(wide(e) for e in after(self.got, *dep))


class Plain:
    def __init__(self, n_tensor):
        self.n_tensor = n_tensor

    def gather(self, w):
        me = lax.axis_index("tensor")
        other = swap(w, self.n_tensor)
        both = jnp.where(me == 0, jnp.stack([w, other]), jnp.stack([other, w]))
        full = lax.all_gather(both, "dp", axis=1, tiled=True)
        return [full.reshape(2 * BLOCKS, BROWS, w.shape[1])]

    def settle(self, keep, sent):
        me = lax.axis_index("tensor")
        h = BLOCKS // 2
        g = jnp.stack([keep.reshape(2, h, BROWS, -1), sent.reshape(2, h, BROWS, -1)], axis=2).reshape(2, D, -1)
        part = lax.psum_scatter(g, "dp", scatter_dimension=1, tiled=True).astype(F32)
        return jnp.where(me == 0, part[0], part[1]) + swap(jnp.where(me == 0, part[1], part[0]), self.n_tensor)

    def total(self, v):
        return lax.psum(v, ("dp", "tensor"))


def make_on_device(n_dp, n_tensor):
    def on_device(
        tokens, segment, cotangent, ln_gain, ln_shift, qkv_weight, qv_bias, out_weight,
        out_bias, layer_scale, up_weight, up_bias, down_weight,
    ):
        me = lax.axis_index("tensor")
        own_first = lambda own, other, axis=0: jnp.where(me == 0, jnp.stack([own, other], axis), jnp.stack([other, own], axis))
        both = lambda own, other: own_first(own, other, 1).transpose(1, 0, 2)
        half = D // 2
        hid_half = up_weight.shape[1]
        wa = jnp.concatenate([qkv_weight[0], qkv_weight[1], qkv_weight[2], out_weight.T], axis=1)
        small = jnp.concatenate([qv_bias.reshape(-1), up_bias])

        def pack_ffn(up, down):
            down_t = down.T
            return [jnp.concatenate([up[:, lo : lo + FCH], down_t[:, lo : lo + FCH]], axis=1) for lo in range(0, hid_half, FCH)]

        def consts(small, segment):
            small = own_first(small, swap(small, n_tensor))
            qb = small[:, : 2 * half].reshape(2, 2, half).transpose(1, 0, 2).reshape(2, D)
            ub = small[:, 2 * half :]
            return (ub[:, :FCH], ub[:, FCH:]) + prepare(segment, me, ln_gain, ln_shift, qb, out_bias, layer_scale)

        def results(out, dxs, vec, ga, gup, gdown):
            qv = lax.dynamic_slice(vec, (8, me * half), (2, half))
            dubs = lax.dynamic_slice(vec, (10 + 2 * me, 0), (2, D)).reshape(hid_half)
            return (
                out, dxs, vec[0:2], vec[2:4],
                jnp.stack([ga[:, i * half : (i + 1) * half] for i in range(3)]),
                qv, ga[:, 3 * half :].T, vec[4:6], vec[6:8],
                gup, dubs, gdown.T,
            )

        pick = lambda v: lax.dynamic_index_in_dim(v, me, 0, keepdims=False)
        if n_dp != 16 or n_tensor != 2:
            tokens, cotangent = pick(tokens), pick(cotangent)
            net = Plain(n_tensor)
            dest = jnp.arange(2 * BLOCKS, dtype=jnp.int32)
            slots = jnp.concatenate([jnp.arange(BLOCKS, dtype=jnp.int32)] * 2)
            ctl = jnp.stack([me, 0]).astype(jnp.int32)
            wa = net.gather(wa)
            wf = [net.gather(w) for w in pack_ffn(up_weight, down_weight)]
            ub1, ub2, segc, segr, ln1, ln2, qbt, ob0 = consts(small, segment)
            q, k, v, o1, lse1 = attn_fwd1(ctl, dest, tokens, segc, segr, ln1, qbt, wa)
            x1, attn, o2, lse2 = attn_fwd2(ctl, dest, tokens, segc, segr, ln1, ob0, q, k, v, o1, wa)
            f, dn, dub1, k1, s1 = ffn(True, ctl, dest, slots, x1, cotangent, segc, ln2, ub1, (), wf[0])
            y0, y1, dx1, vec_f, dub2, k2, s2 = ffn(False, ctl, dest, slots, x1, cotangent, segc, ln2, ub2, (attn, f, dn), wf[1])
            dz1 = attn_bwd(0, ctl, dest, dx1, q, k, v, lse1, segc, segr, ln1, wa)
            dz2 = attn_bwd(1, ctl, dest, dx1, q, k, v, lse2, segc, segr, ln1, wa)
            ka, sa = attn_grad(ctl, slots, tokens, dx1, o1, o2, dz1, dz2, ln1)
            dx, vec = input_grad(ctl, dest, tokens, dx1, dz1, dz2, ln1, vec_f, dub1, dub2, wa)
            gf1, gf2, ga = net.settle(k1, s1), net.settle(k2, s2), net.settle(ka, sa)
            vec = net.total(vec)
            gup = jnp.concatenate([gf1[:, :FCH], gf2[:, :FCH]], axis=1)
            gdown = jnp.concatenate([gf1[:, FCH:], gf2[:, FCH:]], axis=1)
            y = jnp.concatenate([y0, y1])
            return results(both(y, swap(y, n_tensor)), both(dx, swap(dx, n_tensor)), vec, ga, gup, gdown)

        net = Grid()
        place = lax.axis_index("dp") * 2 + me
        bs = net.along([wa] * 3)
        tokens, cotangent, segment, small, place = after((tokens, cotangent, segment, small, place), wa)
        tokens, cotangent = pick(tokens), pick(cotangent)
        ub1, ub2, segc, segr, ln1, ln2, qbt, ob0 = consts(small, segment)
        table = lax.dynamic_index_in_dim(net.tables(), place, 0, keepdims=False)
        bs = after(bs, tokens, cotangent, segc, table)
        s = after(jnp.stack([wa, *bs]))
        fs, es = pack_ffn(*after((up_weight, down_weight), s))
        ra = net.send(s, net.first)
        fz = net.along([after(fs, s)] * 3)
        dest, slots, slots_f = (table[i : i + 2 * BLOCKS] for i in range(0, 6 * BLOCKS, 2 * BLOCKS))
        ctl = jnp.stack([me, lax.axis_index("dp") % 2]).astype(jnp.int32)
        ra = after(ra, dest, qbt)
        s = jnp.concatenate([s, ra])
        r = net.send(s, net.second)
        sc = net.send(s, net.core)
        fz = after(fz, s)
        fs = after(jnp.stack([fs, *fz]))
        ez = net.along([after(es, fs)] * 3)
        r = after(r, sc, fs)
        rc = net.send(r, net.core)
        fs = after(fs, r)
        fr = net.send(fs, net.first)
        fr = after(fr, rc)
        fs = jnp.concatenate([fs, fr])
        r1 = net.send(fs, net.second)
        c1 = net.send(fs, net.core)
        wa = after([s, r, sc, rc], fs)
        q, k, v, o1, lse1 = attn_fwd1(ctl, dest, tokens, segc, segr, ln1, qbt, wa)
        r1, c1, ez = after((r1, c1, ez), o1)
        w1 = [fs, r1, c1, net.send(r1, net.core)]
        es = after(jnp.stack([es, *ez]), r1)
        er = net.send(es, net.first)
        q = after(q, es, r1)
        x1, attn, o2, lse2 = attn_fwd2(ctl, dest, tokens, segc, segr, ln1, ob0, q, k, v, o1, wa)
        w1, er = after((w1, er), x1)
        es = jnp.concatenate([es, er])
        r2 = net.send(es, net.second)
        c2 = net.send(es, net.core)
        w1 = after(w1, es)
        f, dn, dub1, k1, s1 = ffn(True, ctl, dest, slots, x1, cotangent, segc, ln2, ub1, (), w1)
        r2, c2 = after((r2, c2), f)
        w2 = [es, r2, c2, net.send(r2, net.core)]
        g1 = Reduce(net, k1, s1, net.first, net.second)
        y0, y1, dx1, vec_f, dub2, k2, s2 = ffn(False, ctl, dest, slots_f, x1, cotangent, segc, ln2, ub2, (attn, f, dn), w2)
        g2 = Reduce(net, k2, s2, net.x, net.y)
        g1.start(dx1)
        dx1 = after(dx1, g1.sent)
        dz1 = attn_bwd(0, ctl, dest, dx1, q, k, v, lse1, segc, segr, ln1, wa)
        g1.start(dz1[0])
        g2.start(dz1[0], g1.sent)
        z0 = swap(after(y0, g2.sent), n_tensor)
        dx1 = after(dx1, dz1[0], g1.sent, g2.sent)
        dz2 = attn_bwd(1, ctl, dest, dx1, q, k, v, lse2, segc, segr, ln1, wa)
        z1 = swap(after(y1, dz2[0]), n_tensor)
        dx1 = after(dx1, dz2[0], z0)
        ka, sa = attn_grad(ctl, slots, tokens, dx1, o1, o2, dz1, dz2, ln1)
        g = Reduce(net, ka, sa, net.first, net.second)
        g1.start(ka)
        g2.start(ka)
        dx1 = after(dx1, ka, g1.sent, g2.sent, z1)
        dx, vec = input_grad(ctl, dest, tokens, dx1, dz1, dz2, ln1, vec_f, dub1, dub2, wa)
        def add(v, to, *dep):
            v = after(v, *dep)
            return v + net.send(v, to)

        g.start(dx)
        vec = add(add(vec, net.z1, g.sent), net.z2)
        g2.start(g.sent, vec)
        vec = add(vec, net.first)
        y0, y1, z0, z1 = after((y0, y1, z0, z1), g.sent)
        out = both(jnp.concatenate([y0, y1]), jnp.concatenate([z0, z1]))
        gf1 = g1.result(g.sent)
        g.start(g2.sent, gf1, out, vec)
        vec = add(vec, net.second, g.sent)
        dx_other = swap(after(dx, vec), n_tensor)
        g.start(vec)
        gf2 = g2.result(g.sent)
        vec = add(vec, net.core, g.sent)
        gup = jnp.concatenate([gf1[:, :FCH], gf2[:, :FCH]], axis=1)
        gdown = jnp.concatenate([gf1[:, FCH:], gf2[:, FCH:]], axis=1)
        dxs = both(dx, dx_other)
        return results(out, dxs, vec, g.result(dxs), gup, gdown)

    return on_device


def solution(mesh):
    rows = P(None, "dp", None)
    wt = P("tensor", "dp")
    return jax.shard_map(
        make_on_device(mesh.shape["dp"], mesh.shape["tensor"]),
        mesh=mesh,
        in_specs=(
            rows, P(None, "dp"), rows, P(), P(), P(None, "dp", "tensor"), P(None, "tensor"), wt,
            P(), P(), P("dp", "tensor"), P("tensor"), wt,
        ),
        out_specs=(
            rows, rows, P(), P(), P(None, "dp", "tensor"), P(None, "tensor"), wt,
            P(), P(), P("dp", "tensor"), P("tensor"), wt,
        ),
        check_vma=False,
    )
```

```python
import functools

import jax
import jax.numpy as jnp
from jax import lax
from jax.experimental import pallas as pl
from jax.experimental.pallas import tpu as pltpu
from jax.sharding import PartitionSpec as P

D = 768
HEADS = 12
HEAD = D // HEADS
EPS = 1e-06
PAD_ID = 3
NEG = -1e30
BF = jnp.bfloat16
F32 = jnp.float32
LOG2E = 1.4426950408889634

BLOCKS = 16
BROWS = D // BLOCKS


def mm(a, b):
    return jnp.dot(a, b, preferred_element_type=F32)


def mm_nt(a, b):
    return lax.dot_general(a, b, (((1,), (1,)), ((), ())), preferred_element_type=F32)


def mm_tn(a, b):
    return lax.dot_general(a, b, (((0,), (0,)), ((), ())), preferred_element_type=F32)


def row_stats(v):
    mean = jnp.mean(v, axis=-1, keepdims=True)
    c = v - mean
    rstd = lax.rsqrt(jnp.mean(c * c, axis=-1, keepdims=True) + EPS)
    return c * rstd, rstd


def norm_back(xhat, rstd, dn, gain):
    dxh = dn * gain
    m1 = jnp.mean(dxh, axis=-1, keepdims=True)
    m2 = jnp.mean(dxh * xhat, axis=-1, keepdims=True)
    return rstd * (dxh - m1 - xhat * m2)


def col_sum(v):
    return jnp.sum(v, axis=0, keepdims=True)


def load_blocks(dest, parts, dst, sem, cols=slice(None)):
    copies = []
    n = 0
    for part in parts:
        for j in range(part.shape[0]):
            row = pl.multiple_of(dest[n] * BROWS, BROWS)
            copies.append(pltpu.make_async_copy(part.at[j, :, cols], dst.at[pl.ds(row, BROWS)], sem.at[n]))
            n += 1
    for c in copies:
        c.start()
    return copies


def store_copies(core, slots, t, stage, outs, cols, sem):
    keep, send = outs
    copies = []
    half = BLOCKS // 2
    for m in range(half):
        a = pl.multiple_of((2 * m + core) * BROWS, BROWS)
        b = pl.multiple_of((2 * m + 1 - core) * BROWS, BROWS)
        copies.append(pltpu.make_async_copy(stage.at[pl.ds(a, BROWS)], keep.at[slots[t * half + m], :, cols], sem.at[2 * m]))
        copies.append(pltpu.make_async_copy(stage.at[pl.ds(b, BROWS)], send.at[slots[BLOCKS + t * half + m], :, cols], sem.at[2 * m + 1]))
    return copies


def pair_mask(h, dtype=BF):
    lane = lax.broadcasted_iota(jnp.int32, (1, 2 * HEAD), 1)
    return (lane // HEAD == h).astype(dtype)


def call(kernel, name, scalars, ins, outs, scratch, us, vmem=32):
    spaces = {None: pltpu.VMEM, 0: pltpu.VMEM, 1: pl.ANY, "hbm": pl.ANY, "far": pltpu.HBM}
    at = lambda how: pl.BlockSpec(memory_space=spaces[how])
    return pl.pallas_call(
        kernel,
        in_specs=[pl.BlockSpec(memory_space=pltpu.SMEM)] * len(scalars) + [at(how) for _, how in ins],
        out_specs=[at(how) for _, _, how in outs],
        out_shape=[jax.ShapeDtypeStruct(shape, dtype) for shape, dtype, _ in outs],
        scratch_shapes=scratch,
        compiler_params=pltpu.CompilerParams(vmem_limit_bytes=vmem * 1024 * 1024),
        cost_estimate=pl.CostEstimate(flops=us * 5_000_000_000, bytes_accessed=us * 1_000_000, transcendentals=0),
        name=name,
    )(*scalars, *[v for v, _ in ins])


PAIRS = HEADS // 2
HP = PAIRS // 2


def fwd_pairs(q_ref, k_ref, v_ref, bias_s, o_ref, lse_ref):
    scale = (HEAD ** (-0.5)) * LOG2E

    def pair(p, _):
        q2 = q_ref[p]
        k2 = k_ref[p]
        v2 = v_ref[p]

        def head(h, acc):
            m = pair_mask(h)
            s = mm_nt(q2, k2 * m) * scale + bias_s[...]
            top = jnp.max(s, axis=-1, keepdims=True)
            e = jnp.exp2(s - top)
            tot = jnp.sum(e, axis=-1, keepdims=True)
            oh = mm(e.astype(BF), v2 * m) * (1.0 / tot)
            lse_ref[2 * p + h, :, 0 : top.shape[0]] = (top + jnp.log2(tot)).reshape(1, -1)
            return acc + oh

        acc = lax.fori_loop(0, 2, head, jnp.zeros(q2.shape, F32))
        o_ref[p] = acc.astype(BF)
        return 0

    lse_ref[...] = jnp.zeros_like(lse_ref)
    lax.fori_loop(0, HP, pair, 0)


def half_heads(t, src, dst, sem):
    copies = []
    for i, (a, b) in enumerate(zip(src, dst)):
        n = min(a.shape[1], b.shape[1])
        copies.append(pltpu.make_async_copy(a.at[pl.ds(HP * t, HP), 0:n], b.at[:, 0:n], sem.at[i]))
    for c in copies:
        c.start()
    return copies


def attn_fwd1_kernel(nw, rows, rp, cp, ctl, dest, x_ref, segc_ref, segr_ref, ln_ref, qb_ref, *rest):
    w = rest[:nw]
    qh, kh, vh, o_ref, lse_ref, w_s, x_s, bias_s, q_ref, k_ref, v_ref, sem, osem = rest[nw:]
    copies = load_blocks(dest, w, w_s, sem)
    x_s[0:rows, :] = x_ref[...].astype(F32)
    x_s[rows:rp, :] = jnp.zeros((rp - rows, D), F32)
    bias_s[...] = jnp.where(segc_ref[...] == segr_ref[...], 0.0, NEG)
    xhat, _ = row_stats(x_s[...])
    n1 = (xhat * ln_ref[0:1] + ln_ref[1:2]).astype(BF)
    for c in copies:
        c.wait()
    half = D // 2
    k_ref[:, rp:cp, :] = jnp.zeros((PAIRS, cp - rp, 128), BF)
    v_ref[:, rp:cp, :] = jnp.zeros((PAIRS, cp - rp, 128), BF)
    x_s[...] = n1.astype(F32)

    def project(t, _):
        z = mm(x_s[...].astype(BF), w_s[pl.ds(pl.multiple_of(t * D, D), D), 0 : 3 * half]) + qb_ref[pl.ds(t, 1)]
        z = z.astype(BF)
        for i in range(HP):
            q_ref[HP * t + i] = z[:, i * 128 : (i + 1) * 128]
            k_ref[HP * t + i, 0:rp, :] = z[:, half + i * 128 : half + (i + 1) * 128]
            v_ref[HP * t + i, 0:rp, :] = z[:, 2 * half + i * 128 : 2 * half + (i + 1) * 128]
        return 0

    lax.fori_loop(0, 2, project, 0)
    out = [pltpu.make_async_copy(a, b, osem.at[i]) for i, (a, b) in enumerate(((q_ref, qh), (k_ref, kh), (v_ref, vh)))]
    for c in out:
        c.start()
    fwd_pairs(q_ref, k_ref, v_ref, bias_s, o_ref, lse_ref)
    for c in out:
        c.wait()


def attn_fwd2_kernel(nw, rows, rp, cp, ctl, dest, x_ref, segc_ref, segr_ref, ln_ref, ob_ref, qh, kh, vh, o1_ref, *rest):
    w = rest[:nw]
    x1_ref, attn_ref, o_ref, lse_ref, w_s, bias_s, q_s, k_s, v_s, sem, isem = rest[nw:]
    heads = half_heads(1, (qh, kh, vh), (q_s, k_s, v_s), isem)
    half = D // 2
    copies = load_blocks(dest, w, w_s, sem, slice(3 * half, 4 * half))
    bias_s[...] = jnp.where(segc_ref[...] == segr_ref[...], 0.0, NEG)
    for c in heads:
        c.wait()
    fwd_pairs(q_s, k_s, v_s, bias_s, o_ref, lse_ref)
    for c in copies:
        c.wait()
    a = ob_ref[0:1]
    for t, src in enumerate((o1_ref, o_ref)):
        o_t = jnp.concatenate([src[i] for i in range(HP)], axis=1)
        a = a + mm_nt(o_t, w_s[t * D : (t + 1) * D, :]).astype(BF).astype(F32)
    attn_ref[...] = a.astype(BF)
    x1_ref[...] = ln_ref[2:3] * a
    x1_ref[0:rows, :] += x_ref[...].astype(F32)


def attn_fwd1(ctl, dest, tokens, segc, segr, ln, qb, weights):
    rows, rp, cp = tokens.shape[0], segc.shape[0], segr.shape[1]
    wcols = weights[0].shape[2]
    return call(
        functools.partial(attn_fwd1_kernel, len(weights), rows, rp, cp), "attn_fwd1", (ctl, dest),
        [(tokens, None), (segc, None), (segr, None), (ln, None), (qb, None)] + [(w, "hbm") for w in weights],
        [((PAIRS, rp, 128), BF, "far"), ((PAIRS, cp, 128), BF, "far"), ((PAIRS, cp, 128), BF, "far"), ((HP, rp, 128), BF, 0), ((HEADS // 2, 1, cp), F32, 0)],
        [
            pltpu.VMEM((2 * D, wcols), BF), pltpu.VMEM((rp, D), F32), pltpu.VMEM((rp, cp), F32), pltpu.VMEM((PAIRS, rp, 128), BF), pltpu.VMEM((PAIRS, cp, 128), BF), pltpu.VMEM((PAIRS, cp, 128), BF),
            pltpu.SemaphoreType.DMA((2 * BLOCKS,)), pltpu.SemaphoreType.DMA((3,)),
        ],
        14, 48,
    )


def attn_fwd2(ctl, dest, tokens, segc, segr, ln, ob, q, k, v, o1, weights):
    rows, rp, cp = tokens.shape[0], segc.shape[0], segr.shape[1]
    wcols = weights[0].shape[2]
    return call(
        functools.partial(attn_fwd2_kernel, len(weights), rows, rp, cp), "attn_fwd2", (ctl, dest),
        [(tokens, None), (segc, None), (segr, None), (ln, None), (ob, None), (q, "far"), (k, "far"), (v, "far"), (o1, None)] + [(w, "hbm") for w in weights],
        [((rp, D), F32, 0), ((rp, D), BF, 0), ((HP, rp, 128), BF, 0), ((HEADS // 2, 1, cp), F32, 0)],
        [
            pltpu.VMEM((2 * D, wcols // 4), BF), pltpu.VMEM((rp, cp), F32), pltpu.VMEM((HP, rp, 128), BF), pltpu.VMEM((HP, cp, 128), BF), pltpu.VMEM((HP, cp, 128), BF),
            pltpu.SemaphoreType.DMA((2 * BLOCKS,)), pltpu.SemaphoreType.DMA((3,)),
        ],
        12,
    )


def gelu_parts(h):
    x = jnp.abs(h) * 0.7071067811865476
    t = 1.0 / (1.0 + 0.3275911 * x)
    e = jnp.exp2(h * h * (-0.5 * LOG2E))
    poly = t * (0.254829592 * 0.5 + t * (-0.284496736 * 0.5 + t * (1.421413741 * 0.5 + t * (-1.453152027 * 0.5 + t * (1.061405429 * 0.5)))))
    tail = poly * e
    phi = jnp.where(h < 0, tail, 1.0 - tail)
    return phi, phi + h * e * 0.3989422804014327


FCH = 768


def ffn_kernel(rows, rp, first, ctl, dest, slots, x1_ref, cot_ref, segc_ref, ln_ref, ub_ref, *rest):
    if first:
        nw = len(rest) - 16
        w = rest[:nw]
        (f_out, dn_out, dub_ref, keep, send, w_s, n2_s, n2t_s, dfr_s, dft_s, dy_s, stage, f_ref, dn_ref, lsem, ssem) = rest[nw:]
    else:
        attn_ref, fin_ref, dnin_ref = rest[:3]
        nw = len(rest) - 3 - 18
        w = rest[3 : 3 + nw]
        (y0_ref, y1_ref, dx1_ref, vec_ref, dub_ref, keep, send, w_s, n2_s, n2t_s, dfr_s, dft_s, dy_s, stage, f_ref, dn_ref, lsem, ssem) = rest[3 + nw :]
    copies = load_blocks(dest, w, w_s, lsem)
    core = ctl[1]
    live = (segc_ref[...] != PAD_ID).astype(F32)
    xhat, rstd = row_stats(x1_ref[...])
    n2 = (xhat * ln_ref[0:1] + ln_ref[1:2]).astype(BF)
    n2_s[...] = n2
    n2t_s[...] = n2.T
    dy_s[rows:rp, :] = jnp.zeros((rp - rows, D), F32)
    dy_s[0:rows, :] = cot_ref[...].astype(F32)
    dy = dy_s[...] * live
    dy_s[...] = dy
    df = dy * ln_ref[2:3]
    dfr = df.astype(BF)
    dfr_s[...] = dfr
    dft_s[...] = dfr.T
    if not first:
        vec_ref[2:3] = col_sum(df)
    for c in copies:
        c.wait()
    if first:
        f_ref[...] = jnp.zeros((rp, D), F32)
        dn_ref[...] = jnp.zeros((rp, D), F32)
    else:
        f_ref[...] = fin_ref[...].astype(F32)
        dn_ref[...] = dnin_ref[...].astype(F32)
    copies_of = lambda t: store_copies(core, slots, t, stage.at[t], (keep, send), pl.ds(0, 2 * FCH), ssem.at[t])

    def half_units(t, _):
        rows_t = pl.ds(pl.multiple_of(t * D, D), D)
        wu = w_s[rows_t, 0:FCH]
        wd = w_s[rows_t, FCH:]
        hid = mm(n2_s[...], wu) + ub_ref[pl.ds(t, 1)]
        phi, slope = gelu_parts(hid)
        g = (hid * phi).astype(BF)
        dh = (mm(dfr_s[...], wd) * slope).astype(BF)
        dub_ref[pl.ds(t, 1)] = col_sum(dh.astype(F32))
        stage[t, :, 0:FCH] = mm(n2t_s[...], dh).astype(BF)
        stage[t, :, FCH:] = mm(dft_s[...], g).astype(BF)
        for c in copies_of(t):
            c.start()
        f_ref[...] += mm_nt(g, wd)
        dn_ref[...] += mm_nt(dh, wu)
        return 0

    lax.fori_loop(0, 2, half_units, 0)
    pending = copies_of(0) + copies_of(1)
    if first:
        f_out[...] = f_ref[...].astype(BF)
        dn_out[...] = dn_ref[...].astype(BF)
    else:
        ffo = f_ref[...] + ln_ref[3:4]
        dy = dy_s[...]
        vec_ref[3:4] = col_sum(dy * ffo)
        y = (x1_ref[...] + ln_ref[2:3] * ffo).astype(BF)
        cut = y0_ref.shape[0]
        y0_ref[...] = y[0:cut]
        y1_ref[...] = y[cut:rows]
        dn2 = dn_ref[...]
        xhat, rstd = row_stats(x1_ref[...])
        vec_ref[0:1] = col_sum(dn2 * xhat)
        vec_ref[1:2] = col_sum(dn2)
        dx1 = dy + norm_back(xhat, rstd, dn2, ln_ref[0:1])
        dx1_ref[...] = dx1
        vec_ref[4:5] = col_sum(dx1 * ln_ref[4:5])
        vec_ref[5:6] = col_sum(dx1 * attn_ref[...].astype(F32))
        vec_ref[6:8] = jnp.zeros((2, D), F32)
    for c in pending:
        c.wait()


def ffn(first, ctl, dest, slots, x1, cotangent, segc, ln, ub, more, weights):
    rows, rp = cotangent.shape[0], x1.shape[0]
    wcols = weights[0].shape[2]
    if first:
        outs = [((rp, D), BF, 0), ((rp, D), BF, 0)]
    else:
        cut = -(-rows // 32) * 16
        outs = [((cut, D), BF, 0), ((rows - cut, D), BF, 0), ((rp, D), F32, 0), ((8, D), F32, 0)]
    outs += [((2, FCH), F32, 0)] + [((BLOCKS, BROWS, wcols), BF, 1)] * 2
    return call(
        functools.partial(ffn_kernel, rows, rp, first), "ffn_first" if first else "ffn_last", (ctl, dest, slots),
        [(x1, None), (cotangent, None), (segc, None), (ln, None), (ub, None)] + [(v, None) for v in more] + [(w, "hbm") for w in weights],
        outs,
        [
            pltpu.VMEM((2 * D, wcols), BF), pltpu.VMEM((rp, D), BF), pltpu.VMEM((D, rp), BF), pltpu.VMEM((rp, D), BF), pltpu.VMEM((D, rp), BF),
            pltpu.VMEM((rp, D), F32), pltpu.VMEM((2, D, 2 * FCH), BF),
        ]
        + [pltpu.VMEM((rp, D), F32)] * 2
        + [pltpu.SemaphoreType.DMA((2 * BLOCKS,)), pltpu.SemaphoreType.DMA((2, BLOCKS))],
        20, 56,
    )


def attn_bwd_kernel(nw, rp, cp, which, ctl, dest, dx1_ref, qh, kh, vh, lse_ref, segc_ref, segr_ref, ln_ref, *rest):
    w = rest[:nw]
    dq_ref, dk_ref, dv_ref, w_s, do_s, q_s, k_s, v_s, bias_s, sem, isem = rest[nw:]
    t = which[0]
    heads = half_heads(t, (qh, kh, vh), (q_s, k_s, v_s), isem)
    half = D // 2
    copies = load_blocks(dest, w, w_s, sem, slice(3 * half, 4 * half))
    scale = HEAD ** (-0.5)
    bias_s[...] = jnp.where(segc_ref[...] == segr_ref[...], 0.0, NEG)
    q_s[:, rp:cp, :] = jnp.zeros((HP, cp - rp, 128), BF)
    do_s[:, rp:cp, :] = jnp.zeros((HP, cp - rp, 128), BF)
    dar = (dx1_ref[...] * ln_ref[2:3]).astype(BF)
    for c in copies:
        c.wait()
    z = mm(dar, w_s[pl.ds(pl.multiple_of(t * D, D), D), :]).astype(BF)
    for i in range(HP):
        do_s[i, 0:rp, :] = z[:, i * 128 : (i + 1) * 128]
    for c in heads:
        c.wait()

    def pair(p, _):
        q2 = q_s[p]
        do2 = do_s[p]
        k2 = k_s[p]
        v2 = v_s[p]
        def head(h, sums):
            dq, dk, dv = sums
            m = pair_mask(h)
            km = k2 * m
            st = mm_nt(km, q2) * (scale * LOG2E) + bias_s[...]
            pt = jnp.exp2(st - lse_ref[2 * p + h])
            dpt = mm_nt(v2 * m, do2)
            delta = jnp.sum(pt * dpt, axis=0, keepdims=True)
            dst = (pt * (dpt - delta)).astype(BF)
            return dq + mm_tn(dst, km), dk + mm(dst, q2 * m), dv + mm(pt.astype(BF), do2 * m)

        zero = jnp.zeros((rp, 128), F32)
        dq, dk, dv = lax.fori_loop(0, 2, head, (jnp.zeros((cp, 128), F32), zero, zero))
        dq_ref[p] = (dq[0:rp] * scale).astype(BF)
        dk_ref[p] = (dk * scale).astype(BF)
        dv_ref[p] = dv.astype(BF)
        return 0

    lax.fori_loop(0, HP, pair, 0)


def attn_bwd(t, ctl, dest, dx1, q, k, v, lse, segc, segr, ln, weights):
    rp, cp = segc.shape[0], segr.shape[1]
    wcols = weights[0].shape[2]
    return call(
        functools.partial(attn_bwd_kernel, len(weights), rp, cp), "attn_bwd", (jnp.full((1,), t, jnp.int32), ctl, dest),
        [(dx1, None), (q, "far"), (k, "far"), (v, "far")] + [(e, None) for e in (lse, segc, segr, ln)] + [(w, "hbm") for w in weights],
        [((HP, rp, 128), BF, 0)] * 3,
        [
            pltpu.VMEM((2 * D, wcols // 4), BF), pltpu.VMEM((HP, cp, 128), BF), pltpu.VMEM((HP, cp, 128), BF), pltpu.VMEM((HP, rp, 128), BF), pltpu.VMEM((HP, rp, 128), BF),
            pltpu.VMEM((rp, cp), F32), pltpu.SemaphoreType.DMA((2 * BLOCKS,)), pltpu.SemaphoreType.DMA((3,)),
        ],
        15, 52,
    )


def attn_grad_kernel(rows, rp, ctl, slots, x_ref, dx1_ref, o1_ref, o2_ref, dq1, dk1, dv1, dq2, dk2, dv2, ln_ref, keep, send, stage, x_s, ssem):
    core = ctl[1]
    half = D // 2
    x_s[0:rows, :] = x_ref[...].astype(F32)
    x_s[rows:rp, :] = jnp.zeros((rp - rows, D), F32)
    dart = (dx1_ref[...] * ln_ref[2:3]).astype(BF).T
    xhat, _ = row_stats(x_s[...])
    n1t = (xhat * ln_ref[0:1] + ln_ref[1:2]).astype(BF).T
    pend = []
    for t, (o, dz) in enumerate(((o1_ref, (dq1, dk1, dv1)), (o2_ref, (dq2, dk2, dv2)))):
        o_t = jnp.concatenate([o[i] for i in range(HP)], axis=1)
        stage[t, :, 3 * half :] = mm(dart, o_t).astype(BF)
        z = jnp.concatenate([e[i] for e in dz for i in range(HP)], axis=1)
        stage[t, :, 0 : 3 * half] = mm(n1t, z).astype(BF)
        cps = store_copies(core, slots, t, stage.at[t], (keep, send), pl.ds(0, 4 * half), ssem.at[t])
        for c in cps:
            c.start()
        pend += cps
    for c in pend:
        c.wait()


def attn_grad(ctl, slots, tokens, dx1, o1, o2, dz1, dz2, ln):
    rows, rp = tokens.shape[0], dx1.shape[0]
    wcols = 2 * D
    return call(
        functools.partial(attn_grad_kernel, rows, rp), "attn_grad", (ctl, slots),
        [(tokens, None)] + [(e, None) for e in (dx1, o1, o2, *dz1, *dz2, ln)],
        [((BLOCKS, BROWS, wcols), BF, 1)] * 2,
        [pltpu.VMEM((2, D, wcols), BF), pltpu.VMEM((rp, D), F32), pltpu.SemaphoreType.DMA((2, BLOCKS))],
        10, 48,
    )


def input_grad_kernel(nw, rows, rp, ctl, dest, x_ref, dx1_ref, dq1, dk1, dv1, dq2, dk2, dv2, ln_ref, vecf_ref, dub1_ref, dub2_ref, *rest):
    w = rest[:nw]
    dx_ref, vec_ref, w_s, x_s, sem = rest[nw:]
    half = D // 2
    copies = load_blocks(dest, w, w_s, sem, slice(0, 3 * half))
    x_s[0:rows, :] = x_ref[...].astype(F32)
    x_s[rows:rp, :] = jnp.zeros((rp - rows, D), F32)
    xhat, rstd = row_stats(x_s[...])
    for c in copies:
        c.wait()
    dn1 = None
    for t, dz in enumerate(((dq1, dk1, dv1), (dq2, dk2, dv2))):
        z = jnp.concatenate([e[i] for e in dz for i in range(HP)], axis=1)
        part = mm_nt(z, w_s[t * D : (t + 1) * D, :])
        dn1 = part if dn1 is None else dn1 + part
        vec_ref[8:9, t * half : (t + 1) * half] = col_sum(z[:, 0:half].astype(F32))
        vec_ref[9:10, t * half : (t + 1) * half] = col_sum(z[:, 2 * half :].astype(F32))
        vec_ref[10 + 2 * t : 11 + 2 * t] = dub1_ref[t : t + 1]
        vec_ref[11 + 2 * t : 12 + 2 * t] = dub2_ref[t : t + 1]
    vec_ref[0:1] = col_sum(dn1 * xhat)
    vec_ref[2:3] = col_sum(dn1)
    for i, row in enumerate((1, 3, 5, 7, 4, 6)):
        vec_ref[row : row + 1] = vecf_ref[i : i + 1]
    vec_ref[14:16] = jnp.zeros((2, D), F32)
    dx = dx1_ref[...] + norm_back(xhat, rstd, dn1, ln_ref[0:1])
    dx_ref[...] = dx[0:rows].astype(BF)


def input_grad(ctl, dest, tokens, dx1, dz1, dz2, ln, vec_f, dub1, dub2, weights):
    rows, rp = tokens.shape[0], dx1.shape[0]
    wcols = weights[0].shape[2]
    return call(
        functools.partial(input_grad_kernel, len(weights), rows, rp), "input_grad", (ctl, dest),
        [(tokens, None)] + [(e, None) for e in (dx1, *dz1, *dz2, ln, vec_f, dub1, dub2)] + [(w, "hbm") for w in weights],
        [((rows, D), BF, 0), ((16, D), F32, 0)],
        [pltpu.VMEM((2 * D, wcols * 3 // 4), BF), pltpu.VMEM((rp, D), F32), pltpu.SemaphoreType.DMA((2 * BLOCKS,))],
        10,
    )


def prepare(segment, me, ln_gain, ln_shift, qb, out_bias, layer_scale):
    rows = segment.shape[1]
    rp = -(-rows // 16) * 16
    cp = -(-rp // 128) * 128
    seg = lax.dynamic_index_in_dim(segment, me, 0, keepdims=False)
    seg = jnp.concatenate([seg, jnp.full((rp - rows,), -2, jnp.int32), jnp.full((cp - rp,), -1, jnp.int32)])
    segr = seg.reshape(1, cp)
    segc = seg[:rp].reshape(rp, 1)
    half = D // 2
    ln1 = jnp.stack([ln_gain[0], ln_shift[0], layer_scale[0]])
    ln2 = jnp.stack([ln_gain[1], ln_shift[1], layer_scale[1], out_bias[1], layer_scale[0]])
    z = jnp.zeros((2, half), F32)
    qbt = jnp.concatenate([qb[0].reshape(2, half), z, qb[1].reshape(2, half)], axis=1)
    return segc, segr, ln1, ln2, qbt, out_bias[0:1]


def swap(v, n_tensor):
    return lax.ppermute(v, "tensor", [(i, (i + 1) % n_tensor) for i in range(n_tensor)])


def after(v, *done):
    return lax.optimization_barrier((v, done))[0]


class Grid:
    axes = ("dp", "tensor")
    places = [(z, y, c, t) for z in range(4) for y in range(2) for c in range(2) for t in range(2)]

    def number(self, p):
        return ((p[0] * 2 + p[1]) * 2 + p[2]) * 2 + p[3]

    def x(self, p):
        return p[0], p[1], p[2], 1 - p[3]

    def y(self, p):
        return p[0], 1 - p[1], p[2], p[3]

    def core(self, p):
        return p[0], p[1], 1 - p[2], p[3]

    def first(self, p):
        return self.y(p) if p[2] else self.x(p)

    def second(self, p):
        return self.x(p) if p[2] else self.y(p)

    def z1(self, p):
        return p[0] ^ 1, p[1], p[2], p[3]

    def z2(self, p):
        return p[0] ^ 2, p[1], p[2], p[3]

    def z3(self, p):
        return p[0] ^ 3, p[1], p[2], p[3]

    def along(self, v):
        return [self.send(e, to) for e, to in zip(v, (self.z1, self.z2, self.z3))]

    def send(self, v, to):
        return lax.ppermute(v, self.axes, [(self.number(p), self.number(to(p))) for p in self.places])

    def line(self, p):
        return [(p[0] ^ k, p[1], p[2], p[3]) for k in range(4)]

    def held(self, p, first, second):
        b = second(p)
        return self.line(p) + self.line(first(p)) + self.line(b) + self.line(first(b))

    def tables(self):
        where = lambda q: q[3] * BLOCKS + (q[0] * 2 + q[1]) * 2 + q[2]
        half = BLOCKS // 2
        rows = []
        for p in self.places:
            row = [where(q) for e in (p, self.core(p)) for q in self.held(e, self.first, self.second)]
            for route in ((self.first, self.second), (self.x, self.y)):
                at = {where(q): i for e in (p, self.core(p)) for i, q in enumerate(self.held(e, *route))}
                row += [at[t * BLOCKS + 2 * m + p[2]] for t in range(2) for m in range(half)]
                row += [at[t * BLOCKS + 2 * m + 1 - p[2]] for t in range(2) for m in range(half)]
            rows.append(row)
        return jnp.array(rows, jnp.int32)


def wide(v):
    return v.astype(F32)


class Reduce:
    def __init__(self, net, keep, sent, first, second):
        self.net, self.terms, self.sent, self.first, self.second = net, [keep], sent, first, second
        self.stage = 0
        self.got = net.send(sent, net.core)

    def total(self, at):
        return sum(wide(e[at]) for e in self.terms)

    def start(self, *dep):
        self.stage += 1
        n = self.stage
        self.terms.append(after(self.got, *dep))
        if n < 3:
            self.sent = self.total(slice(BLOCKS >> n, 2 * BLOCKS >> n)).astype(BF)
            self.got = self.net.send(self.sent, self.second if n == 1 else self.first)
        else:
            self.sent = [self.total(k).astype(BF) for k in (1, 2, 3)]
            self.got = self.net.along(self.sent)

    def result(self, *dep):
        return self.total(0) + sum(wide(e) for e in after(self.got, *dep))


class Plain:
    def __init__(self, n_tensor):
        self.n_tensor = n_tensor

    def gather(self, w):
        me = lax.axis_index("tensor")
        other = swap(w, self.n_tensor)
        both = jnp.where(me == 0, jnp.stack([w, other]), jnp.stack([other, w]))
        full = lax.all_gather(both, "dp", axis=1, tiled=True)
        return [full.reshape(2 * BLOCKS, BROWS, w.shape[1])]

    def settle(self, keep, sent):
        me = lax.axis_index("tensor")
        h = BLOCKS // 2
        g = jnp.stack([keep.reshape(2, h, BROWS, -1), sent.reshape(2, h, BROWS, -1)], axis=2).reshape(2, D, -1)
        part = lax.psum_scatter(g, "dp", scatter_dimension=1, tiled=True).astype(F32)
        return jnp.where(me == 0, part[0], part[1]) + swap(jnp.where(me == 0, part[1], part[0]), self.n_tensor)

    def total(self, v):
        return lax.psum(v, ("dp", "tensor"))


def make_on_device(n_dp, n_tensor):
    def on_device(
        tokens, segment, cotangent, ln_gain, ln_shift, qkv_weight, qv_bias, out_weight,
        out_bias, layer_scale, up_weight, up_bias, down_weight,
    ):
        me = lax.axis_index("tensor")
        own_first = lambda own, other, axis=0: jnp.where(me == 0, jnp.stack([own, other], axis), jnp.stack([other, own], axis))
        both = lambda own, other: own_first(own, other, 1).transpose(1, 0, 2)
        half = D // 2
        hid_half = up_weight.shape[1]
        wa = jnp.concatenate([qkv_weight[0], qkv_weight[1], qkv_weight[2], out_weight.T], axis=1)
        small = jnp.concatenate([qv_bias.reshape(-1), up_bias])

        def pack_ffn(up, down):
            down_t = down.T
            return [jnp.concatenate([up[:, lo : lo + FCH], down_t[:, lo : lo + FCH]], axis=1) for lo in range(0, hid_half, FCH)]

        def consts(small, segment):
            small = own_first(small, swap(small, n_tensor))
            qb = small[:, : 2 * half].reshape(2, 2, half).transpose(1, 0, 2).reshape(2, D)
            ub = small[:, 2 * half :]
            return (ub[:, :FCH], ub[:, FCH:]) + prepare(segment, me, ln_gain, ln_shift, qb, out_bias, layer_scale)

        def results(out, dxs, vec, ga, gup, gdown):
            qv = lax.dynamic_slice(vec, (8, me * half), (2, half))
            dubs = lax.dynamic_slice(vec, (10 + 2 * me, 0), (2, D)).reshape(hid_half)
            return (
                out, dxs, vec[0:2], vec[2:4],
                jnp.stack([ga[:, i * half : (i + 1) * half] for i in range(3)]),
                qv, ga[:, 3 * half :].T, vec[4:6], vec[6:8],
                gup, dubs, gdown.T,
            )

        pick = lambda v: lax.dynamic_index_in_dim(v, me, 0, keepdims=False)
        if n_dp != 16 or n_tensor != 2:
            tokens, cotangent = pick(tokens), pick(cotangent)
            net = Plain(n_tensor)
            dest = jnp.arange(2 * BLOCKS, dtype=jnp.int32)
            slots = jnp.concatenate([jnp.arange(BLOCKS, dtype=jnp.int32)] * 2)
            ctl = jnp.stack([me, 0]).astype(jnp.int32)
            wa = net.gather(wa)
            wf = [net.gather(w) for w in pack_ffn(up_weight, down_weight)]
            ub1, ub2, segc, segr, ln1, ln2, qbt, ob0 = consts(small, segment)
            q, k, v, o1, lse1 = attn_fwd1(ctl, dest, tokens, segc, segr, ln1, qbt, wa)
            x1, attn, o2, lse2 = attn_fwd2(ctl, dest, tokens, segc, segr, ln1, ob0, q, k, v, o1, wa)
            f, dn, dub1, k1, s1 = ffn(True, ctl, dest, slots, x1, cotangent, segc, ln2, ub1, (), wf[0])
            y0, y1, dx1, vec_f, dub2, k2, s2 = ffn(False, ctl, dest, slots, x1, cotangent, segc, ln2, ub2, (attn, f, dn), wf[1])
            dz1 = attn_bwd(0, ctl, dest, dx1, q, k, v, lse1, segc, segr, ln1, wa)
            dz2 = attn_bwd(1, ctl, dest, dx1, q, k, v, lse2, segc, segr, ln1, wa)
            ka, sa = attn_grad(ctl, slots, tokens, dx1, o1, o2, dz1, dz2, ln1)
            dx, vec = input_grad(ctl, dest, tokens, dx1, dz1, dz2, ln1, vec_f, dub1, dub2, wa)
            gf1, gf2, ga = net.settle(k1, s1), net.settle(k2, s2), net.settle(ka, sa)
            vec = net.total(vec)
            gup = jnp.concatenate([gf1[:, :FCH], gf2[:, :FCH]], axis=1)
            gdown = jnp.concatenate([gf1[:, FCH:], gf2[:, FCH:]], axis=1)
            y = jnp.concatenate([y0, y1])
            return results(both(y, swap(y, n_tensor)), both(dx, swap(dx, n_tensor)), vec, ga, gup, gdown)

        net = Grid()
        place = lax.axis_index("dp") * 2 + me
        bs = net.along([wa] * 3)
        tokens, cotangent, segment, small, place = after((tokens, cotangent, segment, small, place), wa)
        tokens, cotangent = pick(tokens), pick(cotangent)
        ub1, ub2, segc, segr, ln1, ln2, qbt, ob0 = consts(small, segment)
        table = lax.dynamic_index_in_dim(net.tables(), place, 0, keepdims=False)
        bs = after(bs, tokens, cotangent, segc, table)
        s = after(jnp.stack([wa, *bs]))
        fs, es = pack_ffn(*after((up_weight, down_weight), s))
        ra = net.send(s, net.first)
        fz = net.along([after(fs, s)] * 3)
        dest, slots, slots_f = (table[i : i + 2 * BLOCKS] for i in range(0, 6 * BLOCKS, 2 * BLOCKS))
        ctl = jnp.stack([me, lax.axis_index("dp") % 2]).astype(jnp.int32)
        ra = after(ra, dest, qbt)
        s = jnp.concatenate([s, ra])
        r = net.send(s, net.second)
        sc = net.send(s, net.core)
        fz = after(fz, s)
        fs = after(jnp.stack([fs, *fz]))
        ez = net.along([after(es, fs)] * 3)
        r = after(r, sc, fs)
        rc = net.send(r, net.core)
        fs = after(fs, r)
        fr = net.send(fs, net.first)
        fr = after(fr, rc)
        fs = jnp.concatenate([fs, fr])
        r1 = net.send(fs, net.second)
        c1 = net.send(fs, net.core)
        wa = after([s, r, sc, rc], fs)
        q, k, v, o1, lse1 = attn_fwd1(ctl, dest, tokens, segc, segr, ln1, qbt, wa)
        r1, c1, ez = after((r1, c1, ez), o1)
        w1 = [fs, r1, c1, net.send(r1, net.core)]
        es = after(jnp.stack([es, *ez]), r1)
        er = net.send(es, net.first)
        q = after(q, es, r1)
        x1, attn, o2, lse2 = attn_fwd2(ctl, dest, tokens, segc, segr, ln1, ob0, q, k, v, o1, wa)
        w1, er = after((w1, er), x1)
        es = jnp.concatenate([es, er])
        r2 = net.send(es, net.second)
        c2 = net.send(es, net.core)
        w1 = after(w1, es)
        f, dn, dub1, k1, s1 = ffn(True, ctl, dest, slots, x1, cotangent, segc, ln2, ub1, (), w1)
        r2, c2 = after((r2, c2), f)
        w2 = [es, r2, c2, net.send(r2, net.core)]
        g1 = Reduce(net, k1, s1, net.first, net.second)
        y0, y1, dx1, vec_f, dub2, k2, s2 = ffn(False, ctl, dest, slots_f, x1, cotangent, segc, ln2, ub2, (attn, f, dn), w2)
        g2 = Reduce(net, k2, s2, net.x, net.y)
        g1.start(dx1)
        dx1 = after(dx1, g1.sent)
        dz1 = attn_bwd(0, ctl, dest, dx1, q, k, v, lse1, segc, segr, ln1, wa)
        g1.start(dz1[0])
        g2.start(dz1[0], g1.sent)
        z0 = swap(after(y0, g2.sent), n_tensor)
        dx1 = after(dx1, dz1[0], g1.sent, g2.sent)
        dz2 = attn_bwd(1, ctl, dest, dx1, q, k, v, lse2, segc, segr, ln1, wa)
        z1 = swap(after(y1, dz2[0]), n_tensor)
        dx1 = after(dx1, dz2[0], z0)
        ka, sa = attn_grad(ctl, slots, tokens, dx1, o1, o2, dz1, dz2, ln1)
        g = Reduce(net, ka, sa, net.first, net.second)
        g1.start(ka)
        g2.start(ka)
        dx1 = after(dx1, ka, g1.sent, g2.sent, z1)
        dx, vec = input_grad(ctl, dest, tokens, dx1, dz1, dz2, ln1, vec_f, dub1, dub2, wa)
        def add(v, to, *dep):
            v = after(v, *dep)
            return v + net.send(v, to)

        g.start(dx)
        vec = add(add(vec, net.z1, g.sent), net.z2)
        g2.start(g.sent, vec)
        vec = add(vec, net.first)
        y0, y1, z0, z1 = after((y0, y1, z0, z1), g.sent)
        out = both(jnp.concatenate([y0, y1]), jnp.concatenate([z0, z1]))
        gf1 = g1.result(g.sent)
        g.start(g2.sent, gf1, out, vec)
        vec = add(vec, net.second, g.sent)
        dx_other = swap(after(dx, vec), n_tensor)
        g.start(vec)
        gf2 = g2.result(g.sent)
        vec = add(vec, net.core, g.sent)
        gup = jnp.concatenate([gf1[:, :FCH], gf2[:, :FCH]], axis=1)
        gdown = jnp.concatenate([gf1[:, FCH:], gf2[:, FCH:]], axis=1)
        dxs = both(dx, dx_other)
        return results(out, dxs, vec, g.result(dxs), gup, gdown)

    return on_device


def solution(mesh):
    rows = P(None, "dp", None)
    wt = P("tensor", "dp")
    return jax.shard_map(
        make_on_device(mesh.shape["dp"], mesh.shape["tensor"]),
        mesh=mesh,
        in_specs=(
            rows, P(None, "dp"), rows, P(), P(), P(None, "dp", "tensor"), P(None, "tensor"), wt,
            P(), P(), P("dp", "tensor"), P("tensor"), wt,
        ),
        out_specs=(
            rows, rows, P(), P(), P(None, "dp", "tensor"), P(None, "tensor"), wt,
            P(), P(), P("dp", "tensor"), P("tensor"), wt,
        ),
        check_vma=False,
    )
```
